768 devices in a mesh: height: 64 (over y, x, core), plan: 12 (over z).
Axes of the slice: x: 4, y: 8, z: 12, core: 2. Of those that a mesh axis runs over, the one named last changes fastest.
Arguments:
- divergence: float32 [256, 192, 512], P('height', 'plan'), may hold values from -8 to 8
- density: float32 [256, 192, 512], P('height', 'plan'), may hold values from 0.5 to 2
- zones: int32 [256, 192, 512], P('height', 'plan'), may hold values from 0 to 4
Outputs:
- pressure: float32 [256, 192, 512], P('height', 'plan')
The draws below stay inside these ranges and needn't reach their ends.
Inputs may be any that keep to these rules, and one draw needn't show every extreme that they name: `zones`: zone 0 open air, 1 wall, 2 stairwell, 3 open door, 4 closed door.
All inputs are finite; a program needn't handle non-finite values.
Results may differ from the reference program's by a relative error of at most 0.00002.
Values sent between devices are 32-bit elements; how exact they have to be, the bound alone decides.
No kernel may reach another device: no remote copies, remote signals or barrier semaphores. Data moves between devices by JAX's collectives and lax.ppermute only.
A program may use at most 32 MiB of HBM per device.

```python
import math
import jax
import jax.numpy as jnp

NY = 512
PRE = 2
POST = 2
COARSE = 4
NZ = 256
NX = 192


def place_ends(entries, key, least, top_value):
    extent = entries.shape
    index_at = [jax.random.randint(jax.random.fold_in(key, axis), (), 0, extent[axis]) for axis in range(len(extent))]
    entries = entries.at[tuple(index_at)].set(least)
    longest = extent.index(max(extent))
    index_at[longest] = (index_at[longest] + 1) % extent[longest]
    return entries.at[tuple(index_at)].set(top_value)


def shard_levels(rng, dims, pieces, least, high):
    level = 1.0
    for position, blocks in pieces:
        draws = jax.random.uniform(jax.random.fold_in(jax.random.fold_in(rng, 6), position), (blocks,), jnp.float32, least / len(pieces), high / len(pieces))
        level = level * jnp.repeat(jnp.exp(draws), dims[position] // blocks).reshape((-1,) + (1,) * (len(dims) - 1 - position))
    return level


def bell_draw(stream_key, extent, deviation, reach, cuts=(), kind=jnp.bfloat16):
    values = jax.random.normal(stream_key, extent, jnp.float32) * deviation
    if len(cuts) > 0:
        values = shard_levels(stream_key, extent, cuts, -0.22, 0.18) * values
    return jnp.clip(values, min=-reach, max=reach).astype(kind)


def setup_inputs(seed: int = 0) -> dict:
    seeds = jax.random.split(jax.random.key(seed), 4)
    return {
        "divergence": bell_draw(seeds[0], (NZ, NX, NY), 1.0, 8.0, ((0, 64), (1, 12)), jnp.float32),
        "density": jnp.clip(jnp.exp(math.log(2.0) - 1.3862944 * jax.random.uniform(seeds[1], (NZ, NX, NY), jnp.float32) ** shard_levels(seeds[1], (NZ, NX, NY), ((0, 64), (1, 12)), -0.2, 0.2)), 0.5, 2.0),
        "zones": place_ends(jax.random.randint(seeds[2], (NZ, NX, NY), 0, 5), jax.random.fold_in(seeds[2], 1), 0, 4).astype(jnp.int32),
    }


PERMEABILITY = (1.0, 0.1, 0.6, 0.8, 0.25)
OMEGA = 2.0 / 3.0


def conduct(zones, density):
    perm = jnp.zeros(density.shape, jnp.float32)
    for zone_id, value in enumerate(PERMEABILITY):
        perm = perm + jnp.where(zones == zone_id, jnp.float32(value), jnp.float32(0.0))
    return perm / density


def harmonic(first, second):
    return 2.0 * first * second / (first + second)


def neighbours(padded):
    return [padded[:-2, 1:-1, 1:-1], padded[2:, 1:-1, 1:-1],
            padded[1:-1, :-2, 1:-1], padded[1:-1, 2:, 1:-1],
            padded[1:-1, 1:-1, :-2], padded[1:-1, 1:-1, 2:]]


def setup(cond, padder):
    padded = padder(cond - 1.0) + 1.0
    coeffs = [harmonic(cond, other) for other in neighbours(padded)]
    diag = coeffs[0] + coeffs[1] + coeffs[2] + coeffs[3] + coeffs[4] + coeffs[5]
    return coeffs, diag


def stencil(field, coeffs, padder):
    others = neighbours(padder(field))
    total = coeffs[0] * (field - others[0])
    for index in range(1, 6):
        total = total + coeffs[index] * (field - others[index])
    return total


def smooth(field, source, coeffs, diag, padder, count):
    for sweep in range(count):
        field = field + OMEGA * (source - stencil(field, coeffs, padder)) / diag
    return field


def block_sum(field):
    depth, across, along = field.shape
    return field.reshape(depth // 2, 2, across // 2, 2, along // 2, 2).sum(axis=(1, 3, 5))


def prolong(field):
    depth, across, along = field.shape
    wide = jnp.broadcast_to(field[:, None, :, None, :, None], (depth, 2, across, 2, along, 2))
    return wide.reshape(depth * 2, across * 2, along * 2)


def zero_pad(field):
    return jnp.pad(field, 1)


def reference(divergence, density, zones):
    cond0 = conduct(zones, density)
    coeffs0, diag0 = setup(cond0, zero_pad)
    p0 = OMEGA * divergence / diag0
    p0 = smooth(p0, divergence, coeffs0, diag0, zero_pad, PRE - 1)
    f1 = 0.5 * block_sum(divergence - stencil(p0, coeffs0, zero_pad))
    cond1 = 0.125 * block_sum(cond0)
    coeffs1, diag1 = setup(cond1, zero_pad)
    p1 = OMEGA * f1 / diag1
    p1 = smooth(p1, f1, coeffs1, diag1, zero_pad, PRE - 1)
    f2 = 0.5 * block_sum(f1 - stencil(p1, coeffs1, zero_pad))
    cond2 = 0.125 * block_sum(cond1)
    coeffs2, diag2 = setup(cond2, zero_pad)
    p2 = OMEGA * f2 / diag2
    p2 = smooth(p2, f2, coeffs2, diag2, zero_pad, COARSE - 1)
    leftover = f2 - stencil(p2, coeffs2, zero_pad)
    line = jnp.sum(leftover, axis=1, keepdims=True) / jnp.sum(diag2, axis=1, keepdims=True)
    p2 = p2 + line
    p1 = smooth(p1 + prolong(p2), f1, coeffs1, diag1, zero_pad, POST)
    p0 = smooth(p0 + prolong(p1), divergence, coeffs0, diag0, zero_pad, POST)
    return p0
```

```python
import jax
import jax.numpy as jnp
from jax import lax
from jax.experimental import pallas as pl
from jax.experimental.pallas import tpu as pltpu
from jax.sharding import PartitionSpec as P

PERMEABILITY = (1.0, 0.1, 0.6, 0.8, 0.25)
OMEGA = 2.0 / 3.0
F32 = jnp.float32


def vmem(count):
    return [pl.BlockSpec(memory_space=pltpu.VMEM)] * count


def smem():
    return pl.BlockSpec(memory_space=pltpu.SMEM)


def call(body, outs, scratch, where, *arrays, flops=1000000):
    many = isinstance(outs, list)
    shapes = [jax.ShapeDtypeStruct(s, F32) for s in (outs if many else [outs])]
    return pl.pallas_call(
        body,
        out_shape=shapes if many else shapes[0],
        in_specs=([] if where is None else [smem()]) + vmem(len(arrays)),
        out_specs=vmem(len(shapes)) if many else vmem(1)[0],
        scratch_shapes=[pltpu.VMEM(s, F32) for s in scratch],
        compiler_params=pltpu.CompilerParams(vmem_limit_bytes=40 << 20),
    )(*(() if where is None else (where,)), *arrays)


def harmonic(a, b):
    return 2.0 * a * b / (a + b)


def iota(shape, dim):
    return lax.broadcasted_iota(jnp.int32, shape, dim)


def ahead(x, axis):
    return pltpu.roll(x, x.shape[axis] - 1, axis)


def behind(x, axis):
    return pltpu.roll(x, 1, axis)


def y_faces(c):
    lane = iota(c.shape, 1)
    last = c.shape[1] - 1
    full = harmonic(c, jnp.where(lane == last, 1.0, ahead(c, 1)))
    link = jnp.where(lane == last, 0.0, full)
    first = jnp.where(lane == 0, harmonic(c, 1.0), 0.0)
    return link, full + behind(link, 1) + first


def spread(p, below, above, cz0, cz1, cx, cy):
    total = cz0 * below + cz1 * above
    total = total + cx * ahead(p, 0) + behind(cx * p, 0)
    return total + cy * ahead(p, 1) + behind(cy * p, 1)


def pair_matrix(wide):
    shape = (wide, wide // 2)
    return (lax.shift_right_logical(iota(shape, 0), 1) == iota(shape, 1)).astype(F32)


def copy_matrix(narrow):
    shape = (narrow, narrow * 2)
    return (iota(shape, 0) == lax.shift_right_logical(iota(shape, 1), 1)).astype(F32)


def dot(a, b):
    return jnp.dot(a, b, precision=lax.Precision.HIGHEST, preferred_element_type=F32)


def pair_rows(s, x, start, count):
    tiles = x.shape[1] // 128
    for t in range(tiles):
        s[t, 0 : x.shape[0]] = x[:, 128 * t : 128 * t + 128]
    parts = [s[t, pl.ds(start, count, stride=2), :] + s[t, pl.ds(start + 1, count, stride=2), :] for t in range(tiles)]
    return jnp.concatenate(parts, axis=1)


def copy_rows(s, x):
    tiles, count = x.shape[1] // 128, x.shape[0]
    for t in range(tiles):
        s[t, pl.ds(0, count, stride=2), :] = x[:, 128 * t : 128 * t + 128]
        s[t, pl.ds(1, count, stride=2), :] = x[:, 128 * t : 128 * t + 128]
    return jnp.concatenate([s[t, 0 : 2 * count] for t in range(tiles)], axis=1)


def inside(first, index, count):
    at = first + index
    return jnp.logical_and(at >= 0, at < count)


def k_conduct(div, density, zones, out):
    for z in range(4):
        zone = zones[z]
        perm = jnp.where(zone == 0, PERMEABILITY[0], 0.0)
        for zone_id in range(1, 5):
            perm = jnp.where(zone == zone_id, PERMEABILITY[zone_id], perm)
        out[0, z] = perm / density[z]
        out[1, z] = div[z]


def k_rows0(where, own, core, link, cond, div, left, right):
    h, high = where[0], where[2]
    odd = lax.rem(h, 2)
    cond[4:8] = own[0]
    div[4:8] = own[1]

    @pl.when(odd == 0)
    def _():
        cond[0:4] = link[0, 0]
        div[0:4] = link[0, 1]
        cond[8:12] = core[1, 0]
        div[8:12] = core[1, 1]

    @pl.when(odd == 1)
    def _():
        cond[0:4] = core[0, 0]
        div[0:4] = core[0, 1]
        cond[8:12] = link[1, 0]
        div[8:12] = link[1, 1]

    @pl.when(h == 0)
    def _():
        cond[0:4] = jnp.ones((4, 16, 512), F32)

    @pl.when(h == high - 1)
    def _():
        cond[8:12] = jnp.ones((4, 16, 512), F32)

    for z in range(10):
        left[z, 0:4] = cond[z + 1, 0:4]
        left[z, 4:8] = div[z + 1, 0:4]
        right[z, 0:4] = cond[z + 1, 12:16]
        right[z, 4:8] = div[z + 1, 12:16]


def k_level0(where, cond, div, low, high, pre, w_out, g_out, cx_out, cy_out, cz_out, pack, c, g, w, cx, cy, cz, dg, p, rs, c1, st):
    h, plan, n_h, n_p = where[0], where[1], where[2], where[3]
    for z in range(12):
        c[z, 4:20] = cond[z]
        if 1 <= z <= 10:
            c[z, 0:4] = jnp.where(plan == 0, 1.0, low[z - 1, 0:4])
            c[z, 20:24] = jnp.where(plan == n_p - 1, 1.0, high[z - 1, 0:4])
        else:
            c[z, 0:4] = jnp.ones((4, 512), F32)
            c[z, 20:24] = jnp.ones((4, 512), F32)
    for z in range(1, 11):
        g[z, 4:20] = div[z]
        g[z, 0:4] = low[z - 1, 4:8]
        g[z, 20:24] = high[z - 1, 4:8]
    row = iota((24, 512), 0) + (plan * 16 - 4)
    row_in = jnp.logical_and(row >= 0, row < n_p * 16).astype(F32) * OMEGA
    for z in range(11):
        cz[z] = harmonic(c[z], c[z + 1])
    for z in range(1, 11):
        here = c[z]
        fx = harmonic(here, ahead(here, 0))
        link, both = y_faces(here)
        diag = cz[z - 1] + cz[z] + fx + behind(fx, 0) + both
        weight = jnp.where(inside(h * 4 - 4, z, n_h * 4), row_in, 0.0) / diag
        cx[z] = fx
        cy[z] = link
        w[z] = weight
        if 4 <= z <= 7:
            dg[z - 4] = diag
            rs[z - 4] = g[z]
        g[z] = weight * g[z]
    for z in range(2, 10):
        here = g[z]
        total = spread(here, g[z - 1], g[z + 1], cz[z - 1], cz[z], cx[z], cy[z])
        p[z] = here * (1.0 / 3.0) + here + w[z] * total
    for z in range(4, 8):
        here = p[z]
        total = spread(here, p[z - 1], p[z + 1], cz[z - 1], cz[z], cx[z], cy[z])
        rs[z - 4] = rs[z - 4] - dg[z - 4] * here + total
    for z in range(2, 10):
        pre[z - 2] = p[z]
    for z in range(3, 9):
        w_out[z - 3] = w[z]
        g_out[z - 3] = g[z]
        cx_out[z - 3] = cx[z]
        cy_out[z - 3] = cy[z]
    for z in range(2, 9):
        cz_out[z - 2] = cz[z]
    rows = [pair_rows(st.at[z], rs[2 * z] + rs[2 * z + 1], 4, 8) for z in range(2)]
    for z in range(4):
        sums = c[2 * z + 2] + c[2 * z + 3]
        c1[z, 0:8] = pair_rows(st.at[2 + 2 * z], sums, 0, 8)
        c1[z, 8:12] = pair_rows(st.at[3 + 2 * z], sums[16:24], 0, 4)
        c1[z, 12:16] = jnp.full((4, 512), 4.0, F32)
    pairs = pair_matrix(512)
    f1 = 0.5 * dot(jnp.concatenate(rows, axis=0), pairs)
    k1 = 0.125 * dot(jnp.concatenate([c1[z] for z in range(4)], axis=0), pairs)
    k1 = [k1[16 * z : 16 * z + 16] for z in range(4)]
    for z in range(2):
        here = k1[z + 1]
        fx = harmonic(here, ahead(here, 0))
        link, both = y_faces(here)
        diag = harmonic(here, k1[z]) + harmonic(here, k1[z + 2]) + fx + behind(fx, 0) + both
        c1[z, :, 0:256] = here
        c1[z, :, 256:512] = diag
        pack[z, 0:8] = OMEGA * f1[8 * z : 8 * z + 8] / c1[z, 2:10, 256:512]
        pack[z, 8:16] = c1[z, 2:10, 0:256]


def k_rows1(where, chip, link, third, g, c, left, right, s):
    h, high = where[0], where[2]
    odd = lax.rem(h, 2)

    @pl.when(odd == 0)
    def _():
        s[0:4] = link[0]
        s[4:8] = chip[...]
        s[8:10] = third[1]

    @pl.when(odd == 1)
    def _():
        s[0:2] = third[0]
        s[2:6] = chip[...]
        s[6:10] = link[1]

    for z in range(10):
        keep = inside(h * 2 - 4, z, high * 2)
        g[z] = jnp.where(keep, s[z, 0:8], 0.0)
        c[z] = jnp.where(keep, s[z, 8:16], 1.0)
    for z in range(10):
        left[z, 0:4] = g[z, 0:4]
        left[z, 4:8] = c[z, 0:4]
        right[z, 0:4] = g[z, 4:8]
        right[z, 4:8] = c[z, 4:8]


def k_level1(where, g_in, c_in, low, high, pre, w_out, g_out, cx_out, cy_out, cz_out, copies, c, g, w, cx, cy, cz, dg, rs, st):
    h, plan, n_h, n_p = where[0], where[1], where[2], where[3]
    for z in range(10):
        g[z, 4:12] = g_in[z]
        c[z, 4:12] = c_in[z]
        g[z, 0:4] = jnp.where(plan == 0, 0.0, low[z, 0:4])
        c[z, 0:4] = jnp.where(plan == 0, 1.0, low[z, 4:8])
        g[z, 12:16] = jnp.where(plan == n_p - 1, 0.0, high[z, 0:4])
        c[z, 12:16] = jnp.where(plan == n_p - 1, 1.0, high[z, 4:8])
    row = iota((16, 256), 0) + (plan * 8 - 4)
    row_in = jnp.logical_and(row >= 0, row < n_p * 8).astype(F32) * OMEGA
    for z in range(9):
        cz[z] = harmonic(c[z], c[z + 1])
    for z in range(1, 9):
        here = c[z]
        fx = harmonic(here, ahead(here, 0))
        link, both = y_faces(here)
        diag = cz[z - 1] + cz[z] + fx + behind(fx, 0) + both
        cx[z] = fx
        cy[z] = link
        w[z] = jnp.where(inside(h * 2 - 4, z, n_h * 2), row_in, 0.0) / diag
        if 4 <= z <= 5:
            dg[z - 4] = diag
    for z in range(1, 9):
        here = g[z]
        total = spread(here, g[z - 1], g[z + 1], cz[z - 1], cz[z], cx[z], cy[z])
        pre[z - 1] = here * (1.0 / 3.0) + here + w[z] * total
    for z in range(4, 6):
        here = pre[z - 1]
        total = spread(here, pre[z - 2], pre[z], cz[z - 1], cz[z], cx[z], cy[z])
        rs[z - 4] = (g[z] - OMEGA * here + w[z] * total) * dg[z - 4] * 1.5
    for z in range(2, 8):
        w_out[z - 2] = w[z]
        g_out[z - 2] = g[z]
        cx_out[z - 2] = cx[z]
        cy_out[z - 2] = cy[z]
    for z in range(1, 8):
        cz_out[z - 1] = cz[z]
    rows = [pair_rows(st.at[0], rs[0] + rs[1], 0, 8)]
    rows += [pair_rows(st.at[z + 1], c[2 * z + 2] + c[2 * z + 3], 0, 8) for z in range(3)]
    pairs = pair_matrix(256)
    both = jnp.concatenate(rows, axis=0)
    down = dot(both, pairs)
    f2 = 0.5 * down[0:8]
    k2 = [0.125 * down[8 * z + 8 : 8 * z + 16] for z in range(3)]
    here = k2[1]
    fx = harmonic(here, ahead(here, 0))
    link, share = y_faces(here)
    diag = harmonic(here, k2[0]) + harmonic(here, k2[2]) + fx + behind(fx, 0) + share
    dg[0, 0:8, 0:128] = diag
    dg[0, 8:16, 0:128] = here
    tile_g = OMEGA * f2[2:6] / dg[0, 2:6, 0:128]
    tile_c = dg[0, 10:14, 0:128]
    for i in range(copies.shape[0]):
        copies[i, 0:4] = tile_g
        copies[i, 4:8] = tile_c


def k_wide(tiles, copies):
    n = tiles.shape[0]
    for t in range(n):
        copies[0, 4 * t : 4 * t + 4] = tiles[t, 0:4]
        copies[0, 4 * n + 4 * t : 4 * n + 4 * t + 4] = tiles[t, 4:8]
    for i in range(1, copies.shape[0]):
        copies[i] = copies[0]


def k_up(where, block, outer, pre1, w1, g1, cx1, cy1, cz1, pre0, w0, g0, cx0, cy0, cz0, out, s, c, g, w, cx, cy, cz, dg, pa, pb, p2, u1, q1, u0, q0, s1, s0):
    h, plan, n_h = where[0], where[1], where[2]
    wide = s.shape[1] // 2
    s[0:6] = outer[0]
    s[6:14] = block[...]
    s[14:20] = outer[1]
    q = lax.rem(h, 8)
    for z in range(13):
        keep = inside(h - 6, z, n_h)
        g[z] = jnp.where(keep, s[q + z, 0:wide], 0.0)
        c[z] = jnp.where(keep, s[q + z, wide : 2 * wide], 1.0)
    row = iota((wide, 128), 0)
    for z in range(12):
        cz[z] = harmonic(c[z], c[z + 1])
    for z in range(1, 12):
        here = c[z]
        full = harmonic(here, jnp.where(row == wide - 1, 1.0, ahead(here, 0)))
        fx = jnp.where(row == wide - 1, 0.0, full)
        first = jnp.where(row == 0, harmonic(here, 1.0), 0.0)
        link, both = y_faces(here)
        diag = cz[z - 1] + cz[z] + full + behind(fx, 0) + first + both
        cx[z] = fx
        cy[z] = link
        w[z] = jnp.where(inside(h - 6, z, n_h), OMEGA, 0.0) / diag
        dg[z] = diag

    def step(source, z):
        here = source[z]
        total = spread(here, source[z - 1], source[z + 1], cz[z - 1], cz[z], cx[z], cy[z])
        return here * (1.0 / 3.0) + g[z] + w[z] * total

    for z in range(1, 12):
        pa[z] = step(g, z)
    for z in range(2, 11):
        pb[z] = step(pa, z)
    for z in range(3, 10):
        pa[z] = step(pb, z)
    for z in range(4, 9):
        here = pa[z]
        extra = (step(pa, z) - here) * dg[z] * 1.5
        line = jnp.sum(extra, axis=0, keepdims=True) / jnp.sum(dg[z], axis=0, keepdims=True)
        p2[z - 4, 0:8] = jnp.zeros((8, 128), F32)
        p2[z - 4, wide + 8 : wide + 16] = jnp.zeros((8, 128), F32)
        p2[z - 4, 8 : wide + 8] = here + line
    rows = jnp.concatenate([p2[z, pl.ds(plan * 4 + 6, 8), :] for z in range(5)], axis=0)
    rows = dot(rows, copy_matrix(128))
    for z in range(5):
        u1[z] = copy_rows(s1.at[z], rows[8 * z : 8 * z + 8])
    for z in range(1, 9):
        q1[z - 1] = pre1[z - 1] + u1[z // 2]
    mid = []
    for z in range(2, 8):
        here = q1[z - 1]
        total = spread(here, q1[z - 2], q1[z], cz1[z - 2], cz1[z - 1], cx1[z - 2], cy1[z - 2])
        pb_rows = here * (1.0 / 3.0) + g1[z - 2] + w1[z - 2] * total
        mid.append(pb_rows)
    for z in range(6):
        q1[z] = mid[z]
    low = []
    for z in range(3, 7):
        here = q1[z - 2]
        total = spread(here, q1[z - 3], q1[z - 1], cz1[z - 2], cz1[z - 1], cx1[z - 2], cy1[z - 2])
        low.append(here * (1.0 / 3.0) + g1[z - 2] + w1[z - 2] * total)
    for z in range(4):
        q1[z] = low[z]
    rows = jnp.concatenate([q1[z] for z in range(4)], axis=0)
    rows = dot(rows, copy_matrix(256))
    for z in range(4):
        u0[z] = copy_rows(s0.at[z], rows[16 * z : 16 * z + 16])
    for z in range(2, 10):
        q0[z - 2] = pre0[z - 2] + u0[z // 2 - 1, 4:28]
    for z in range(3, 9):
        here = q0[z - 2]
        total = spread(here, q0[z - 3], q0[z - 1], cz0[z - 3], cz0[z - 2], cx0[z - 3], cy0[z - 3])
        u0[z - 3, 0:24] = here * (1.0 / 3.0) + g0[z - 3] + w0[z - 3] * total
    for z in range(4, 8):
        here = u0[z - 3, 0:24]
        total = spread(here, u0[z - 4, 0:24], u0[z - 2, 0:24], cz0[z - 3], cz0[z - 2], cx0[z - 3], cy0[z - 3])
        q0[z - 4] = here * (1.0 / 3.0) + g0[z - 3] + w0[z - 3] * total
        out[z - 4] = q0[z - 4, 4:20]


def on_device(divergence, density, zones):
    n_h, n_p = lax.axis_size("height"), lax.axis_size("plan")
    h, plan = lax.axis_index("height"), lax.axis_index("plan")
    odd = lax.rem(h, 2)
    where = jnp.stack([h, plan, jnp.int32(n_h), jnp.int32(n_p)])
    cores = [[i, i + 1] for i in range(0, n_h, 2)]
    links = [[i, (i + 1) % n_h] for i in range(1, n_h, 2)]

    def pair(x, groups):
        return lax.all_gather(x, "height", axis=0, tiled=False, axis_index_groups=groups)

    def beside(low_rows, high_rows):
        up = [(i, i + 1) for i in range(n_p - 1)]
        down = [(i + 1, i) for i in range(n_p - 1)]
        return lax.ppermute(high_rows, "plan", up), lax.ppermute(low_rows, "plan", down)

    own = call(k_conduct, (2, 4, 16, 512), [], None, divergence, density, zones)
    core = pair(own, cores)
    link = pair(own, links)
    tall = (12, 16, 512)
    cond, div, left, right = call(k_rows0, [tall, tall, (10, 8, 512), (10, 8, 512)], [], where, own, core, link)
    low, high = beside(left, right)
    box = (12, 24, 512)
    eight, six, seven = (8, 24, 512), (6, 24, 512), (7, 24, 512)
    *level0, pack = call(
        k_level0,
        [eight, six, six, six, six, seven, (2, 16, 256)],
        [box] * 6 + [(4, 24, 512), box, (4, 24, 512), (4, 16, 512), (10, 4, 24, 128)],
        where, cond, div, low, high,
    )
    chip = pair(pack, cores).reshape(4, 16, 256)
    link = pair(chip, links)
    third = pair(jnp.where(odd == 0, link[0, 2:4], link[1, 0:2]), cores)
    g1, c1, left, right = call(k_rows1, [(10, 8, 256)] * 4, [(10, 16, 256)], where, chip, link, third)
    low, high = beside(left, right)
    box = (10, 16, 256)
    eight, six, seven = (8, 16, 256), (6, 16, 256), (7, 16, 256)
    *level1, tiles = call(
        k_level1,
        [eight, six, six, six, six, seven, (n_p, 8, 128)],
        [box] * 6 + [(2, 16, 256), (2, 16, 256), (4, 2, 16, 128)],
        where, g1, c1, low, high,
    )
    tiles = lax.all_to_all(tiles, "plan", split_axis=0, concat_axis=0, tiled=True)
    wide = n_p * 4
    block = call(k_wide, (8, 2 * wide, 128), [], None, tiles)
    rows = [[8 * y + i for i in range(8)] for y in range(n_h // 8)]
    block = lax.all_to_all(block, "height", split_axis=0, concat_axis=0, tiled=True, axis_index_groups=rows)
    cross = []
    for y in range(n_h // 8 - 1):
        for i in range(0, 8, 2):
            cross += [(8 * y + i + 1, 8 * y + 8 + i), (8 * y + 8 + i, 8 * y + i + 1)]
    part = lax.dynamic_slice_in_dim(block, 2 * odd, 6, 0)
    outer = pair(lax.ppermute(part, "height", cross), cores)
    flat = (13, wide, 128)
    return call(
        k_up,
        (4, 16, 512),
        [(20, 2 * wide, 128)] + [flat] * 9 + [(5, wide + 16, 128), (5, 16, 256), (8, 16, 256), (6, 32, 512), (8, 24, 512), (5, 2, 16, 128), (4, 4, 32, 128)],
        where, block, outer, *level1, *level0,
    )


def solution(mesh):
    return jax.shard_map(
        on_device,
        mesh=mesh,
        in_specs=(P("height", "plan", None), P("height", "plan", None), P("height", "plan", None)),
        out_specs=P("height", "plan", None),
        check_vma=False,
    )
```

```python
import jax
import jax.numpy as jnp
from jax import lax
from jax.experimental import pallas as pl
from jax.experimental.pallas import tpu as pltpu
from jax.sharding import PartitionSpec as P

PERMEABILITY = (1.0, 0.1, 0.6, 0.8, 0.25)
OMEGA = 2.0 / 3.0
F32 = jnp.float32


def vmem(count):
    return [pl.BlockSpec(memory_space=pltpu.VMEM)] * count


def smem():
    return pl.BlockSpec(memory_space=pltpu.SMEM)


def call(body, outs, scratch, where, *arrays, flops=1000000):
    many = isinstance(outs, list)
    shapes = [pltpu.VMEM(s, F32) for s in (outs if many else [outs])]
    return pl.pallas_call(
        body,
        out_shape=shapes if many else shapes[0],
        in_specs=([] if where is None else [smem()]) + vmem(len(arrays)),
        out_specs=vmem(len(shapes)) if many else vmem(1)[0],
        scratch_shapes=[pltpu.VMEM(s, F32) for s in scratch],
        compiler_params=pltpu.CompilerParams(vmem_limit_bytes=40 << 20),
    )(*(() if where is None else (where,)), *arrays)


def harmonic(a, b):
    return 2.0 * a * b / (a + b)


def iota(shape, dim):
    return lax.broadcasted_iota(jnp.int32, shape, dim)


def ahead(x, axis):
    return pltpu.roll(x, x.shape[axis] - 1, axis)


def behind(x, axis):
    return pltpu.roll(x, 1, axis)


def y_faces(c):
    lane = iota(c.shape, 1)
    last = c.shape[1] - 1
    full = harmonic(c, jnp.where(lane == last, 1.0, ahead(c, 1)))
    link = jnp.where(lane == last, 0.0, full)
    first = jnp.where(iota((c.shape[0], 128), 1) == 0, harmonic(c[:, 0:128], 1.0), 0.0)
    if c.shape[1] > 128:
        first = jnp.concatenate([first, jnp.zeros((c.shape[0], c.shape[1] - 128), F32)], axis=1)
    return link, full + behind(link, 1) + first


def spread(p, below, above, cz0, cz1, cx, cy):
    total = cz0 * below + cz1 * above
    total = total + cx * ahead(p, 0) + behind(cx * p, 0)
    return total + cy * ahead(p, 1) + behind(cy * p, 1)


def pair_matrix(wide):
    shape = (wide, wide // 2)
    return (lax.shift_right_logical(iota(shape, 0), 1) == iota(shape, 1)).astype(jnp.bfloat16)


def copy_matrix(narrow):
    shape = (narrow, narrow * 2)
    return (iota(shape, 0) == lax.shift_right_logical(iota(shape, 1), 1)).astype(jnp.bfloat16)


def dot(a, ones):
    total = None
    for _ in range(3):
        part = a.astype(jnp.bfloat16)
        a = a - part.astype(F32)
        term = jnp.dot(part, ones, preferred_element_type=F32)
        total = term if total is None else total + term
    return total


def pair_rows(s, x, start, count):
    tiles = x.shape[1] // 128
    for t in range(tiles):
        s[t, 0 : x.shape[0]] = x[:, 128 * t : 128 * t + 128]
    parts = [s[t, pl.ds(start, count, stride=2), :] + s[t, pl.ds(start + 1, count, stride=2), :] for t in range(tiles)]
    return jnp.concatenate(parts, axis=1)


def copy_rows(s, x):
    tiles, count = x.shape[1] // 128, x.shape[0]
    for t in range(tiles):
        s[t, pl.ds(0, count, stride=2), :] = x[:, 128 * t : 128 * t + 128]
        s[t, pl.ds(1, count, stride=2), :] = x[:, 128 * t : 128 * t + 128]
    return jnp.concatenate([s[t, 0 : 2 * count] for t in range(tiles)], axis=1)


def inside(first, index, count):
    at = first + index
    return jnp.logical_and(at >= 0, at < count)


def k_conduct(div, density, zones, out, dens, zone_ids, sems):
    loads = []
    for z in range(4):
        loads.append(pltpu.make_async_copy(density.at[z], dens.at[z], sems.at[0, z]))
        loads.append(pltpu.make_async_copy(zones.at[z], zone_ids.at[z], sems.at[1, z]))
    loads += [pltpu.make_async_copy(div.at[z], out.at[1, z], sems.at[2, z]) for z in range(4)]
    for load in loads:
        load.start()
    for z in range(4):
        loads[2 * z].wait()
        loads[2 * z + 1].wait()
        zone = zone_ids[z]
        perm = jnp.where(zone == 0, PERMEABILITY[0], 0.0)
        for zone_id in range(1, 5):
            perm = jnp.where(zone == zone_id, PERMEABILITY[zone_id], perm)
        out[0, z] = perm / dens[z]
    for load in loads[8:]:
        load.wait()


def conductance(divergence, density, zones):
    shape = divergence.shape
    return pl.pallas_call(
        k_conduct,
        out_shape=pltpu.VMEM((2,) + shape, F32),
        in_specs=[pl.BlockSpec(memory_space=pl.ANY)] * 3,
        out_specs=vmem(1)[0],
        scratch_shapes=[pltpu.VMEM(shape, F32), pltpu.VMEM(shape, jnp.int32), pltpu.SemaphoreType.DMA((3, 4))],
    )(divergence, density, zones)


def stack0(where, own, core, link, put):
    h, high = where[0], where[2]
    odd = lax.rem(h, 2)
    for z in range(4, 8):
        put(z, own, z - 4, None)

    @pl.when(odd == 0)
    def _():
        for z in range(4):
            put(z, link, z, h == 0)
            put(z + 8, core.at[1], z, None)

    @pl.when(odd == 1)
    def _():
        for z in range(4):
            put(z, core.at[0], z, None)
            put(z + 8, link, z, h == high - 1)


MESSAGE0 = (
    (4, 0, 0, 4, 3), (5, 1, 0, 4, 3), (6, 2, 0, 4, 3), (7, 3, 0, 4, 3),
    (3, 4, 0, 3, 2), (2, 4, 5, 2, 1), (8, 5, 0, 3, 2), (9, 5, 5, 2, 1),
    (1, 0, 7, 1, 0), (10, 3, 7, 1, 0),
)


def k_edges0(where, own, core, link, left, right):
    places = {m[0]: m[1:] for m in MESSAGE0}

    def put(z, block, layer, outside):
        if z not in places:
            return
        group, at, n_cond, n_div = places[z]
        for to, cond_first, div_first in ((left, 0, 0), (right, 16 - n_cond, 16 - n_div)):
            rows = block[0, layer, cond_first : cond_first + n_cond]
            to[group, at : at + n_cond] = rows if outside is None else jnp.where(outside, 1.0, rows)
            if n_div:
                to[group, at + n_cond : at + n_cond + n_div] = block[1, layer, div_first : div_first + n_div]

    for group in range(1, 3):
        left[group, 7:8] = jnp.zeros((1, 512), F32)
        right[group, 7:8] = jnp.zeros((1, 512), F32)
    stack0(where, own, core, link, put)


def k_level0(where, own, core, near, low, high, pre, w_out, g_out, cx_out, cy_out, cz_out, pack, c, g, w, cx, cy, cz, dg, p, rs, c1, st):
    h, plan, n_h, n_p = where[0], where[1], where[2], where[3]

    def put(z, block, layer, outside):
        c[z, 4:20] = block[0, layer] if outside is None else jnp.where(outside, 1.0, block[0, layer])
        g[z, 4:20] = block[1, layer]

    stack0(where, own, core, near, put)
    for z in range(12):
        for first in (0, 20):
            c[z, first : first + 4] = jnp.ones((4, 512), F32)
            g[z, first : first + 4] = jnp.zeros((4, 512), F32)
    for z, group, at, n_cond, n_div in MESSAGE0:
        mid, end = at + n_cond, at + n_cond + n_div
        c[z, 4 - n_cond : 4] = jnp.where(plan == 0, 1.0, low[group, at:mid])
        c[z, 20 : 20 + n_cond] = jnp.where(plan == n_p - 1, 1.0, high[group, at:mid])
        if n_div:
            g[z, 4 - n_div : 4] = low[group, mid:end]
            g[z, 20 : 20 + n_div] = high[group, mid:end]
    row = iota((24, 512), 0) + (plan * 16 - 4)
    row_in = jnp.logical_and(row >= 0, row < n_p * 16).astype(F32) * OMEGA
    for z in range(11):
        cz[z] = harmonic(c[z], c[z + 1])
    for z in range(1, 11):
        here = c[z]
        fx = harmonic(here, ahead(here, 0))
        link, both = y_faces(here)
        diag = cz[z - 1] + cz[z] + fx + behind(fx, 0) + both
        weight = jnp.where(inside(h * 4 - 4, z, n_h * 4), row_in, 0.0) / diag
        cx[z] = fx
        cy[z] = link
        w[z] = weight
        if 4 <= z <= 7:
            dg[z - 4] = diag
            rs[z - 4] = g[z]
        g[z] = weight * g[z]
    for z in range(2, 10):
        here = g[z]
        total = spread(here, g[z - 1], g[z + 1], cz[z - 1], cz[z], cx[z], cy[z])
        p[z] = here * (1.0 / 3.0) + here + w[z] * total
    for z in range(4, 8):
        here = p[z]
        total = spread(here, p[z - 1], p[z + 1], cz[z - 1], cz[z], cx[z], cy[z])
        rs[z - 4] = rs[z - 4] - dg[z - 4] * here + total
    for z in range(2, 10):
        pre[z - 2] = p[z]
    for z in range(3, 9):
        w_out[z - 3] = w[z]
        g_out[z - 3] = g[z]
        cx_out[z - 3] = cx[z]
        cy_out[z - 3] = cy[z]
    for z in range(2, 9):
        cz_out[z - 2] = cz[z]
    rows = [pair_rows(st.at[z], rs[2 * z] + rs[2 * z + 1], 4, 8) for z in range(2)]
    for z in range(4):
        sums = c[2 * z + 2] + c[2 * z + 3]
        c1[z, 0:8] = pair_rows(st.at[2 + 2 * z], sums, 0, 8)
        c1[z, 8:12] = pair_rows(st.at[3 + 2 * z], sums[16:24], 0, 4)
        c1[z, 12:16] = jnp.full((4, 512), 4.0, F32)
    pairs = pair_matrix(512)
    f1 = 0.5 * dot(jnp.concatenate(rows, axis=0), pairs)
    k1 = 0.125 * dot(jnp.concatenate([c1[z] for z in range(4)], axis=0), pairs)
    k1 = [k1[16 * z : 16 * z + 16] for z in range(4)]
    for z in range(2):
        here = k1[z + 1]
        fx = harmonic(here, ahead(here, 0))
        link, both = y_faces(here)
        diag = harmonic(here, k1[z]) + harmonic(here, k1[z + 2]) + fx + behind(fx, 0) + both
        c1[z, :, 0:256] = here
        c1[z, :, 256:512] = diag
        pack[z, 0:8] = OMEGA * f1[8 * z : 8 * z + 8] / c1[z, 2:10, 256:512]
        pack[z, 8:16] = c1[z, 2:10, 0:256]


def layers1(chip, two):
    below = [two.at[0, 1, z] for z in range(2)] + [two.at[0, 0, z] for z in range(2)]
    above = [two.at[1, 0, z] for z in range(2)] + [two.at[1, 1, z] for z in range(2)]
    return below + [chip.at[z] for z in range(4)] + above


def k_edges1(where, chip, two, edge):
    h, high = where[0], where[2]
    odd = lax.rem(h, 2)
    for side in range(2):

        @pl.when(odd == side)
        def _():
            for z, rows in enumerate(layers1(chip, two)):
                keep = inside((h - side) * 2 - 4, z, high * 2)
                edge[z, 0:4] = jnp.where(keep, rows[4 * side : 4 * side + 4], 0.0)
                edge[z, 4:8] = jnp.where(keep, rows[4 * side + 8 : 4 * side + 12], 1.0)


def k_level1(where, chip, two, sides, pre, w_out, g_out, cx_out, cy_out, cz_out, copies, c, g, w, cx, cy, cz, dg, rs, st):
    h, plan, n_h, n_p = where[0], where[1], where[2], where[3]

    odd = lax.rem(h, 2)
    for side in range(2):

        @pl.when(odd == side)
        def _():
            for z, rows in enumerate(layers1(chip, two)[2 * side : 2 * side + 10]):
                keep = inside(h * 2 - 4, z, n_h * 2)
                g[z, 4:12] = jnp.where(keep, rows[0:8], 0.0)
                c[z, 4:12] = jnp.where(keep, rows[8:16], 1.0)

    for z in range(10):
        low, high = sides[0, 2 * odd + z], sides[1, 2 * odd + z]
        g[z, 0:4] = jnp.where(plan == 0, 0.0, low[0:4])
        c[z, 0:4] = jnp.where(plan == 0, 1.0, low[4:8])
        g[z, 12:16] = jnp.where(plan == n_p - 1, 0.0, high[0:4])
        c[z, 12:16] = jnp.where(plan == n_p - 1, 1.0, high[4:8])
    row = iota((16, 256), 0) + (plan * 8 - 4)
    row_in = jnp.logical_and(row >= 0, row < n_p * 8).astype(F32) * OMEGA
    for z in range(9):
        cz[z] = harmonic(c[z], c[z + 1])
    for z in range(1, 9):
        here = c[z]
        fx = harmonic(here, ahead(here, 0))
        link, both = y_faces(here)
        diag = cz[z - 1] + cz[z] + fx + behind(fx, 0) + both
        cx[z] = fx
        cy[z] = link
        w[z] = jnp.where(inside(h * 2 - 4, z, n_h * 2), row_in, 0.0) / diag
        if 4 <= z <= 5:
            dg[z - 4] = diag
    for z in range(1, 9):
        here = g[z]
        total = spread(here, g[z - 1], g[z + 1], cz[z - 1], cz[z], cx[z], cy[z])
        pre[z - 1] = here * (1.0 / 3.0) + here + w[z] * total
    for z in range(4, 6):
        here = pre[z - 1]
        total = spread(here, pre[z - 2], pre[z], cz[z - 1], cz[z], cx[z], cy[z])
        rs[z - 4] = (g[z] - OMEGA * here + w[z] * total) * dg[z - 4] * 1.5
    for z in range(2, 8):
        w_out[z - 2] = w[z]
        g_out[z - 2] = g[z]
        cx_out[z - 2] = cx[z]
        cy_out[z - 2] = cy[z]
    for z in range(1, 8):
        cz_out[z - 1] = cz[z]
    rows = [pair_rows(st.at[0], rs[0] + rs[1], 0, 8)]
    rows += [pair_rows(st.at[z + 1], c[2 * z + 2] + c[2 * z + 3], 0, 8) for z in range(3)]
    pairs = pair_matrix(256)
    both = jnp.concatenate(rows, axis=0)
    down = dot(both, pairs)
    f2 = 0.5 * down[0:8]
    k2 = [0.125 * down[8 * z + 8 : 8 * z + 16] for z in range(3)]
    here = k2[1]
    fx = harmonic(here, ahead(here, 0))
    link, share = y_faces(here)
    diag = harmonic(here, k2[0]) + harmonic(here, k2[2]) + fx + behind(fx, 0) + share
    dg[0, 0:8, 0:128] = diag
    dg[0, 8:16, 0:128] = here
    tile_g = OMEGA * f2[2:6] / dg[0, 2:6, 0:128]
    tile_c = dg[0, 10:14, 0:128]
    for i in range(copies.shape[0]):
        copies[i, 0:4] = tile_g
        copies[i, 4:8] = tile_c


def k_up(where, block, outer, pre1, w1, g1, cx1, cy1, cz1, pre0, w0, g0, cx0, cy0, cz0, out, sems, s, c, g, w, cx, cy, cz, dg, pa, pb, p2, u1, q1, u0, q0, s1, s0, done):
    h, plan, n_h = where[0], where[1], where[2]
    wide = s.shape[1] // 2
    tiles = wide // 4
    for z in range(14):
        for t in range(tiles):
            at = tiles * (z % 2) + t
            rows = block.at[at] if 6 <= z < 8 else outer.at[z // 8, z % 8 // 2 if z < 6 else (z - 8) // 2, at]
            s[z, 4 * t : 4 * t + 4] = rows[0:4]
            s[z, wide + 4 * t : wide + 4 * t + 4] = rows[4:8]
    q = lax.rem(h, 2)
    for z in range(13):
        keep = inside(h - 6, z, n_h)
        g[z] = jnp.where(keep, s[q + z, 0:wide], 0.0)
        c[z] = jnp.where(keep, s[q + z, wide : 2 * wide], 1.0)
    row = iota((wide, 128), 0)
    for z in range(12):
        cz[z] = harmonic(c[z], c[z + 1])
    for z in range(1, 12):
        here = c[z]
        full = harmonic(here, jnp.where(row == wide - 1, 1.0, ahead(here, 0)))
        fx = jnp.where(row == wide - 1, 0.0, full)
        first = jnp.where(row[0:8] == 0, harmonic(here[0:8], 1.0), 0.0)
        first = jnp.concatenate([first, jnp.zeros((wide - 8, 128), F32)], axis=0)
        link, both = y_faces(here)
        diag = cz[z - 1] + cz[z] + full + behind(fx, 0) + first + both
        cx[z] = fx
        cy[z] = link
        w[z] = jnp.where(inside(h - 6, z, n_h), OMEGA, 0.0) / diag
        dg[z] = diag

    def step(source, z):
        here = source[z]
        total = spread(here, source[z - 1], source[z + 1], cz[z - 1], cz[z], cx[z], cy[z])
        return here * (1.0 / 3.0) + g[z] + w[z] * total

    for z in range(1, 12):
        pa[z] = step(g, z)
    for z in range(2, 11):
        pb[z] = step(pa, z)
    for z in range(3, 10):
        pa[z] = step(pb, z)
    for z in range(4, 9):
        here = pa[z]
        extra = (step(pa, z) - here) * dg[z] * 1.5
        line = jnp.sum(extra, axis=0, keepdims=True) / jnp.sum(dg[z], axis=0, keepdims=True)
        p2[z - 4, 0:8] = jnp.zeros((8, 128), F32)
        p2[z - 4, wide + 8 : wide + 16] = jnp.zeros((8, 128), F32)
        p2[z - 4, 8 : wide + 8] = here + line
    rows = jnp.concatenate([p2[z, pl.ds(plan * 4 + 6, 8), :] for z in range(5)], axis=0)
    rows = dot(rows, copy_matrix(128))
    for z in range(5):
        u1[z] = copy_rows(s1.at[z], rows[8 * z : 8 * z + 8])
    for z in range(1, 9):
        q1[z - 1] = pre1[z - 1] + u1[z // 2]
    mid = []
    for z in range(2, 8):
        here = q1[z - 1]
        total = spread(here, q1[z - 2], q1[z], cz1[z - 2], cz1[z - 1], cx1[z - 2], cy1[z - 2])
        pb_rows = here * (1.0 / 3.0) + g1[z - 2] + w1[z - 2] * total
        mid.append(pb_rows)
    for z in range(6):
        q1[z] = mid[z]
    low = []
    for z in range(3, 7):
        here = q1[z - 2]
        total = spread(here, q1[z - 3], q1[z - 1], cz1[z - 2], cz1[z - 1], cx1[z - 2], cy1[z - 2])
        low.append(here * (1.0 / 3.0) + g1[z - 2] + w1[z - 2] * total)
    for z in range(4):
        q1[z] = low[z]
    rows = jnp.concatenate([q1[z] for z in range(4)], axis=0)
    rows = dot(rows, copy_matrix(256))
    for z in range(4):
        u0[z] = copy_rows(s0.at[z], rows[16 * z : 16 * z + 16])
    for z in range(2, 10):
        q0[z - 2] = pre0[z - 2] + u0[z // 2 - 1, 4:28]
    for z in range(3, 9):
        here = q0[z - 2]
        total = spread(here, q0[z - 3], q0[z - 1], cz0[z - 3], cz0[z - 2], cx0[z - 3], cy0[z - 3])
        u0[z - 3, 0:24] = here * (1.0 / 3.0) + g0[z - 3] + w0[z - 3] * total
    stores = []
    for z in range(4, 8):
        here = u0[z - 3, 0:24]
        total = spread(here, u0[z - 4, 0:24], u0[z - 2, 0:24], cz0[z - 3], cz0[z - 2], cx0[z - 3], cy0[z - 3])
        q0[z - 4] = here * (1.0 / 3.0) + g0[z - 3] + w0[z - 3] * total
        done[z - 4] = q0[z - 4, 4:20]
        stores.append(pltpu.make_async_copy(done.at[z - 4], out.at[z - 4], sems.at[z - 4]))
        stores[-1].start()
    for store in stores:
        store.wait()


def on_device(divergence, density, zones):
    n_h, n_p = lax.axis_size("height"), lax.axis_size("plan")
    h, plan = lax.axis_index("height"), lax.axis_index("plan")
    odd = lax.rem(h, 2)
    where = jnp.stack([h, plan, jnp.int32(n_h), jnp.int32(n_p)])
    cores = [[i, i + 1] for i in range(0, n_h, 2)]
    links = [[i, (i + 1) % n_h] for i in range(1, n_h, 2)]

    def pair(x, groups):
        return lax.all_gather(x, "height", axis=0, tiled=False, axis_index_groups=groups)

    def beside(low_rows, high_rows):
        up = [(i, i + 1) for i in range(n_p - 1)]
        down = [(i + 1, i) for i in range(n_p - 1)]
        return lax.ppermute(high_rows, "plan", up), lax.ppermute(low_rows, "plan", down)

    own = conductance(divergence, density, zones)
    swap = [(i, i + 1) for i in range(1, n_h - 1, 2)] + [(i + 1, i) for i in range(1, n_h - 1, 2)]
    near = lax.ppermute(own, "height", swap)
    core = pair(own, cores)
    left, right = call(k_edges0, [(6, 8, 512)] * 2, [], where, own, core, near)
    low, high = beside(left, right)
    box = (12, 24, 512)
    eight, six, seven = (8, 24, 512), (6, 24, 512), (7, 24, 512)
    *level0, pack = call(
        k_level0,
        [eight, six, six, six, six, seven, (2, 16, 256)],
        [box] * 6 + [(4, 24, 512), box, (4, 24, 512), (4, 16, 512), (10, 4, 24, 128)],
        where, own, core, near, low, high,
    )
    near = lax.ppermute(pack, "height", swap)
    skip = [(i, i + 2) for i in range(0, n_h - 2, 2)] + [(i + 2, i) for i in range(1, n_h - 2, 2)]
    beyond = lax.ppermute(pack, "height", skip)
    chip = pair(pack, cores).reshape(4, 16, 256)
    two = pair(jnp.stack([near, beyond]), cores)
    edge = call(k_edges1, (12, 8, 256), [], where, chip, two)
    across = [[(2 * i + 1) * n_p + t, 2 * i * n_p + (t + 1) % n_p] for i in range(n_h // 2) for t in range(n_p)]
    edge = lax.all_gather(edge, ("height", "plan"), axis=0, tiled=False, axis_index_groups=across)
    sides = pair(lax.dynamic_index_in_dim(edge, odd, 0, keepdims=False), cores)
    box = (10, 16, 256)
    eight, six, seven = (8, 16, 256), (6, 16, 256), (7, 16, 256)
    *level1, tiles = call(
        k_level1,
        [eight, six, six, six, six, seven, (2 * n_p, 8, 128)],
        [box] * 6 + [(2, 16, 256), (2, 16, 256), (4, 2, 16, 128)],
        where, chip, two, sides,
    )
    groups = [[(2 * i + k) * n_p + t for k in range(2) for t in range(n_p)] for i in range(n_h // 2)]
    block = lax.all_to_all(tiles, ("height", "plan"), split_axis=0, concat_axis=0, tiled=True, axis_index_groups=groups)
    near = pair(block, links)
    far = pair(near, [[i, (i + 5) % n_h] for i in range(1, n_h, 2)])
    side = jnp.where(odd == 0, jnp.concatenate([far[0], near[0:1]]), jnp.concatenate([near[1:2], far[1]]))
    outer = pair(side, cores)
    wide = n_p * 4
    flat = (13, wide, 128)
    arrays = (block, outer, *level1, *level0)
    scratch = [(14, 2 * wide, 128)] + [flat] * 9
    scratch += [(5, wide + 16, 128), (5, 16, 256), (8, 16, 256), (6, 32, 512), (8, 24, 512), (5, 2, 16, 128), (4, 4, 32, 128), (4, 16, 512)]
    return pl.pallas_call(
        k_up,
        out_shape=jax.ShapeDtypeStruct((4, 16, 512), F32),
        in_specs=[smem()] + vmem(len(arrays)),
        out_specs=pl.BlockSpec(memory_space=pl.ANY),
        scratch_shapes=[pltpu.SemaphoreType.DMA((4,))] + [pltpu.VMEM(s, F32) for s in scratch],
        compiler_params=pltpu.CompilerParams(vmem_limit_bytes=40 << 20),
    )(where, *arrays)


def solution(mesh):
    return jax.shard_map(
        on_device,
        mesh=mesh,
        in_specs=(P("height", "plan", None), P("height", "plan", None), P("height", "plan", None)),
        out_specs=P("height", "plan", None),
        check_vma=False,
    )
```

```python
import jax
import jax.numpy as jnp
from jax import lax
from jax.experimental import pallas as pl
from jax.experimental.pallas import tpu as pltpu
from jax.sharding import PartitionSpec as P

PERMEABILITY = (1.0, 0.1, 0.6, 0.8, 0.25)
OMEGA = 2.0 / 3.0
F32 = jnp.float32


def vmem(count):
    return [pl.BlockSpec(memory_space=pltpu.VMEM)] * count


def position():
    return lax.axis_index("height"), lax.axis_index("plan"), lax.axis_size("height"), lax.axis_size("plan")


def call(body, outs, scratch, *arrays):
    many = isinstance(outs, list)
    shapes = [pltpu.VMEM(s, F32) for s in (outs if many else [outs])]
    return pl.pallas_call(
        body,
        out_shape=shapes if many else shapes[0],
        in_specs=vmem(len(arrays)),
        out_specs=vmem(len(shapes)) if many else vmem(1)[0],
        scratch_shapes=[pltpu.VMEM(s, F32) for s in scratch],
        compiler_params=pltpu.CompilerParams(vmem_limit_bytes=40 << 20),
    )(*arrays)


def harmonic(a, b):
    return 2.0 * a * b / (a + b)


def iota(shape, dim):
    return lax.broadcasted_iota(jnp.int32, shape, dim)


def ahead(x, axis):
    return pltpu.roll(x, x.shape[axis] - 1, axis)


def behind(x, axis):
    return pltpu.roll(x, 1, axis)


def y_faces(c):
    lane = iota(c.shape, 1)
    last = c.shape[1] - 1
    full = harmonic(c, jnp.where(lane == last, 1.0, ahead(c, 1)))
    link = jnp.where(lane == last, 0.0, full)
    first = jnp.where(iota((c.shape[0], 128), 1) == 0, harmonic(c[:, 0:128], 1.0), 0.0)
    if c.shape[1] > 128:
        first = jnp.concatenate([first, jnp.zeros((c.shape[0], c.shape[1] - 128), F32)], axis=1)
    return link, full + behind(link, 1) + first


def spread(p, below, above, cz0, cz1, cx, cy):
    total = cz0 * below + cz1 * above
    total = total + cx * ahead(p, 0) + behind(cx * p, 0)
    return total + cy * ahead(p, 1) + behind(cy * p, 1)


def pair_matrix(wide):
    shape = (wide, wide // 2)
    return (lax.shift_right_logical(iota(shape, 0), 1) == iota(shape, 1)).astype(jnp.bfloat16)


def copy_matrix(narrow):
    shape = (narrow, narrow * 2)
    return (iota(shape, 0) == lax.shift_right_logical(iota(shape, 1), 1)).astype(jnp.bfloat16)


def dot(a, ones):
    total = None
    for _ in range(3):
        part = a.astype(jnp.bfloat16)
        a = a - part.astype(F32)
        term = jnp.dot(part, ones, preferred_element_type=F32)
        total = term if total is None else total + term
    return total


def pair_rows(s, x, start, count):
    tiles = x.shape[1] // 128
    for t in range(tiles):
        s[t, 0 : x.shape[0]] = x[:, 128 * t : 128 * t + 128]
    parts = [s[t, pl.ds(start, count, stride=2), :] + s[t, pl.ds(start + 1, count, stride=2), :] for t in range(tiles)]
    return jnp.concatenate(parts, axis=1)


def copy_rows(s, x):
    tiles, count = x.shape[1] // 128, x.shape[0]
    for t in range(tiles):
        s[t, pl.ds(0, count, stride=2), :] = x[:, 128 * t : 128 * t + 128]
        s[t, pl.ds(1, count, stride=2), :] = x[:, 128 * t : 128 * t + 128]
    return jnp.concatenate([s[t, 0 : 2 * count] for t in range(tiles)], axis=1)


def inside(first, index, count):
    at = first + index
    return jnp.logical_and(at >= 0, at < count)


def k_conduct(div, density, zones, out, dens, zone_ids, sems):
    loads = []
    for z in range(4):
        loads.append(pltpu.make_async_copy(density.at[z], dens.at[z], sems.at[0, z]))
        loads.append(pltpu.make_async_copy(zones.at[z], zone_ids.at[z], sems.at[1, z]))
    loads += [pltpu.make_async_copy(div.at[z], out.at[1, z], sems.at[2, z]) for z in range(4)]
    for load in loads:
        load.start()
    for z in range(4):
        loads[2 * z].wait()
        loads[2 * z + 1].wait()
        zone = zone_ids[z]
        perm = jnp.where(zone == 0, PERMEABILITY[0], 0.0)
        for zone_id in range(1, 5):
            perm = jnp.where(zone == zone_id, PERMEABILITY[zone_id], perm)
        out[0, z] = perm / dens[z]
    for load in loads[8:]:
        load.wait()


def conductance(divergence, density, zones):
    shape = divergence.shape
    return pl.pallas_call(
        k_conduct,
        out_shape=pltpu.VMEM((2,) + shape, F32),
        in_specs=[pl.BlockSpec(memory_space=pl.ANY)] * 3,
        out_specs=vmem(1)[0],
        scratch_shapes=[pltpu.VMEM(shape, F32), pltpu.VMEM(shape, jnp.int32), pltpu.SemaphoreType.DMA((3, 4))],
    )(divergence, density, zones)


def stack0(own, core, link, put):
    h, _, high, _ = position()
    odd = lax.rem(h, 2)
    for z in range(4, 8):
        put(z, own, z - 4, None)

    @pl.when(odd == 0)
    def _():
        for z in range(4):
            put(z, link, z, h == 0)
            put(z + 8, core.at[1], z, None)

    @pl.when(odd == 1)
    def _():
        for z in range(4):
            put(z, core.at[0], z, None)
            put(z + 8, link, z, h == high - 1)


def k_edges0(core, edge):
    odd = lax.rem(lax.axis_index("height"), 2)
    for side in range(2):

        @pl.when(odd == side)
        def _():
            for z in range(8):
                edge[z, 0:4] = core[z // 4, 0, z % 4, 12 * side : 12 * side + 4]
                edge[z, 4:7] = core[z // 4, 1, z % 4, 13 * side : 13 * side + 3]
                edge[z, 7:8] = jnp.zeros((1, 512), F32)


def k_level0(own, core, near, sides, corner, pre, w_out, g_out, cx_out, cy_out, cz_out, pack, c, g, w, cx, cy, cz, dg, p, rs, c1, st):
    h, plan, n_h, n_p = position()

    def put(z, block, layer, outside):
        c[z, 4:20] = block[0, layer] if outside is None else jnp.where(outside, 1.0, block[0, layer])
        g[z, 4:20] = block[1, layer]

    stack0(own, core, near, put)
    for z in range(12):
        for first in (0, 20):
            c[z, first : first + 4] = jnp.ones((4, 512), F32)
            g[z, first : first + 4] = jnp.zeros((4, 512), F32)
    odd = lax.rem(h, 2)
    for par in range(2):

        @pl.when(odd == par)
        def _():
            for z in range(1, 11):
                inner = z < 8 if par else z >= 4
                at = z if par else z - 4
                for side, first, end in ((0, 0, plan == 0), (1, 20, plan == n_p - 1)):
                    rows = sides.at[side, at] if inner else corner.at[par, side, z - 8 if par else z - 1]
                    out = end if inner else jnp.logical_or(end, h == (n_h - 1 if par else 0))
                    c[z, first : first + 4] = jnp.where(out, 1.0, rows[0:4])
                    g[z, first + 1 - side : first + 4 - side] = rows[4:7]

    row = iota((24, 512), 0) + (plan * 16 - 4)
    row_in = jnp.logical_and(row >= 0, row < n_p * 16).astype(F32) * OMEGA
    for z in range(11):
        cz[z] = harmonic(c[z], c[z + 1])
    for z in range(1, 11):
        here = c[z]
        fx = harmonic(here, ahead(here, 0))
        link, both = y_faces(here)
        diag = cz[z - 1] + cz[z] + fx + behind(fx, 0) + both
        weight = jnp.where(inside(h * 4 - 4, z, n_h * 4), row_in, 0.0) / diag
        cx[z] = fx
        cy[z] = link
        w[z] = weight
        if 4 <= z <= 7:
            dg[z - 4] = diag
            rs[z - 4] = g[z]
        g[z] = weight * g[z]
    for z in range(2, 10):
        here = g[z]
        total = spread(here, g[z - 1], g[z + 1], cz[z - 1], cz[z], cx[z], cy[z])
        p[z] = here * (1.0 / 3.0) + here + w[z] * total
    for z in range(4, 8):
        here = p[z]
        total = spread(here, p[z - 1], p[z + 1], cz[z - 1], cz[z], cx[z], cy[z])
        rs[z - 4] = rs[z - 4] - dg[z - 4] * here + total
    for z in range(2, 10):
        pre[z - 2] = p[z]
    for z in range(3, 9):
        w_out[z - 3] = w[z]
        g_out[z - 3] = g[z]
        cx_out[z - 3] = cx[z]
        cy_out[z - 3] = cy[z]
    for z in range(2, 9):
        cz_out[z - 2] = cz[z]
    rows = [pair_rows(st.at[z], rs[2 * z] + rs[2 * z + 1], 4, 8) for z in range(2)]
    for z in range(4):
        sums = c[2 * z + 2] + c[2 * z + 3]
        c1[z, 0:8] = pair_rows(st.at[2 + 2 * z], sums, 0, 8)
        c1[z, 8:12] = pair_rows(st.at[3 + 2 * z], sums[16:24], 0, 4)
        c1[z, 12:16] = jnp.full((4, 512), 4.0, F32)
    pairs = pair_matrix(512)
    f1 = 0.5 * dot(jnp.concatenate(rows, axis=0), pairs)
    k1 = 0.125 * dot(jnp.concatenate([c1[z] for z in range(4)], axis=0), pairs)
    k1 = [k1[16 * z : 16 * z + 16] for z in range(4)]
    for z in range(2):
        here = k1[z + 1]
        fx = harmonic(here, ahead(here, 0))
        link, both = y_faces(here)
        diag = harmonic(here, k1[z]) + harmonic(here, k1[z + 2]) + fx + behind(fx, 0) + both
        c1[z, :, 0:256] = here
        c1[z, :, 256:512] = diag
        pack[z, 0:8] = OMEGA * f1[8 * z : 8 * z + 8] / c1[z, 2:10, 256:512]
        pack[z, 8:16] = c1[z, 2:10, 0:256]


def k_edges1(chip, edge):
    odd = lax.rem(lax.axis_index("height"), 2)
    for side in range(2):

        @pl.when(odd == side)
        def _():
            for z in range(4):
                edge[z, 0:4] = chip[z, 4 * side : 4 * side + 4]
                edge[z, 4:8] = chip[z, 4 * side + 8 : 4 * side + 12]


def window1(even_layers, odd_layers, first, g, c):
    h, plan, n_h, n_p = position()
    for side, layers in ((0, even_layers), (1, odd_layers)):

        @pl.when(lax.rem(h, 2) == side)
        def _():
            for z, rows in enumerate(layers):
                keep = inside(first, z, n_h * 2)
                low, high = jnp.logical_and(keep, plan > 0), jnp.logical_and(keep, plan < n_p - 1)
                g[z, 4:12] = jnp.where(keep, rows[0:8], 0.0)
                c[z, 4:12] = jnp.where(keep, rows[8:16], 1.0)
                g[z, 0:4] = jnp.where(low, rows[16:20], 0.0)
                c[z, 0:4] = jnp.where(low, rows[20:24], 1.0)
                g[z, 12:16] = jnp.where(high, rows[24:28], 0.0)
                c[z, 12:16] = jnp.where(high, rows[28:32], 1.0)


def couple1(count, first, c, w, cx, cy, cz):
    h, plan, n_h, n_p = position()
    row = iota((16, 256), 0) + (plan * 8 - 4)
    row_in = jnp.logical_and(row >= 0, row < n_p * 8).astype(F32) * OMEGA
    for z in range(count - 1):
        cz[z] = harmonic(c[z], c[z + 1])
    diags = {}
    for z in range(1, count - 1):
        here = c[z]
        fx = harmonic(here, ahead(here, 0))
        link, both = y_faces(here)
        diags[z] = cz[z - 1] + cz[z] + fx + behind(fx, 0) + both
        cx[z] = fx
        cy[z] = link
        w[z] = jnp.where(inside(first, z, n_h * 2), row_in, 0.0) / diags[z]
    return diags


def k_level1_wide(full, two, pre, w_out, g_out, cx_out, cy_out, cz_out, c, g, w, cx, cy, cz):
    first = lax.axis_index("height") * 2 - 4
    layers = [two.at[0, z] for z in range(4)] + [full.at[z] for z in range(4)] + [two.at[1, z] for z in range(4)]
    window1(layers[0:10], layers[2:12], first, g, c)
    couple1(10, first, c, w, cx, cy, cz)
    for z in range(1, 9):
        here = g[z]
        total = spread(here, g[z - 1], g[z + 1], cz[z - 1], cz[z], cx[z], cy[z])
        pre[z - 1] = here * (1.0 / 3.0) + here + w[z] * total
    for z in range(2, 8):
        w_out[z - 2] = w[z]
        g_out[z - 2] = g[z]
        cx_out[z - 2] = cx[z]
        cy_out[z - 2] = cy[z]
    for z in range(1, 8):
        cz_out[z - 1] = cz[z]


def k_level1(full, near, copies, c, g, w, cx, cy, cz, p, rs, dg, st):
    first = lax.axis_index("height") * 2 - 2
    middle = [full.at[z] for z in range(4)]
    window1([near.at[0, 2], near.at[0, 3]] + middle, middle + [near.at[1, 0], near.at[1, 1]], first, g, c)
    diags = couple1(6, first, c, w, cx, cy, cz)
    for z in range(2):
        rs[z] = diags[z + 2]
    for z in range(1, 5):
        here = g[z]
        total = spread(here, g[z - 1], g[z + 1], cz[z - 1], cz[z], cx[z], cy[z])
        p[z] = here * (1.0 / 3.0) + here + w[z] * total
    for z in range(2, 4):
        here = p[z]
        total = spread(here, p[z - 1], p[z + 1], cz[z - 1], cz[z], cx[z], cy[z])
        rs[z - 2] = (g[z] - OMEGA * here + w[z] * total) * rs[z - 2] * 1.5
    rows = [pair_rows(st.at[0], rs[0] + rs[1], 0, 8)]
    rows += [pair_rows(st.at[z + 1], c[2 * z] + c[2 * z + 1], 0, 8) for z in range(3)]
    pairs = pair_matrix(256)
    both = jnp.concatenate(rows, axis=0)
    down = dot(both, pairs)
    f2 = 0.5 * down[0:8]
    k2 = [0.125 * down[8 * z + 8 : 8 * z + 16] for z in range(3)]
    here = k2[1]
    fx = harmonic(here, ahead(here, 0))
    link, share = y_faces(here)
    diag = harmonic(here, k2[0]) + harmonic(here, k2[2]) + fx + behind(fx, 0) + share
    dg[0, 0:8, 0:128] = diag
    dg[0, 8:16, 0:128] = here
    tile_g = OMEGA * f2[2:6] / dg[0, 2:6, 0:128]
    tile_c = dg[0, 10:14, 0:128]
    for i in range(copies.shape[0]):
        copies[i, 0:4] = tile_g
        copies[i, 4:8] = tile_c


def k_up(block, outer, pre1, w1, g1, cx1, cy1, cz1, pre0, w0, g0, cx0, cy0, cz0, out, sems, s, c, g, w, cx, cy, cz, dg, pa, pb, p2, u1, q1, u0, q0, s1, s0, done):
    h, plan, n_h, _ = position()
    wide = s.shape[1] // 2
    tiles = wide // 4
    for z in range(14):
        for t in range(tiles):
            at = tiles * (z % 2) + t
            rows = block.at[at] if 6 <= z < 8 else outer.at[z // 8, z % 8 // 2 if z < 6 else (z - 8) // 2, at]
            s[z, 4 * t : 4 * t + 4] = rows[0:4]
            s[z, wide + 4 * t : wide + 4 * t + 4] = rows[4:8]
    q = lax.rem(h, 2)
    for z in range(13):
        keep = inside(h - 6, z, n_h)
        g[z] = jnp.where(keep, s[q + z, 0:wide], 0.0)
        c[z] = jnp.where(keep, s[q + z, wide : 2 * wide], 1.0)
    row = iota((wide, 128), 0)
    for z in range(12):
        cz[z] = harmonic(c[z], c[z + 1])
    for z in range(1, 12):
        here = c[z]
        full = harmonic(here, jnp.where(row == wide - 1, 1.0, ahead(here, 0)))
        fx = jnp.where(row == wide - 1, 0.0, full)
        first = jnp.where(row[0:8] == 0, harmonic(here[0:8], 1.0), 0.0)
        first = jnp.concatenate([first, jnp.zeros((wide - 8, 128), F32)], axis=0)
        link, both = y_faces(here)
        diag = cz[z - 1] + cz[z] + full + behind(fx, 0) + first + both
        cx[z] = fx
        cy[z] = link
        w[z] = jnp.where(inside(h - 6, z, n_h), OMEGA, 0.0) / diag
        dg[z] = diag

    def step(source, z):
        here = source[z]
        total = spread(here, source[z - 1], source[z + 1], cz[z - 1], cz[z], cx[z], cy[z])
        return here * (1.0 / 3.0) + g[z] + w[z] * total

    for z in range(1, 12):
        pa[z] = step(g, z)
    for z in range(2, 11):
        pb[z] = step(pa, z)
    for z in range(3, 10):
        pa[z] = step(pb, z)
    for z in range(4, 9):
        here = pa[z]
        extra = (step(pa, z) - here) * dg[z] * 1.5
        line = jnp.sum(extra, axis=0, keepdims=True) / jnp.sum(dg[z], axis=0, keepdims=True)
        p2[z - 4, 0:8] = jnp.zeros((8, 128), F32)
        p2[z - 4, wide + 8 : wide + 16] = jnp.zeros((8, 128), F32)
        p2[z - 4, 8 : wide + 8] = here + line
    rows = jnp.concatenate([p2[z, pl.ds(plan * 4 + 6, 8), :] for z in range(5)], axis=0)
    rows = dot(rows, copy_matrix(128))
    for z in range(5):
        u1[z] = copy_rows(s1.at[z], rows[8 * z : 8 * z + 8])
    for z in range(1, 9):
        q1[z - 1] = pre1[z - 1] + u1[z // 2]
    mid = []
    for z in range(2, 8):
        here = q1[z - 1]
        total = spread(here, q1[z - 2], q1[z], cz1[z - 2], cz1[z - 1], cx1[z - 2], cy1[z - 2])
        pb_rows = here * (1.0 / 3.0) + g1[z - 2] + w1[z - 2] * total
        mid.append(pb_rows)
    for z in range(6):
        q1[z] = mid[z]
    low = []
    for z in range(3, 7):
        here = q1[z - 2]
        total = spread(here, q1[z - 3], q1[z - 1], cz1[z - 2], cz1[z - 1], cx1[z - 2], cy1[z - 2])
        low.append(here * (1.0 / 3.0) + g1[z - 2] + w1[z - 2] * total)
    for z in range(4):
        q1[z] = low[z]
    rows = jnp.concatenate([q1[z] for z in range(4)], axis=0)
    rows = dot(rows, copy_matrix(256))
    for z in range(4):
        u0[z] = copy_rows(s0.at[z], rows[16 * z : 16 * z + 16])
    for z in range(2, 10):
        q0[z - 2] = pre0[z - 2] + u0[z // 2 - 1, 4:28]
    for z in range(3, 9):
        here = q0[z - 2]
        total = spread(here, q0[z - 3], q0[z - 1], cz0[z - 3], cz0[z - 2], cx0[z - 3], cy0[z - 3])
        u0[z - 3, 0:24] = here * (1.0 / 3.0) + g0[z - 3] + w0[z - 3] * total
    stores = []
    for z in range(4, 8):
        here = u0[z - 3, 0:24]
        total = spread(here, u0[z - 4, 0:24], u0[z - 2, 0:24], cz0[z - 3], cz0[z - 2], cx0[z - 3], cy0[z - 3])
        q0[z - 4] = here * (1.0 / 3.0) + g0[z - 3] + w0[z - 3] * total
        done[z - 4] = q0[z - 4, 4:20]
        stores.append(pltpu.make_async_copy(done.at[z - 4], out.at[z - 4], sems.at[z - 4]))
        stores[-1].start()
    for store in stores:
        store.wait()


def on_device(divergence, density, zones):
    n_h, n_p = lax.axis_size("height"), lax.axis_size("plan")
    odd = lax.rem(lax.axis_index("height"), 2)
    cores = [[i, i + 1] for i in range(0, n_h, 2)]
    links = [[i, (i + 1) % n_h] for i in range(1, n_h, 2)]

    def pair(x, groups):
        return lax.all_gather(x, "height", axis=0, tiled=False, axis_index_groups=groups)

    own = conductance(divergence, density, zones)
    swap = [(i, i + 1) for i in range(1, n_h - 1, 2)] + [(i + 1, i) for i in range(1, n_h - 1, 2)]
    near = lax.ppermute(own, "height", swap)
    core = pair(own, cores)
    across = [[(2 * i + 1) * n_p + t, 2 * i * n_p + (t + 1) % n_p] for i in range(n_h // 2) for t in range(n_p)]

    def both_sides(edge):
        met = lax.all_gather(edge, ("height", "plan"), axis=0, tiled=False, axis_index_groups=across)
        return pair(lax.dynamic_index_in_dim(met, odd, 0, keepdims=False), cores)

    sides = both_sides(call(k_edges0, (8, 8, 512), [], core))
    corner = pair(lax.dynamic_slice_in_dim(sides, 5 * odd, 3, 1), links)
    box = (12, 24, 512)
    eight, six, seven = (8, 24, 512), (6, 24, 512), (7, 24, 512)
    *level0, pack = call(
        k_level0,
        [eight, six, six, six, six, seven, (2, 16, 256)],
        [box] * 6 + [(4, 24, 512), box, (4, 24, 512), (4, 16, 512), (10, 4, 24, 128)],
        own, core, near, sides, corner,
    )
    chip = pair(pack, cores).reshape(4, 16, 256)
    sides = both_sides(call(k_edges1, (4, 8, 256), [], chip))
    full = jnp.concatenate([chip, sides[0], sides[1]], axis=1)
    near = pair(full, links)
    box = (6, 16, 256)
    tiles = call(k_level1, (2 * n_p, 8, 128), [box] * 7 + [(2, 16, 256), (2, 16, 256), (4, 2, 16, 128)], full, near)
    two = pair(lax.dynamic_index_in_dim(near, odd, 0, keepdims=False), cores)
    box = (10, 16, 256)
    eight, six, seven = (8, 16, 256), (6, 16, 256), (7, 16, 256)
    level1 = call(k_level1_wide, [eight, six, six, six, six, seven], [box] * 6, full, two)
    groups = [[(2 * i + k) * n_p + t for k in range(2) for t in range(n_p)] for i in range(n_h // 2)]
    block = lax.all_to_all(tiles, ("height", "plan"), split_axis=0, concat_axis=0, tiled=True, axis_index_groups=groups)
    near = pair(block, links)
    far = pair(near, [[i, (i + 5) % n_h] for i in range(1, n_h, 2)])
    side = jnp.where(odd == 0, jnp.concatenate([far[0], near[0:1]]), jnp.concatenate([near[1:2], far[1]]))
    outer = pair(side, cores)
    wide = n_p * 4
    flat = (13, wide, 128)
    arrays = (block, outer, *level1, *level0)
    scratch = [(14, 2 * wide, 128)] + [flat] * 9
    scratch += [(5, wide + 16, 128), (5, 16, 256), (8, 16, 256), (6, 32, 512), (8, 24, 512), (5, 2, 16, 128), (4, 4, 32, 128), (4, 16, 512)]
    return pl.pallas_call(
        k_up,
        out_shape=jax.ShapeDtypeStruct((4, 16, 512), F32),
        in_specs=vmem(len(arrays)),
        out_specs=pl.BlockSpec(memory_space=pl.ANY),
        scratch_shapes=[pltpu.SemaphoreType.DMA((4,))] + [pltpu.VMEM(s, F32) for s in scratch],
        compiler_params=pltpu.CompilerParams(vmem_limit_bytes=40 << 20),
    )(*arrays)


def solution(mesh):
    return jax.shard_map(
        on_device,
        mesh=mesh,
        in_specs=(P("height", "plan", None), P("height", "plan", None), P("height", "plan", None)),
        out_specs=P("height", "plan", None),
        check_vma=False,
    )
```

```python
import jax
import jax.numpy as jnp
from jax import lax
from jax.experimental import pallas as pl
from jax.experimental.pallas import tpu as pltpu
from jax.sharding import PartitionSpec as P

PERMEABILITY = (1.0, 0.1, 0.6, 0.8, 0.25)
OMEGA = 2.0 / 3.0
F32 = jnp.float32


def vmem(count):
    return [pl.BlockSpec(memory_space=pltpu.VMEM)] * count


def position():
    return lax.axis_index("height"), lax.axis_index("plan"), lax.axis_size("height"), lax.axis_size("plan")


def call(body, outs, scratch, *arrays):
    many = isinstance(outs, list)
    shapes = [pltpu.VMEM(s, F32) for s in (outs if many else [outs])]
    return pl.pallas_call(
        body,
        out_shape=shapes if many else shapes[0],
        in_specs=vmem(len(arrays)),
        out_specs=vmem(len(shapes)) if many else vmem(1)[0],
        scratch_shapes=[pltpu.VMEM(s, F32) for s in scratch],
        compiler_params=pltpu.CompilerParams(vmem_limit_bytes=40 << 20),
    )(*arrays)


def harmonic(a, b):
    return 2.0 * a * b / (a + b)


def iota(shape, dim):
    return lax.broadcasted_iota(jnp.int32, shape, dim)


def ahead(x, axis):
    return pltpu.roll(x, x.shape[axis] - 1, axis)


def behind(x, axis):
    return pltpu.roll(x, 1, axis)


def y_faces(c):
    lane = iota(c.shape, 1)
    last = c.shape[1] - 1
    full = harmonic(c, jnp.where(lane == last, 1.0, ahead(c, 1)))
    link = jnp.where(lane == last, 0.0, full)
    first = jnp.where(iota((c.shape[0], 128), 1) == 0, harmonic(c[:, 0:128], 1.0), 0.0)
    if c.shape[1] > 128:
        first = jnp.concatenate([first, jnp.zeros((c.shape[0], c.shape[1] - 128), F32)], axis=1)
    return link, full + behind(link, 1) + first


def spread(p, below, above, cz0, cz1, cx, cy):
    total = cz0 * below + cz1 * above
    total = total + cx * ahead(p, 0) + behind(cx * p, 0)
    return total + cy * ahead(p, 1) + behind(cy * p, 1)


def pair_matrix(wide):
    shape = (wide, wide // 2)
    return (lax.shift_right_logical(iota(shape, 0), 1) == iota(shape, 1)).astype(jnp.bfloat16)


def copy_matrix(narrow):
    shape = (narrow, narrow * 2)
    return (iota(shape, 0) == lax.shift_right_logical(iota(shape, 1), 1)).astype(jnp.bfloat16)


def dot(a, ones):
    total = None
    for _ in range(3):
        part = a.astype(jnp.bfloat16)
        a = a - part.astype(F32)
        term = jnp.dot(part, ones, preferred_element_type=F32)
        total = term if total is None else total + term
    return total


def pair_rows(s, x, start, count):
    tiles = x.shape[1] // 128
    for t in range(tiles):
        s[t, 0 : x.shape[0]] = x[:, 128 * t : 128 * t + 128]
    parts = [s[t, pl.ds(start, count, stride=2), :] + s[t, pl.ds(start + 1, count, stride=2), :] for t in range(tiles)]
    return jnp.concatenate(parts, axis=1)


def copy_rows(s, x):
    tiles, count = x.shape[1] // 128, x.shape[0]
    for t in range(tiles):
        s[t, pl.ds(0, count, stride=2), :] = x[:, 128 * t : 128 * t + 128]
        s[t, pl.ds(1, count, stride=2), :] = x[:, 128 * t : 128 * t + 128]
    return jnp.concatenate([s[t, 0 : 2 * count] for t in range(tiles)], axis=1)


def inside(first, index, count):
    at = first + index
    return jnp.logical_and(at >= 0, at < count)


def k_conduct(div, density, zones, out, dens, zone_ids, sems):
    loads = []
    for z in range(4):
        loads.append(pltpu.make_async_copy(density.at[z], dens.at[z], sems.at[0, z]))
        loads.append(pltpu.make_async_copy(zones.at[z], zone_ids.at[z], sems.at[1, z]))
    loads += [pltpu.make_async_copy(div.at[z], out.at[1, z], sems.at[2, z]) for z in range(4)]
    for load in loads:
        load.start()
    for z in range(4):
        loads[2 * z].wait()
        loads[2 * z + 1].wait()
        zone = zone_ids[z]
        perm = jnp.where(zone == 0, PERMEABILITY[0], 0.0)
        for zone_id in range(1, 5):
            perm = jnp.where(zone == zone_id, PERMEABILITY[zone_id], perm)
        out[0, z] = perm / dens[z]
    for load in loads[8:]:
        load.wait()


def conductance(divergence, density, zones):
    shape = divergence.shape
    return pl.pallas_call(
        k_conduct,
        out_shape=pltpu.VMEM((2,) + shape, F32),
        in_specs=[pl.BlockSpec(memory_space=pl.ANY)] * 3,
        out_specs=vmem(1)[0],
        scratch_shapes=[pltpu.VMEM(shape, F32), pltpu.VMEM(shape, jnp.int32), pltpu.SemaphoreType.DMA((3, 4))],
    )(divergence, density, zones)


def stack0(core, near, put):
    h, _, high, _ = position()
    odd = lax.rem(h, 2)

    @pl.when(odd == 0)
    def _():
        for z in range(4):
            put(z, near[0, z], near[0, 4 + z], h == 0)
            put(z + 4, core[0, 0, z], core[0, 1, z], None)
            put(z + 8, core[1, 0, z], core[1, 1, z], None)

    @pl.when(odd == 1)
    def _():
        for z in range(4):
            put(z, core[0, 0, z], core[0, 1, z], None)
            put(z + 4, core[1, 0, z], core[1, 1, z], None)
            put(z + 8, near[1, z], near[1, 4 + z], h == high - 1)


def k_edges0(core, edge):
    odd = lax.rem(lax.axis_index("height"), 2)
    for side in range(2):

        @pl.when(odd == side)
        def _():
            for z in range(8):
                edge[z, 0:4] = core[z // 4, 0, z % 4, 12 * side : 12 * side + 4]
                edge[z, 4:7] = core[z // 4, 1, z % 4, 13 * side : 13 * side + 3]
                edge[z, 7:8] = jnp.zeros((1, 512), F32)


def k_level0(core, near, sides, pre, w_out, g_out, cx_out, cy_out, cz_out, pack, c, g, w, cx, cy, cz, dg, p, rs, c1, st):
    h, plan, n_h, n_p = position()

    def put(z, cond, div, outside):
        c[z, 4:20] = cond if outside is None else jnp.where(outside, 1.0, cond)
        g[z, 4:20] = div

    stack0(core, near, put)
    for z in range(12):
        for first in (0, 20):
            c[z, first : first + 4] = jnp.ones((4, 512), F32)
            g[z, first : first + 4] = jnp.zeros((4, 512), F32)
    odd = lax.rem(h, 2)
    for par in range(2):

        @pl.when(odd == par)
        def _():
            for z in range(1, 11):
                inner = z < 8 if par else z >= 4
                at = z if par else z - 4
                for side, first, end in ((0, 0, plan == 0), (1, 20, plan == n_p - 1)):
                    rows = sides.at[side, at] if inner else near.at[par, z if par else z + 7, pl.ds(8 * side, 8)]
                    out = end if inner else jnp.logical_or(end, h == (n_h - 1 if par else 0))
                    c[z, first : first + 4] = jnp.where(out, 1.0, rows[0:4])
                    g[z, first + 1 - side : first + 4 - side] = rows[4:7]

    row = iota((24, 512), 0) + (plan * 16 - 4)
    row_in = jnp.logical_and(row >= 0, row < n_p * 16).astype(F32) * OMEGA
    for z in range(11):
        cz[z] = harmonic(c[z], c[z + 1])
    for z in range(1, 11):
        here = c[z]
        fx = harmonic(here, ahead(here, 0))
        link, both = y_faces(here)
        diag = cz[z - 1] + cz[z] + fx + behind(fx, 0) + both
        weight = jnp.where(inside(h * 4 - 4, z, n_h * 4), row_in, 0.0) / diag
        cx[z] = fx
        cy[z] = link
        w[z] = weight
        if 4 <= z <= 7:
            dg[z - 4] = diag
            rs[z - 4] = g[z]
        g[z] = weight * g[z]
    for z in range(2, 10):
        here = g[z]
        total = spread(here, g[z - 1], g[z + 1], cz[z - 1], cz[z], cx[z], cy[z])
        p[z] = here * (1.0 / 3.0) + here + w[z] * total
    for z in range(4, 8):
        here = p[z]
        total = spread(here, p[z - 1], p[z + 1], cz[z - 1], cz[z], cx[z], cy[z])
        rs[z - 4] = rs[z - 4] - dg[z - 4] * here + total
    for z in range(2, 10):
        pre[z - 2] = p[z]
    for z in range(3, 9):
        w_out[z - 3] = w[z]
        g_out[z - 3] = g[z]
        cx_out[z - 3] = cx[z]
        cy_out[z - 3] = cy[z]
    for z in range(2, 9):
        cz_out[z - 2] = cz[z]
    rows = [pair_rows(st.at[z], rs[2 * z] + rs[2 * z + 1], 4, 8) for z in range(2)]
    for z in range(4):
        sums = c[2 * z + 2] + c[2 * z + 3]
        c1[z, 0:8] = pair_rows(st.at[2 + 2 * z], sums, 0, 8)
        c1[z, 8:12] = pair_rows(st.at[3 + 2 * z], sums[16:24], 0, 4)
        c1[z, 12:16] = jnp.full((4, 512), 4.0, F32)
    pairs = pair_matrix(512)
    f1 = 0.5 * dot(jnp.concatenate(rows, axis=0), pairs)
    k1 = 0.125 * dot(jnp.concatenate([c1[z] for z in range(4)], axis=0), pairs)
    k1 = [k1[16 * z : 16 * z + 16] for z in range(4)]
    for z in range(2):
        here = k1[z + 1]
        fx = harmonic(here, ahead(here, 0))
        link, both = y_faces(here)
        diag = harmonic(here, k1[z]) + harmonic(here, k1[z + 2]) + fx + behind(fx, 0) + both
        c1[z, :, 0:256] = here
        c1[z, :, 256:512] = diag
        pack[z, 0:8] = OMEGA * f1[8 * z : 8 * z + 8] / c1[z, 2:10, 256:512]
        pack[z, 8:16] = c1[z, 2:10, 0:256]


def k_edges1(chip, edge):
    odd = lax.rem(lax.axis_index("height"), 2)
    for side in range(2):

        @pl.when(odd == side)
        def _():
            for z in range(4):
                edge[z, 0:4] = chip[z, 4 * side : 4 * side + 4]
                edge[z, 4:8] = chip[z, 4 * side + 8 : 4 * side + 12]


def window1(even_layers, odd_layers, first, g, c):
    h, plan, n_h, n_p = position()
    for side, layers in ((0, even_layers), (1, odd_layers)):

        @pl.when(lax.rem(h, 2) == side)
        def _():
            for z, rows in enumerate(layers):
                keep = inside(first, z, n_h * 2)
                low, high = jnp.logical_and(keep, plan > 0), jnp.logical_and(keep, plan < n_p - 1)
                g[z, 4:12] = jnp.where(keep, rows[0:8], 0.0)
                c[z, 4:12] = jnp.where(keep, rows[8:16], 1.0)
                g[z, 0:4] = jnp.where(low, rows[16:20], 0.0)
                c[z, 0:4] = jnp.where(low, rows[20:24], 1.0)
                g[z, 12:16] = jnp.where(high, rows[24:28], 0.0)
                c[z, 12:16] = jnp.where(high, rows[28:32], 1.0)


def couple1(count, first, c, w, cx, cy, cz):
    h, plan, n_h, n_p = position()
    row = iota((16, 256), 0) + (plan * 8 - 4)
    row_in = jnp.logical_and(row >= 0, row < n_p * 8).astype(F32) * OMEGA
    for z in range(count - 1):
        cz[z] = harmonic(c[z], c[z + 1])
    diags = {}
    for z in range(1, count - 1):
        here = c[z]
        fx = harmonic(here, ahead(here, 0))
        link, both = y_faces(here)
        diags[z] = cz[z - 1] + cz[z] + fx + behind(fx, 0) + both
        cx[z] = fx
        cy[z] = link
        w[z] = jnp.where(inside(first, z, n_h * 2), row_in, 0.0) / diags[z]
    return diags


def k_level1_wide(full, two, pre, w_out, g_out, cx_out, cy_out, cz_out, c, g, w, cx, cy, cz):
    first = lax.axis_index("height") * 2 - 4
    layers = [two.at[0, z] for z in range(4)] + [full.at[z] for z in range(4)] + [two.at[1, z] for z in range(4)]
    window1(layers[0:10], layers[2:12], first, g, c)
    couple1(10, first, c, w, cx, cy, cz)
    for z in range(1, 9):
        here = g[z]
        total = spread(here, g[z - 1], g[z + 1], cz[z - 1], cz[z], cx[z], cy[z])
        pre[z - 1] = here * (1.0 / 3.0) + here + w[z] * total
    for z in range(2, 8):
        w_out[z - 2] = w[z]
        g_out[z - 2] = g[z]
        cx_out[z - 2] = cx[z]
        cy_out[z - 2] = cy[z]
    for z in range(1, 8):
        cz_out[z - 1] = cz[z]


def k_level1(full, near, copies, c, g, w, cx, cy, cz, p, rs, dg, st):
    first = lax.axis_index("height") * 2 - 2
    middle = [full.at[z] for z in range(4)]
    window1([near.at[0, 2], near.at[0, 3]] + middle, middle + [near.at[1, 0], near.at[1, 1]], first, g, c)
    diags = couple1(6, first, c, w, cx, cy, cz)
    for z in range(2):
        rs[z] = diags[z + 2]
    for z in range(1, 5):
        here = g[z]
        total = spread(here, g[z - 1], g[z + 1], cz[z - 1], cz[z], cx[z], cy[z])
        p[z] = here * (1.0 / 3.0) + here + w[z] * total
    for z in range(2, 4):
        here = p[z]
        total = spread(here, p[z - 1], p[z + 1], cz[z - 1], cz[z], cx[z], cy[z])
        rs[z - 2] = (g[z] - OMEGA * here + w[z] * total) * rs[z - 2] * 1.5
    rows = [pair_rows(st.at[0], rs[0] + rs[1], 0, 8)]
    rows += [pair_rows(st.at[z + 1], c[2 * z] + c[2 * z + 1], 0, 8) for z in range(3)]
    pairs = pair_matrix(256)
    both = jnp.concatenate(rows, axis=0)
    down = dot(both, pairs)
    f2 = 0.5 * down[0:8]
    k2 = [0.125 * down[8 * z + 8 : 8 * z + 16] for z in range(3)]
    here = k2[1]
    fx = harmonic(here, ahead(here, 0))
    link, share = y_faces(here)
    diag = harmonic(here, k2[0]) + harmonic(here, k2[2]) + fx + behind(fx, 0) + share
    dg[0, 0:8, 0:128] = diag
    dg[0, 8:16, 0:128] = here
    tile_g = OMEGA * f2[2:6] / dg[0, 2:6, 0:128]
    tile_c = dg[0, 10:14, 0:128]
    for i in range(copies.shape[0]):
        copies[i, 0:4] = tile_g
        copies[i, 4:8] = tile_c


def k_up(block, outer, pre1, w1, g1, cx1, cy1, cz1, pre0, w0, g0, cx0, cy0, cz0, out, sems, s, c, g, w, cx, cy, cz, dg, pa, pb, p2, u1, q1, u0, q0, s1, s0, done):
    h, plan, n_h, _ = position()
    wide = s.shape[1] // 2
    tiles = wide // 4
    for z in range(14):
        for t in range(tiles):
            at = tiles * (z % 2) + t
            rows = block.at[at] if 6 <= z < 8 else outer.at[z // 8, z % 8 // 2, at]
            s[z, 4 * t : 4 * t + 4] = rows[0:4]
            s[z, wide + 4 * t : wide + 4 * t + 4] = rows[4:8]
    q = lax.rem(h, 2)
    for z in range(13):
        keep = inside(h - 6, z, n_h)
        g[z] = jnp.where(keep, s[q + z, 0:wide], 0.0)
        c[z] = jnp.where(keep, s[q + z, wide : 2 * wide], 1.0)
    row = iota((wide, 128), 0)
    for z in range(12):
        cz[z] = harmonic(c[z], c[z + 1])
    for z in range(1, 12):
        here = c[z]
        full = harmonic(here, jnp.where(row == wide - 1, 1.0, ahead(here, 0)))
        fx = jnp.where(row == wide - 1, 0.0, full)
        first = jnp.where(row[0:8] == 0, harmonic(here[0:8], 1.0), 0.0)
        first = jnp.concatenate([first, jnp.zeros((wide - 8, 128), F32)], axis=0)
        link, both = y_faces(here)
        diag = cz[z - 1] + cz[z] + full + behind(fx, 0) + first + both
        cx[z] = fx
        cy[z] = link
        w[z] = jnp.where(inside(h - 6, z, n_h), OMEGA, 0.0) / diag
        dg[z] = diag

    def step(source, z):
        here = source[z]
        total = spread(here, source[z - 1], source[z + 1], cz[z - 1], cz[z], cx[z], cy[z])
        return here * (1.0 / 3.0) + g[z] + w[z] * total

    for z in range(1, 12):
        pa[z] = step(g, z)
    for z in range(2, 11):
        pb[z] = step(pa, z)
    for z in range(3, 10):
        pa[z] = step(pb, z)
    for z in range(4, 9):
        here = pa[z]
        extra = (step(pa, z) - here) * dg[z] * 1.5
        line = jnp.sum(extra, axis=0, keepdims=True) / jnp.sum(dg[z], axis=0, keepdims=True)
        p2[z - 4, 0:8] = jnp.zeros((8, 128), F32)
        p2[z - 4, wide + 8 : wide + 16] = jnp.zeros((8, 128), F32)
        p2[z - 4, 8 : wide + 8] = here + line
    rows = jnp.concatenate([p2[z, pl.ds(plan * 4 + 6, 8), :] for z in range(5)], axis=0)
    rows = dot(rows, copy_matrix(128))
    for z in range(5):
        u1[z] = copy_rows(s1.at[z], rows[8 * z : 8 * z + 8])
    for z in range(1, 9):
        q1[z - 1] = pre1[z - 1] + u1[z // 2]
    mid = []
    for z in range(2, 8):
        here = q1[z - 1]
        total = spread(here, q1[z - 2], q1[z], cz1[z - 2], cz1[z - 1], cx1[z - 2], cy1[z - 2])
        pb_rows = here * (1.0 / 3.0) + g1[z - 2] + w1[z - 2] * total
        mid.append(pb_rows)
    for z in range(6):
        q1[z] = mid[z]
    low = []
    for z in range(3, 7):
        here = q1[z - 2]
        total = spread(here, q1[z - 3], q1[z - 1], cz1[z - 2], cz1[z - 1], cx1[z - 2], cy1[z - 2])
        low.append(here * (1.0 / 3.0) + g1[z - 2] + w1[z - 2] * total)
    for z in range(4):
        q1[z] = low[z]
    rows = jnp.concatenate([q1[z] for z in range(4)], axis=0)
    rows = dot(rows, copy_matrix(256))
    for z in range(4):
        u0[z] = copy_rows(s0.at[z], rows[16 * z : 16 * z + 16])
    for z in range(2, 10):
        q0[z - 2] = pre0[z - 2] + u0[z // 2 - 1, 4:28]
    for z in range(3, 9):
        here = q0[z - 2]
        total = spread(here, q0[z - 3], q0[z - 1], cz0[z - 3], cz0[z - 2], cx0[z - 3], cy0[z - 3])
        u0[z - 3, 0:24] = here * (1.0 / 3.0) + g0[z - 3] + w0[z - 3] * total
    stores = []
    for z in range(4, 8):
        here = u0[z - 3, 0:24]
        total = spread(here, u0[z - 4, 0:24], u0[z - 2, 0:24], cz0[z - 3], cz0[z - 2], cx0[z - 3], cy0[z - 3])
        q0[z - 4] = here * (1.0 / 3.0) + g0[z - 3] + w0[z - 3] * total
        done[z - 4] = q0[z - 4, 4:20]
        stores.append(pltpu.make_async_copy(done.at[z - 4], out.at[z - 4], sems.at[z - 4]))
        stores[-1].start()
    for store in stores:
        store.wait()


def on_device(divergence, density, zones):
    n_h, n_p = lax.axis_size("height"), lax.axis_size("plan")
    odd = lax.rem(lax.axis_index("height"), 2)
    cores = [[i, i + 1] for i in range(0, n_h, 2)]

    def reach(step, others):
        pairs = [(i, i + step) for i in range(1, n_h - step, 2)] + others
        ends = sorted(set(range(n_h)) - {i for both in pairs for i in both})
        groups = [[i * n_p + t, j * n_p + t] for i, j in pairs for t in range(n_p)]
        return groups + [[i * n_p + t, i * n_p + t + 1] for i in ends for t in range(0, n_p, 2)]

    def meet(x, groups):
        return lax.all_gather(x, ("height", "plan"), axis=0, tiled=False, axis_index_groups=groups)

    def pair(x):
        return lax.all_gather(x, "height", axis=0, tiled=False, axis_index_groups=cores)

    links, leaps = reach(1, []), reach(5, [(0, 4), (n_h - 5, n_h - 1)])
    own = conductance(divergence, density, zones)
    core = pair(own)
    across = [[(2 * i + 1) * n_p + t, 2 * i * n_p + (t + 1) % n_p] for i in range(n_h // 2) for t in range(n_p)]

    def both_sides(edge):
        return pair(lax.dynamic_index_in_dim(meet(edge, across), odd, 0, keepdims=False))

    sides = both_sides(call(k_edges0, (8, 8, 512), [], core))
    corner = lax.dynamic_slice_in_dim(sides, 5 * odd, 3, 1)
    corner = jnp.concatenate([corner[0], corner[1]], axis=1)
    near = meet(jnp.concatenate([own.reshape(8, 16, 512), corner], axis=0), links)
    box = (12, 24, 512)
    eight, six, seven = (8, 24, 512), (6, 24, 512), (7, 24, 512)
    *level0, pack = call(
        k_level0,
        [eight, six, six, six, six, seven, (2, 16, 256)],
        [box] * 6 + [(4, 24, 512), box, (4, 24, 512), (4, 16, 512), (10, 4, 24, 128)],
        core, near, sides,
    )
    chip = pair(pack).reshape(4, 16, 256)
    sides = both_sides(call(k_edges1, (4, 8, 256), [], chip))
    full = jnp.concatenate([chip, sides[0], sides[1]], axis=1)
    near = meet(full, links)
    box = (6, 16, 256)
    tiles = call(k_level1, (2 * n_p, 8, 128), [box] * 7 + [(2, 16, 256), (2, 16, 256), (4, 2, 16, 128)], full, near)
    two = pair(lax.dynamic_index_in_dim(near, odd, 0, keepdims=False))
    box = (10, 16, 256)
    eight, six, seven = (8, 16, 256), (6, 16, 256), (7, 16, 256)
    level1 = call(k_level1_wide, [eight, six, six, six, six, seven], [box] * 6, full, two)
    groups = [[(2 * i + k) * n_p + t for k in range(2) for t in range(n_p)] for i in range(n_h // 2)]
    block = lax.all_to_all(tiles, ("height", "plan"), split_axis=0, concat_axis=0, tiled=True, axis_index_groups=groups)
    near = meet(block, links)
    far = meet(near, leaps)
    side = jnp.where(odd == 0, jnp.concatenate([far[0], near[0:1]]), jnp.concatenate([near[1:2], far[1]]))
    outer = pair(side)
    wide = n_p * 4
    flat = (13, wide, 128)
    arrays = (block, outer, *level1, *level0)
    scratch = [(14, 2 * wide, 128)] + [flat] * 9
    scratch += [(5, wide + 16, 128), (5, 16, 256), (8, 16, 256), (6, 32, 512), (8, 24, 512), (5, 2, 16, 128), (4, 4, 32, 128), (4, 16, 512)]
    return pl.pallas_call(
        k_up,
        out_shape=jax.ShapeDtypeStruct((4, 16, 512), F32),
        in_specs=vmem(len(arrays)),
        out_specs=pl.BlockSpec(memory_space=pl.ANY),
        scratch_shapes=[pltpu.SemaphoreType.DMA((4,))] + [pltpu.VMEM(s, F32) for s in scratch],
        compiler_params=pltpu.CompilerParams(vmem_limit_bytes=40 << 20),
    )(*arrays)


def solution(mesh):
    return jax.shard_map(
        on_device,
        mesh=mesh,
        in_specs=(P("height", "plan", None), P("height", "plan", None), P("height", "plan", None)),
        out_specs=P("height", "plan", None),
        check_vma=False,
    )
```

```python
import jax
import jax.numpy as jnp
from jax import lax
from jax.experimental import pallas as pl
from jax.experimental.pallas import tpu as pltpu
from jax.sharding import PartitionSpec as P

PERMEABILITY = (1.0, 0.1, 0.6, 0.8, 0.25)
OMEGA = 2.0 / 3.0
F32 = jnp.float32


def vmem(count):
    return [pl.BlockSpec(memory_space=pltpu.VMEM)] * count


def position():
    return lax.axis_index("height"), lax.axis_index("plan"), lax.axis_size("height"), lax.axis_size("plan")


def call(body, outs, scratch, *arrays):
    many = isinstance(outs, list)
    shapes = [pltpu.VMEM(s, F32) for s in (outs if many else [outs])]
    return pl.pallas_call(
        body,
        out_shape=shapes if many else shapes[0],
        in_specs=vmem(len(arrays)),
        out_specs=vmem(len(shapes)) if many else vmem(1)[0],
        scratch_shapes=[pltpu.VMEM(s, F32) for s in scratch],
        compiler_params=pltpu.CompilerParams(vmem_limit_bytes=40 << 20),
    )(*arrays)


def harmonic(a, b):
    return 2.0 * a * b / (a + b)


def iota(shape, dim):
    return lax.broadcasted_iota(jnp.int32, shape, dim)


def ahead(x, axis):
    return pltpu.roll(x, x.shape[axis] - 1, axis)


def behind(x, axis):
    return pltpu.roll(x, 1, axis)


def y_faces(c):
    lane = iota(c.shape, 1)
    last = c.shape[1] - 1
    full = harmonic(c, jnp.where(lane == last, 1.0, ahead(c, 1)))
    link = jnp.where(lane == last, 0.0, full)
    first = jnp.where(iota((c.shape[0], 128), 1) == 0, harmonic(c[:, 0:128], 1.0), 0.0)
    if c.shape[1] > 128:
        first = jnp.concatenate([first, jnp.zeros((c.shape[0], c.shape[1] - 128), F32)], axis=1)
    return link, full + behind(link, 1) + first


def spread(p, below, above, cz0, cz1, cx, cy):
    total = cz0 * below + cz1 * above
    total = total + cx * ahead(p, 0) + behind(cx * p, 0)
    return total + cy * ahead(p, 1) + behind(cy * p, 1)


def pair_matrix(wide):
    shape = (wide, wide // 2)
    return (lax.shift_right_logical(iota(shape, 0), 1) == iota(shape, 1)).astype(jnp.bfloat16)


def copy_matrix(narrow):
    shape = (narrow, narrow * 2)
    return (iota(shape, 0) == lax.shift_right_logical(iota(shape, 1), 1)).astype(jnp.bfloat16)


def dot(a, ones):
    total = None
    for _ in range(3):
        part = a.astype(jnp.bfloat16)
        a = a - part.astype(F32)
        term = jnp.dot(part, ones, preferred_element_type=F32)
        total = term if total is None else total + term
    return total


def pair_rows(s, x, start, count):
    tiles = x.shape[1] // 128
    for t in range(tiles):
        s[t, 0 : x.shape[0]] = x[:, 128 * t : 128 * t + 128]
    parts = [s[t, pl.ds(start, count, stride=2), :] + s[t, pl.ds(start + 1, count, stride=2), :] for t in range(tiles)]
    return jnp.concatenate(parts, axis=1)


def copy_rows(s, x):
    tiles, count = x.shape[1] // 128, x.shape[0]
    for t in range(tiles):
        s[t, pl.ds(0, count, stride=2), :] = x[:, 128 * t : 128 * t + 128]
        s[t, pl.ds(1, count, stride=2), :] = x[:, 128 * t : 128 * t + 128]
    return jnp.concatenate([s[t, 0 : 2 * count] for t in range(tiles)], axis=1)


def inside(first, index, count):
    at = first + index
    return jnp.logical_and(at >= 0, at < count)


def k_conduct(div, density, zones, out, dens, zone_ids, sems):
    loads = []
    for z in range(4):
        loads.append(pltpu.make_async_copy(density.at[z], dens.at[z], sems.at[0, z]))
        loads.append(pltpu.make_async_copy(zones.at[z], zone_ids.at[z], sems.at[1, z]))
    loads += [pltpu.make_async_copy(div.at[z], out.at[1, z], sems.at[2, z]) for z in range(4)]
    for load in loads:
        load.start()
    for z in range(4):
        loads[2 * z].wait()
        loads[2 * z + 1].wait()
        zone = zone_ids[z]
        perm = jnp.where(zone == 0, PERMEABILITY[0], 0.0)
        for zone_id in range(1, 5):
            perm = jnp.where(zone == zone_id, PERMEABILITY[zone_id], perm)
        out[0, z] = perm / dens[z]
    for load in loads[8:]:
        load.wait()


def conductance(divergence, density, zones):
    shape = divergence.shape
    return pl.pallas_call(
        k_conduct,
        out_shape=pltpu.VMEM((2,) + shape, F32),
        in_specs=[pl.BlockSpec(memory_space=pl.ANY)] * 3,
        out_specs=vmem(1)[0],
        scratch_shapes=[pltpu.VMEM(shape, F32), pltpu.VMEM(shape, jnp.int32), pltpu.SemaphoreType.DMA((3, 4))],
    )(divergence, density, zones)


BESIDE = ((1, 112, 3, 2), (2, 122, 2, 1), (3, 128, 1, 0))
MESSAGE = 136


def k_message0(core, sides, out):
    odd = lax.rem(lax.axis_index("height"), 2)
    out[128:136] = jnp.zeros((8, 512), F32)
    for par in range(2):

        @pl.when(odd == par)
        def _():
            for d in range(1, 5):
                out[16 * d - 16 : 16 * d] = core[par, 0, 4 - d if par else d - 1]
                if d < 4:
                    out[48 + 16 * d : 64 + 16 * d] = core[par, 1, 4 - d if par else d - 1]
            for d, at, n_cond, n_div in BESIDE:
                layer = 8 - d if par else d - 1
                for side in range(2):
                    cond, div = (0, 4) if side else (4 - n_cond, 7 - n_div)
                    out[at : at + n_cond] = sides[side, layer, cond : cond + n_cond]
                    if n_div:
                        out[at + n_cond : at + n_cond + n_div] = sides[side, layer, div : div + n_div]
                    at += n_cond + n_div


def stack0(core, near, put):
    h, _, high, _ = position()
    odd = lax.rem(h, 2)

    def far(par, d):
        return near[par, 16 * d - 16 : 16 * d], near[par, 48 + 16 * d : 64 + 16 * d] if d < 4 else None

    @pl.when(odd == 0)
    def _():
        for z in range(4):
            put(z, *far(0, 4 - z), h == 0)
            put(z + 4, core[0, 0, z], core[0, 1, z], None)
            put(z + 8, core[1, 0, z], core[1, 1, z], None)

    @pl.when(odd == 1)
    def _():
        for z in range(4):
            put(z, core[0, 0, z], core[0, 1, z], None)
            put(z + 4, core[1, 0, z], core[1, 1, z], None)
            put(z + 8, *far(1, z + 1), h == high - 1)


def k_edges0(core, edge):
    odd = lax.rem(lax.axis_index("height"), 2)
    for side in range(2):

        @pl.when(odd == side)
        def _():
            for z in range(8):
                edge[z, 0:4] = core[z // 4, 0, z % 4, 12 * side : 12 * side + 4]
                edge[z, 4:7] = core[z // 4, 1, z % 4, 13 * side : 13 * side + 3]
                edge[z, 7:8] = jnp.zeros((1, 512), F32)


def k_level0(core, near, sides, pre, w_out, g_out, cx_out, cy_out, cz_out, pack, c, g, w, cx, cy, cz, dg, p, rs, c1, st):
    h, plan, n_h, n_p = position()

    def put(z, cond, div, outside):
        c[z, 4:20] = cond if outside is None else jnp.where(outside, 1.0, cond)
        if div is not None:
            g[z, 4:20] = div

    stack0(core, near, put)
    for z in range(12):
        for first in (0, 20):
            c[z, first : first + 4] = jnp.ones((4, 512), F32)
            g[z, first : first + 4] = jnp.zeros((4, 512), F32)
    odd = lax.rem(h, 2)
    for par in range(2):

        @pl.when(odd == par)
        def _():
            for z in range(1, 8) if par else range(4, 11):
                for side, first, end in ((0, 0, plan == 0), (1, 20, plan == n_p - 1)):
                    rows = sides.at[side, z if par else z - 4]
                    c[z, first : first + 4] = jnp.where(end, 1.0, rows[0:4])
                    g[z, first + 1 - side : first + 4 - side] = rows[4:7]
            for d, at, n_cond, n_div in BESIDE:
                z = 7 + d if par else 4 - d
                for side, end in ((0, plan == 0), (1, plan == n_p - 1)):
                    out = jnp.logical_or(end, h == (n_h - 1 if par else 0))
                    first = 20 if side else 4 - n_cond
                    c[z, first : first + n_cond] = jnp.where(out, 1.0, near[par, at : at + n_cond])
                    first = 20 if side else 4 - n_div
                    if n_div:
                        g[z, first : first + n_div] = near[par, at + n_cond : at + n_cond + n_div]
                    at += n_cond + n_div

    row = iota((24, 512), 0) + (plan * 16 - 4)
    row_in = jnp.logical_and(row >= 0, row < n_p * 16).astype(F32) * OMEGA
    for z in range(11):
        cz[z] = harmonic(c[z], c[z + 1])
    for z in range(1, 11):
        here = c[z]
        fx = harmonic(here, ahead(here, 0))
        link, both = y_faces(here)
        diag = cz[z - 1] + cz[z] + fx + behind(fx, 0) + both
        weight = jnp.where(inside(h * 4 - 4, z, n_h * 4), row_in, 0.0) / diag
        cx[z] = fx
        cy[z] = link
        w[z] = weight
        if 4 <= z <= 7:
            dg[z - 4] = diag
            rs[z - 4] = g[z]
        g[z] = weight * g[z]
    for z in range(2, 10):
        here = g[z]
        total = spread(here, g[z - 1], g[z + 1], cz[z - 1], cz[z], cx[z], cy[z])
        p[z] = here * (1.0 / 3.0) + here + w[z] * total
    for z in range(4, 8):
        here = p[z]
        total = spread(here, p[z - 1], p[z + 1], cz[z - 1], cz[z], cx[z], cy[z])
        rs[z - 4] = rs[z - 4] - dg[z - 4] * here + total
    for z in range(2, 10):
        pre[z - 2] = p[z]
    for z in range(3, 9):
        w_out[z - 3] = w[z]
        g_out[z - 3] = g[z]
        cx_out[z - 3] = cx[z]
        cy_out[z - 3] = cy[z]
    for z in range(2, 9):
        cz_out[z - 2] = cz[z]
    rows = [pair_rows(st.at[z], rs[2 * z] + rs[2 * z + 1], 4, 8) for z in range(2)]
    for z in range(4):
        sums = c[2 * z + 2] + c[2 * z + 3]
        c1[z, 0:8] = pair_rows(st.at[2 + 2 * z], sums, 0, 8)
        c1[z, 8:12] = pair_rows(st.at[3 + 2 * z], sums[16:24], 0, 4)
        c1[z, 12:16] = jnp.full((4, 512), 4.0, F32)
    pairs = pair_matrix(512)
    f1 = 0.5 * dot(jnp.concatenate(rows, axis=0), pairs)
    k1 = 0.125 * dot(jnp.concatenate([c1[z] for z in range(4)], axis=0), pairs)
    k1 = [k1[16 * z : 16 * z + 16] for z in range(4)]
    for z in range(2):
        here = k1[z + 1]
        fx = harmonic(here, ahead(here, 0))
        link, both = y_faces(here)
        diag = harmonic(here, k1[z]) + harmonic(here, k1[z + 2]) + fx + behind(fx, 0) + both
        c1[z, :, 0:256] = here
        c1[z, :, 256:512] = diag
        pack[z, 0:8] = OMEGA * f1[8 * z : 8 * z + 8] / c1[z, 2:10, 256:512]
        pack[z, 8:16] = c1[z, 2:10, 0:256]


def k_edges1(chip, edge):
    odd = lax.rem(lax.axis_index("height"), 2)
    for side in range(2):

        @pl.when(odd == side)
        def _():
            for z in range(4):
                edge[z, 0:4] = chip[z, 4 * side : 4 * side + 4]
                edge[z, 4:8] = chip[z, 4 * side + 8 : 4 * side + 12]


def window1(even_layers, odd_layers, first, g, c):
    h, plan, n_h, n_p = position()
    for side, layers in ((0, even_layers), (1, odd_layers)):

        @pl.when(lax.rem(h, 2) == side)
        def _():
            for z, rows in enumerate(layers):
                keep = inside(first, z, n_h * 2)
                low, high = jnp.logical_and(keep, plan > 0), jnp.logical_and(keep, plan < n_p - 1)
                g[z, 4:12] = jnp.where(keep, rows[0:8], 0.0)
                c[z, 4:12] = jnp.where(keep, rows[8:16], 1.0)
                g[z, 0:4] = jnp.where(low, rows[16:20], 0.0)
                c[z, 0:4] = jnp.where(low, rows[20:24], 1.0)
                g[z, 12:16] = jnp.where(high, rows[24:28], 0.0)
                c[z, 12:16] = jnp.where(high, rows[28:32], 1.0)


def couple1(count, first, c, w, cx, cy, cz):
    h, plan, n_h, n_p = position()
    row = iota((16, 256), 0) + (plan * 8 - 4)
    row_in = jnp.logical_and(row >= 0, row < n_p * 8).astype(F32) * OMEGA
    for z in range(count - 1):
        cz[z] = harmonic(c[z], c[z + 1])
    diags = {}
    for z in range(1, count - 1):
        here = c[z]
        fx = harmonic(here, ahead(here, 0))
        link, both = y_faces(here)
        diags[z] = cz[z - 1] + cz[z] + fx + behind(fx, 0) + both
        cx[z] = fx
        cy[z] = link
        w[z] = jnp.where(inside(first, z, n_h * 2), row_in, 0.0) / diags[z]
    return diags


def k_level1_wide(full, two, pre, w_out, g_out, cx_out, cy_out, cz_out, c, g, w, cx, cy, cz):
    first = lax.axis_index("height") * 2 - 4
    layers = [two.at[0, z] for z in range(4)] + [full.at[z] for z in range(4)] + [two.at[1, z] for z in range(4)]
    window1(layers[0:10], layers[2:12], first, g, c)
    couple1(10, first, c, w, cx, cy, cz)
    for z in range(1, 9):
        here = g[z]
        total = spread(here, g[z - 1], g[z + 1], cz[z - 1], cz[z], cx[z], cy[z])
        pre[z - 1] = here * (1.0 / 3.0) + here + w[z] * total
    for z in range(2, 8):
        w_out[z - 2] = w[z]
        g_out[z - 2] = g[z]
        cx_out[z - 2] = cx[z]
        cy_out[z - 2] = cy[z]
    for z in range(1, 8):
        cz_out[z - 1] = cz[z]


def k_level1(full, near, copies, c, g, w, cx, cy, cz, p, rs, dg, st):
    first = lax.axis_index("height") * 2 - 2
    middle = [full.at[z] for z in range(4)]
    window1([near.at[0, 2], near.at[0, 3]] + middle, middle + [near.at[1, 0], near.at[1, 1]], first, g, c)
    diags = couple1(6, first, c, w, cx, cy, cz)
    for z in range(2):
        rs[z] = diags[z + 2]
    for z in range(1, 5):
        here = g[z]
        total = spread(here, g[z - 1], g[z + 1], cz[z - 1], cz[z], cx[z], cy[z])
        p[z] = here * (1.0 / 3.0) + here + w[z] * total
    for z in range(2, 4):
        here = p[z]
        total = spread(here, p[z - 1], p[z + 1], cz[z - 1], cz[z], cx[z], cy[z])
        rs[z - 2] = (g[z] - OMEGA * here + w[z] * total) * rs[z - 2] * 1.5
    rows = [pair_rows(st.at[0], rs[0] + rs[1], 0, 8)]
    rows += [pair_rows(st.at[z + 1], c[2 * z] + c[2 * z + 1], 0, 8) for z in range(3)]
    pairs = pair_matrix(256)
    both = jnp.concatenate(rows, axis=0)
    down = dot(both, pairs)
    f2 = 0.5 * down[0:8]
    k2 = [0.125 * down[8 * z + 8 : 8 * z + 16] for z in range(3)]
    here = k2[1]
    fx = harmonic(here, ahead(here, 0))
    link, share = y_faces(here)
    diag = harmonic(here, k2[0]) + harmonic(here, k2[2]) + fx + behind(fx, 0) + share
    dg[0, 0:8, 0:128] = diag
    dg[0, 8:16, 0:128] = here
    tile_g = OMEGA * f2[2:6] / dg[0, 2:6, 0:128]
    tile_c = dg[0, 10:14, 0:128]
    for i in range(copies.shape[0]):
        copies[i, 0:4] = tile_g
        copies[i, 4:8] = tile_c


def k_up(block, outer, pre1, w1, g1, cx1, cy1, cz1, pre0, w0, g0, cx0, cy0, cz0, out, sems, s, c, g, w, cx, cy, cz, dg, pa, pb, p2, u1, q1, u0, q0, s1, s0, done):
    h, plan, n_h, _ = position()
    wide = s.shape[1] // 2
    tiles = wide // 4
    for z in range(14):
        for t in range(tiles):
            at = tiles * (z % 2) + t
            rows = block.at[at] if 6 <= z < 8 else outer.at[z // 8, z % 8 // 2, at]
            s[z, 4 * t : 4 * t + 4] = rows[0:4]
            s[z, wide + 4 * t : wide + 4 * t + 4] = rows[4:8]
    q = lax.rem(h, 2)
    for z in range(13):
        keep = inside(h - 6, z, n_h)
        g[z] = jnp.where(keep, s[q + z, 0:wide], 0.0)
        c[z] = jnp.where(keep, s[q + z, wide : 2 * wide], 1.0)
    row = iota((wide, 128), 0)
    for z in range(12):
        cz[z] = harmonic(c[z], c[z + 1])
    for z in range(1, 12):
        here = c[z]
        full = harmonic(here, jnp.where(row == wide - 1, 1.0, ahead(here, 0)))
        fx = jnp.where(row == wide - 1, 0.0, full)
        first = jnp.where(row[0:8] == 0, harmonic(here[0:8], 1.0), 0.0)
        first = jnp.concatenate([first, jnp.zeros((wide - 8, 128), F32)], axis=0)
        link, both = y_faces(here)
        diag = cz[z - 1] + cz[z] + full + behind(fx, 0) + first + both
        cx[z] = fx
        cy[z] = link
        w[z] = jnp.where(inside(h - 6, z, n_h), OMEGA, 0.0) / diag
        dg[z] = diag

    def step(source, z):
        here = source[z]
        total = spread(here, source[z - 1], source[z + 1], cz[z - 1], cz[z], cx[z], cy[z])
        return here * (1.0 / 3.0) + g[z] + w[z] * total

    for z in range(1, 12):
        pa[z] = step(g, z)
    for z in range(2, 11):
        pb[z] = step(pa, z)
    for z in range(3, 10):
        pa[z] = step(pb, z)
    for z in range(4, 9):
        here = pa[z]
        extra = (step(pa, z) - here) * dg[z] * 1.5
        line = jnp.sum(extra, axis=0, keepdims=True) / jnp.sum(dg[z], axis=0, keepdims=True)
        p2[z - 4, 0:8] = jnp.zeros((8, 128), F32)
        p2[z - 4, wide + 8 : wide + 16] = jnp.zeros((8, 128), F32)
        p2[z - 4, 8 : wide + 8] = here + line
    rows = jnp.concatenate([p2[z, pl.ds(plan * 4 + 6, 8), :] for z in range(5)], axis=0)
    rows = dot(rows, copy_matrix(128))
    for z in range(5):
        u1[z] = copy_rows(s1.at[z], rows[8 * z : 8 * z + 8])
    for z in range(1, 9):
        q1[z - 1] = pre1[z - 1] + u1[z // 2]
    mid = []
    for z in range(2, 8):
        here = q1[z - 1]
        total = spread(here, q1[z - 2], q1[z], cz1[z - 2], cz1[z - 1], cx1[z - 2], cy1[z - 2])
        pb_rows = here * (1.0 / 3.0) + g1[z - 2] + w1[z - 2] * total
        mid.append(pb_rows)
    for z in range(6):
        q1[z] = mid[z]
    low = []
    for z in range(3, 7):
        here = q1[z - 2]
        total = spread(here, q1[z - 3], q1[z - 1], cz1[z - 2], cz1[z - 1], cx1[z - 2], cy1[z - 2])
        low.append(here * (1.0 / 3.0) + g1[z - 2] + w1[z - 2] * total)
    for z in range(4):
        q1[z] = low[z]
    rows = jnp.concatenate([q1[z] for z in range(4)], axis=0)
    rows = dot(rows, copy_matrix(256))
    for z in range(4):
        u0[z] = copy_rows(s0.at[z], rows[16 * z : 16 * z + 16])
    for z in range(2, 10):
        q0[z - 2] = pre0[z - 2] + u0[z // 2 - 1, 4:28]
    for z in range(3, 9):
        here = q0[z - 2]
        total = spread(here, q0[z - 3], q0[z - 1], cz0[z - 3], cz0[z - 2], cx0[z - 3], cy0[z - 3])
        u0[z - 3, 0:24] = here * (1.0 / 3.0) + g0[z - 3] + w0[z - 3] * total
    stores = []
    for z in range(4, 8):
        here = u0[z - 3, 0:24]
        total = spread(here, u0[z - 4, 0:24], u0[z - 2, 0:24], cz0[z - 3], cz0[z - 2], cx0[z - 3], cy0[z - 3])
        q0[z - 4] = here * (1.0 / 3.0) + g0[z - 3] + w0[z - 3] * total
        done[z - 4] = q0[z - 4, 4:20]
        stores.append(pltpu.make_async_copy(done.at[z - 4], out.at[z - 4], sems.at[z - 4]))
        stores[-1].start()
    for store in stores:
        store.wait()


def on_device(divergence, density, zones):
    n_h, n_p = lax.axis_size("height"), lax.axis_size("plan")
    odd = lax.rem(lax.axis_index("height"), 2)
    cores = [[i, i + 1] for i in range(0, n_h, 2)]

    def reach(step, others):
        pairs = [(i, i + step) for i in range(1, n_h - step, 2)] + others
        ends = sorted(set(range(n_h)) - {i for both in pairs for i in both})
        groups = [[i * n_p + t, j * n_p + t] for i, j in pairs for t in range(n_p)]
        return groups + [[i * n_p + t, i * n_p + t + 1] for i in ends for t in range(0, n_p, 2)]

    def meet(x, groups):
        return lax.all_gather(x, ("height", "plan"), axis=0, tiled=False, axis_index_groups=groups)

    def pair(x):
        return lax.all_gather(x, "height", axis=0, tiled=False, axis_index_groups=cores)

    links, leaps = reach(1, []), reach(5, [(0, 4), (n_h - 5, n_h - 1)])
    own = conductance(divergence, density, zones)
    core = pair(own)
    across = [[(2 * i + 1) * n_p + t, 2 * i * n_p + (t + 1) % n_p] for i in range(n_h // 2) for t in range(n_p)]

    def both_sides(edge):
        return pair(lax.dynamic_index_in_dim(meet(edge, across), odd, 0, keepdims=False))

    sides = both_sides(call(k_edges0, (8, 8, 512), [], core))
    near = meet(call(k_message0, (MESSAGE, 512), [], core, sides), links)
    box = (12, 24, 512)
    eight, six, seven = (8, 24, 512), (6, 24, 512), (7, 24, 512)
    *level0, pack = call(
        k_level0,
        [eight, six, six, six, six, seven, (2, 16, 256)],
        [box] * 6 + [(4, 24, 512), box, (4, 24, 512), (4, 16, 512), (10, 4, 24, 128)],
        core, near, sides,
    )
    chip = pair(pack).reshape(4, 16, 256)
    sides = both_sides(call(k_edges1, (4, 8, 256), [], chip))
    full = jnp.concatenate([chip, sides[0], sides[1]], axis=1)
    near = meet(full, links)
    box = (6, 16, 256)
    tiles = call(k_level1, (2 * n_p, 8, 128), [box] * 7 + [(2, 16, 256), (2, 16, 256), (4, 2, 16, 128)], full, near)
    two = pair(lax.dynamic_index_in_dim(near, odd, 0, keepdims=False))
    box = (10, 16, 256)
    eight, six, seven = (8, 16, 256), (6, 16, 256), (7, 16, 256)
    level1 = call(k_level1_wide, [eight, six, six, six, six, seven], [box] * 6, full, two)
    groups = [[(2 * i + k) * n_p + t for k in range(2) for t in range(n_p)] for i in range(n_h // 2)]
    block = lax.all_to_all(tiles, ("height", "plan"), split_axis=0, concat_axis=0, tiled=True, axis_index_groups=groups)
    near = meet(block, links)
    far = meet(near, leaps)
    side = jnp.where(odd == 0, jnp.concatenate([far[0], near[0:1]]), jnp.concatenate([near[1:2], far[1]]))
    outer = pair(side)
    wide = n_p * 4
    flat = (13, wide, 128)
    arrays = (block, outer, *level1, *level0)
    scratch = [(14, 2 * wide, 128)] + [flat] * 9
    scratch += [(5, wide + 16, 128), (5, 16, 256), (8, 16, 256), (6, 32, 512), (8, 24, 512), (5, 2, 16, 128), (4, 4, 32, 128), (4, 16, 512)]
    return pl.pallas_call(
        k_up,
        out_shape=jax.ShapeDtypeStruct((4, 16, 512), F32),
        in_specs=vmem(len(arrays)),
        out_specs=pl.BlockSpec(memory_space=pl.ANY),
        scratch_shapes=[pltpu.SemaphoreType.DMA((4,))] + [pltpu.VMEM(s, F32) for s in scratch],
        compiler_params=pltpu.CompilerParams(vmem_limit_bytes=40 << 20),
    )(*arrays)


def solution(mesh):
    return jax.shard_map(
        on_device,
        mesh=mesh,
        in_specs=(P("height", "plan", None), P("height", "plan", None), P("height", "plan", None)),
        out_specs=P("height", "plan", None),
        check_vma=False,
    )
```

```python
import jax
import jax.numpy as jnp
from jax import lax
from jax.experimental import pallas as pl
from jax.experimental.pallas import tpu as pltpu
from jax.sharding import PartitionSpec as P

PERMEABILITY = (1.0, 0.1, 0.6, 0.8, 0.25)
OMEGA = 2.0 / 3.0
F32 = jnp.float32


def vmem(count):
    return [pl.BlockSpec(memory_space=pltpu.VMEM)] * count


def position():
    return lax.axis_index("height"), lax.axis_index("plan"), lax.axis_size("height"), lax.axis_size("plan")


def call(body, outs, scratch, *arrays):
    many = isinstance(outs, list)
    shapes = [pltpu.VMEM(s, F32) for s in (outs if many else [outs])]
    return pl.pallas_call(
        body,
        out_shape=shapes if many else shapes[0],
        in_specs=vmem(len(arrays)),
        out_specs=vmem(len(shapes)) if many else vmem(1)[0],
        scratch_shapes=[pltpu.VMEM(s, F32) for s in scratch],
        compiler_params=pltpu.CompilerParams(vmem_limit_bytes=40 << 20),
    )(*arrays)


def harmonic(a, b):
    return 2.0 * a * b / (a + b)


def iota(shape, dim):
    return lax.broadcasted_iota(jnp.int32, shape, dim)


def ahead(x, axis):
    return pltpu.roll(x, x.shape[axis] - 1, axis)


def behind(x, axis):
    return pltpu.roll(x, 1, axis)


def y_faces(c):
    lane = iota(c.shape, 1)
    last = c.shape[1] - 1
    full = harmonic(c, jnp.where(lane == last, 1.0, ahead(c, 1)))
    link = jnp.where(lane == last, 0.0, full)
    first = jnp.where(iota((c.shape[0], 128), 1) == 0, harmonic(c[:, 0:128], 1.0), 0.0)
    if c.shape[1] > 128:
        first = jnp.concatenate([first, jnp.zeros((c.shape[0], c.shape[1] - 128), F32)], axis=1)
    return link, full + behind(link, 1) + first


def spread(p, below, above, cz0, cz1, cx, cy):
    total = cz0 * below + cz1 * above
    total = total + cx * ahead(p, 0) + behind(cx * p, 0)
    return total + cy * ahead(p, 1) + behind(cy * p, 1)


def pair_matrix(wide):
    shape = (wide, wide // 2)
    return (lax.shift_right_logical(iota(shape, 0), 1) == iota(shape, 1)).astype(jnp.bfloat16)


def copy_matrix(narrow):
    shape = (narrow, narrow * 2)
    return (iota(shape, 0) == lax.shift_right_logical(iota(shape, 1), 1)).astype(jnp.bfloat16)


def dot(a, ones):
    total = None
    for _ in range(3):
        part = a.astype(jnp.bfloat16)
        a = a - part.astype(F32)
        term = jnp.dot(part, ones, preferred_element_type=F32)
        total = term if total is None else total + term
    return total


def pair_rows(s, x, start, count):
    tiles = x.shape[1] // 128
    for t in range(tiles):
        s[t, 0 : x.shape[0]] = x[:, 128 * t : 128 * t + 128]
    parts = [s[t, pl.ds(start, count, stride=2), :] + s[t, pl.ds(start + 1, count, stride=2), :] for t in range(tiles)]
    return jnp.concatenate(parts, axis=1)


def copy_rows(s, x):
    tiles, count = x.shape[1] // 128, x.shape[0]
    for t in range(tiles):
        s[t, pl.ds(0, count, stride=2), :] = x[:, 128 * t : 128 * t + 128]
        s[t, pl.ds(1, count, stride=2), :] = x[:, 128 * t : 128 * t + 128]
    return jnp.concatenate([s[t, 0 : 2 * count] for t in range(tiles)], axis=1)


def inside(first, index, count):
    at = first + index
    return jnp.logical_and(at >= 0, at < count)


def k_conduct(div, density, zones, out, dens, zone_ids, sems):
    loads = []
    for z in range(4):
        loads.append(pltpu.make_async_copy(density.at[z], dens.at[z], sems.at[0, z]))
        loads.append(pltpu.make_async_copy(zones.at[z], zone_ids.at[z], sems.at[1, z]))
    loads += [pltpu.make_async_copy(div.at[z], out.at[1, z], sems.at[2, z]) for z in range(4)]
    for load in loads:
        load.start()
    for z in range(4):
        loads[2 * z].wait()
        loads[2 * z + 1].wait()
        zone = zone_ids[z]
        perm = jnp.where(zone == 0, PERMEABILITY[0], 0.0)
        for zone_id in range(1, 5):
            perm = jnp.where(zone == zone_id, PERMEABILITY[zone_id], perm)
        out[0, z] = perm / dens[z]
    for load in loads[8:]:
        load.wait()


def conductance(divergence, density, zones):
    shape = divergence.shape
    return pl.pallas_call(
        k_conduct,
        out_shape=pltpu.VMEM((2,) + shape, F32),
        in_specs=[pl.BlockSpec(memory_space=pl.ANY)] * 3,
        out_specs=vmem(1)[0],
        scratch_shapes=[pltpu.VMEM(shape, F32), pltpu.VMEM(shape, jnp.int32), pltpu.SemaphoreType.DMA((3, 4))],
    )(divergence, density, zones)


BESIDE = ((1, 112, 3, 2), (2, 122, 2, 1), (3, 128, 1, 0))
MESSAGE = 136


def k_message0(core, sides, out):
    odd = lax.rem(lax.axis_index("height"), 2)
    out[128:136] = jnp.zeros((8, 512), F32)
    for par in range(2):

        @pl.when(odd == par)
        def _():
            for d in range(1, 5):
                out[16 * d - 16 : 16 * d] = core[par, 0, 4 - d if par else d - 1]
                if d < 4:
                    out[48 + 16 * d : 64 + 16 * d] = core[par, 1, 4 - d if par else d - 1]
            for d, at, n_cond, n_div in BESIDE:
                layer = 8 - d if par else d - 1
                for side in range(2):
                    cond, div = (0, 4) if side else (4 - n_cond, 7 - n_div)
                    out[at : at + n_cond] = sides[side, layer, cond : cond + n_cond]
                    if n_div:
                        out[at + n_cond : at + n_cond + n_div] = sides[side, layer, div : div + n_div]
                    at += n_cond + n_div


def stack0(core, near, put):
    h, _, high, _ = position()
    odd = lax.rem(h, 2)

    def far(par, d):
        return near[par, 16 * d - 16 : 16 * d], near[par, 48 + 16 * d : 64 + 16 * d] if d < 4 else None

    @pl.when(odd == 0)
    def _():
        for z in range(4):
            put(z, *far(0, 4 - z), h == 0)
            put(z + 4, core[0, 0, z], core[0, 1, z], None)
            put(z + 8, core[1, 0, z], core[1, 1, z], None)

    @pl.when(odd == 1)
    def _():
        for z in range(4):
            put(z, core[0, 0, z], core[0, 1, z], None)
            put(z + 4, core[1, 0, z], core[1, 1, z], None)
            put(z + 8, *far(1, z + 1), h == high - 1)


def k_edges0(core, edge):
    odd = lax.rem(lax.axis_index("height"), 2)
    for side in range(2):

        @pl.when(odd == side)
        def _():
            for z in range(8):
                edge[z, 0:4] = core[z // 4, 0, z % 4, 12 * side : 12 * side + 4]
                edge[z, 4:7] = core[z // 4, 1, z % 4, 13 * side : 13 * side + 3]
                edge[z, 7:8] = jnp.zeros((1, 512), F32)


def k_level0(core, near, sides, pre, w_out, g_out, cx_out, cy_out, cz_out, pack, c, g, w, cx, cy, cz, dg, p, rs, c1, st):
    h, plan, n_h, n_p = position()

    def put(z, cond, div, outside):
        c[z, 4:20] = cond if outside is None else jnp.where(outside, 1.0, cond)
        if div is not None:
            g[z, 4:20] = div

    stack0(core, near, put)
    for z in range(12):
        for first in (0, 20):
            c[z, first : first + 4] = jnp.ones((4, 512), F32)
            g[z, first : first + 4] = jnp.zeros((4, 512), F32)
    odd = lax.rem(h, 2)
    for par in range(2):

        @pl.when(odd == par)
        def _():
            for z in range(1, 8) if par else range(4, 11):
                for side, first, end in ((0, 0, plan == 0), (1, 20, plan == n_p - 1)):
                    rows = sides.at[side, z if par else z - 4]
                    c[z, first : first + 4] = jnp.where(end, 1.0, rows[0:4])
                    g[z, first + 1 - side : first + 4 - side] = rows[4:7]
            for d, at, n_cond, n_div in BESIDE:
                z = 7 + d if par else 4 - d
                for side, end in ((0, plan == 0), (1, plan == n_p - 1)):
                    out = jnp.logical_or(end, h == (n_h - 1 if par else 0))
                    first = 20 if side else 4 - n_cond
                    c[z, first : first + n_cond] = jnp.where(out, 1.0, near[par, at : at + n_cond])
                    first = 20 if side else 4 - n_div
                    if n_div:
                        g[z, first : first + n_div] = near[par, at + n_cond : at + n_cond + n_div]
                    at += n_cond + n_div

    row = iota((24, 512), 0) + (plan * 16 - 4)
    row_in = jnp.logical_and(row >= 0, row < n_p * 16).astype(F32) * OMEGA
    for z in range(11):
        cz[z] = harmonic(c[z], c[z + 1])
    for z in range(1, 11):
        here = c[z]
        fx = harmonic(here, ahead(here, 0))
        link, both = y_faces(here)
        diag = cz[z - 1] + cz[z] + fx + behind(fx, 0) + both
        weight = jnp.where(inside(h * 4 - 4, z, n_h * 4), row_in, 0.0) / diag
        cx[z] = fx
        cy[z] = link
        w[z] = weight
        if 4 <= z <= 7:
            dg[z - 4] = diag
            rs[z - 4] = g[z]
        g[z] = weight * g[z]
    for z in range(2, 10):
        here = g[z]
        total = spread(here, g[z - 1], g[z + 1], cz[z - 1], cz[z], cx[z], cy[z])
        p[z] = here * (1.0 / 3.0) + here + w[z] * total
    for z in range(4, 8):
        here = p[z]
        total = spread(here, p[z - 1], p[z + 1], cz[z - 1], cz[z], cx[z], cy[z])
        rs[z - 4] = rs[z - 4] - dg[z - 4] * here + total
    for z in range(2, 10):
        pre[z - 2] = p[z]
    for z in range(3, 9):
        w_out[z - 3] = w[z]
        g_out[z - 3] = g[z]
        cx_out[z - 3] = cx[z]
        cy_out[z - 3] = cy[z]
    for z in range(2, 9):
        cz_out[z - 2] = cz[z]
    rows = [pair_rows(st.at[z], rs[2 * z] + rs[2 * z + 1], 4, 8) for z in range(2)]
    for z in range(4):
        sums = c[2 * z + 2] + c[2 * z + 3]
        c1[z, 0:8] = pair_rows(st.at[2 + 2 * z], sums, 0, 8)
        c1[z, 8:12] = pair_rows(st.at[3 + 2 * z], sums[16:24], 0, 4)
        c1[z, 12:16] = jnp.full((4, 512), 4.0, F32)
    pairs = pair_matrix(512)
    f1 = 0.5 * dot(jnp.concatenate(rows, axis=0), pairs)
    k1 = 0.125 * dot(jnp.concatenate([c1[z] for z in range(4)], axis=0), pairs)
    k1 = [k1[16 * z : 16 * z + 16] for z in range(4)]
    for z in range(2):
        here = k1[z + 1]
        fx = harmonic(here, ahead(here, 0))
        link, both = y_faces(here)
        diag = harmonic(here, k1[z]) + harmonic(here, k1[z + 2]) + fx + behind(fx, 0) + both
        c1[z, :, 0:256] = here
        c1[z, :, 256:512] = diag
        pack[z, 0:8] = OMEGA * f1[8 * z : 8 * z + 8] / c1[z, 2:10, 256:512]
        pack[z, 8:16] = c1[z, 2:10, 0:256]


def k_edges1(chip, edge):
    odd = lax.rem(lax.axis_index("height"), 2)
    for side in range(2):

        @pl.when(odd == side)
        def _():
            for z in range(4):
                edge[z, 0:4] = chip[z, 4 * side : 4 * side + 4]
                edge[z, 4:8] = chip[z, 4 * side + 8 : 4 * side + 12]


def window1(even_layers, odd_layers, first, g, c):
    h, plan, n_h, n_p = position()
    for side, layers in ((0, even_layers), (1, odd_layers)):

        @pl.when(lax.rem(h, 2) == side)
        def _():
            for z, rows in enumerate(layers):
                keep = inside(first, z, n_h * 2)
                low, high = jnp.logical_and(keep, plan > 0), jnp.logical_and(keep, plan < n_p - 1)
                g[z, 4:12] = jnp.where(keep, rows[0:8], 0.0)
                c[z, 4:12] = jnp.where(keep, rows[8:16], 1.0)
                g[z, 0:4] = jnp.where(low, rows[16:20], 0.0)
                c[z, 0:4] = jnp.where(low, rows[20:24], 1.0)
                g[z, 12:16] = jnp.where(high, rows[24:28], 0.0)
                c[z, 12:16] = jnp.where(high, rows[28:32], 1.0)


def couple1(count, first, c, w, cx, cy, cz):
    h, plan, n_h, n_p = position()
    row = iota((16, 256), 0) + (plan * 8 - 4)
    row_in = jnp.logical_and(row >= 0, row < n_p * 8).astype(F32) * OMEGA
    for z in range(count - 1):
        cz[z] = harmonic(c[z], c[z + 1])
    diags = {}
    for z in range(1, count - 1):
        here = c[z]
        fx = harmonic(here, ahead(here, 0))
        link, both = y_faces(here)
        diags[z] = cz[z - 1] + cz[z] + fx + behind(fx, 0) + both
        cx[z] = fx
        cy[z] = link
        w[z] = jnp.where(inside(first, z, n_h * 2), row_in, 0.0) / diags[z]
    return diags


def k_level1_wide(full, two, pre, w_out, g_out, cx_out, cy_out, cz_out, c, g, w, cx, cy, cz):
    first = lax.axis_index("height") * 2 - 4
    layers = [two.at[0, z] for z in range(4)] + [full.at[z] for z in range(4)] + [two.at[1, z] for z in range(4)]
    window1(layers[0:10], layers[2:12], first, g, c)
    couple1(10, first, c, w, cx, cy, cz)
    for z in range(1, 9):
        here = g[z]
        total = spread(here, g[z - 1], g[z + 1], cz[z - 1], cz[z], cx[z], cy[z])
        pre[z - 1] = here * (1.0 / 3.0) + here + w[z] * total
    for z in range(2, 8):
        w_out[z - 2] = w[z]
        g_out[z - 2] = g[z]
        cx_out[z - 2] = cx[z]
        cy_out[z - 2] = cy[z]
    for z in range(1, 8):
        cz_out[z - 1] = cz[z]


def k_level1(full, near, copies, c, g, w, cx, cy, cz, p, rs, dg, st):
    first = lax.axis_index("height") * 2 - 2
    middle = [full.at[z] for z in range(4)]
    window1([near.at[0, 2], near.at[0, 3]] + middle, middle + [near.at[1, 0], near.at[1, 1]], first, g, c)
    diags = couple1(6, first, c, w, cx, cy, cz)
    for z in range(2):
        rs[z] = diags[z + 2]
    for z in range(1, 5):
        here = g[z]
        total = spread(here, g[z - 1], g[z + 1], cz[z - 1], cz[z], cx[z], cy[z])
        p[z] = here * (1.0 / 3.0) + here + w[z] * total
    for z in range(2, 4):
        here = p[z]
        total = spread(here, p[z - 1], p[z + 1], cz[z - 1], cz[z], cx[z], cy[z])
        rs[z - 2] = (g[z] - OMEGA * here + w[z] * total) * rs[z - 2] * 1.5
    rows = [pair_rows(st.at[0], rs[0] + rs[1], 0, 8)]
    rows += [pair_rows(st.at[z + 1], c[2 * z] + c[2 * z + 1], 0, 8) for z in range(3)]
    pairs = pair_matrix(256)
    both = jnp.concatenate(rows, axis=0)
    down = dot(both, pairs)
    f2 = 0.5 * down[0:8]
    k2 = [0.125 * down[8 * z + 8 : 8 * z + 16] for z in range(3)]
    here = k2[1]
    fx = harmonic(here, ahead(here, 0))
    link, share = y_faces(here)
    diag = harmonic(here, k2[0]) + harmonic(here, k2[2]) + fx + behind(fx, 0) + share
    dg[0, 0:8, 0:128] = diag
    dg[0, 8:16, 0:128] = here
    tile_g = OMEGA * f2[2:6] / dg[0, 2:6, 0:128]
    tile_c = dg[0, 10:14, 0:128]
    for i in range(copies.shape[0]):
        copies[i, 0:4] = tile_g
        copies[i, 4:8] = tile_c


def k_up(block, outer, pre1, w1, g1, cx1, cy1, cz1, pre0, w0, g0, cx0, cy0, cz0, out, sems, s, c, g, w, cx, cy, cz, dg, pa, pb, p2, u1, q1, u0, q0, s1, s0, done):
    h, plan, n_h, _ = position()
    wide = s.shape[1] // 2
    tiles = wide // 4
    for z in range(14):
        for t in range(tiles):
            at = tiles * (z % 2) + t
            rows = block.at[at] if 6 <= z < 8 else outer.at[z // 8, z % 8 // 2, at]
            s[z, 4 * t : 4 * t + 4] = rows[0:4]
            s[z, wide + 4 * t : wide + 4 * t + 4] = rows[4:8]
    q = lax.rem(h, 2)
    for z in range(13):
        keep = inside(h - 6, z, n_h)
        g[z] = jnp.where(keep, s[q + z, 0:wide], 0.0)
        c[z] = jnp.where(keep, s[q + z, wide : 2 * wide], 1.0)
    row = iota((wide, 128), 0)
    for z in range(12):
        cz[z] = harmonic(c[z], c[z + 1])
    for z in range(1, 12):
        here = c[z]
        full = harmonic(here, jnp.where(row == wide - 1, 1.0, ahead(here, 0)))
        fx = jnp.where(row == wide - 1, 0.0, full)
        first = jnp.where(row[0:8] == 0, harmonic(here[0:8], 1.0), 0.0)
        first = jnp.concatenate([first, jnp.zeros((wide - 8, 128), F32)], axis=0)
        link, both = y_faces(here)
        diag = cz[z - 1] + cz[z] + full + behind(fx, 0) + first + both
        cx[z] = fx
        cy[z] = link
        w[z] = jnp.where(inside(h - 6, z, n_h), OMEGA, 0.0) / diag
        dg[z] = diag

    def step(source, z):
        here = source[z]
        total = spread(here, source[z - 1], source[z + 1], cz[z - 1], cz[z], cx[z], cy[z])
        return here * (1.0 / 3.0) + g[z] + w[z] * total

    for z in range(1, 12):
        pa[z] = step(g, z)
    for z in range(2, 11):
        pb[z] = step(pa, z)
    for z in range(3, 10):
        pa[z] = step(pb, z)
    for z in range(4, 9):
        here = pa[z]
        extra = (step(pa, z) - here) * dg[z] * 1.5
        line = jnp.sum(extra, axis=0, keepdims=True) / jnp.sum(dg[z], axis=0, keepdims=True)
        p2[z - 4, 0:8] = jnp.zeros((8, 128), F32)
        p2[z - 4, wide + 8 : wide + 16] = jnp.zeros((8, 128), F32)
        p2[z - 4, 8 : wide + 8] = here + line
    rows = jnp.concatenate([p2[z, pl.ds(plan * 4 + 6, 8), :] for z in range(5)], axis=0)
    rows = dot(rows, copy_matrix(128))
    for z in range(5):
        u1[z] = copy_rows(s1.at[z], rows[8 * z : 8 * z + 8])
    for z in range(1, 9):
        q1[z - 1] = pre1[z - 1] + u1[z // 2]
    mid = []
    for z in range(2, 8):
        here = q1[z - 1]
        total = spread(here, q1[z - 2], q1[z], cz1[z - 2], cz1[z - 1], cx1[z - 2], cy1[z - 2])
        pb_rows = here * (1.0 / 3.0) + g1[z - 2] + w1[z - 2] * total
        mid.append(pb_rows)
    for z in range(6):
        q1[z] = mid[z]
    low = []
    for z in range(3, 7):
        here = q1[z - 2]
        total = spread(here, q1[z - 3], q1[z - 1], cz1[z - 2], cz1[z - 1], cx1[z - 2], cy1[z - 2])
        low.append(here * (1.0 / 3.0) + g1[z - 2] + w1[z - 2] * total)
    for z in range(4):
        q1[z] = low[z]
    rows = jnp.concatenate([q1[z] for z in range(4)], axis=0)
    rows = dot(rows, copy_matrix(256))
    for z in range(4):
        u0[z] = copy_rows(s0.at[z], rows[16 * z : 16 * z + 16])
    for z in range(2, 10):
        q0[z - 2] = pre0[z - 2] + u0[z // 2 - 1, 4:28]
    for z in range(3, 9):
        here = q0[z - 2]
        total = spread(here, q0[z - 3], q0[z - 1], cz0[z - 3], cz0[z - 2], cx0[z - 3], cy0[z - 3])
        u0[z - 3, 0:24] = here * (1.0 / 3.0) + g0[z - 3] + w0[z - 3] * total
    stores = []
    for z in range(4, 8):
        here = u0[z - 3, 0:24]
        total = spread(here, u0[z - 4, 0:24], u0[z - 2, 0:24], cz0[z - 3], cz0[z - 2], cx0[z - 3], cy0[z - 3])
        q0[z - 4] = here * (1.0 / 3.0) + g0[z - 3] + w0[z - 3] * total
        done[z - 4] = q0[z - 4, 4:20]
        stores.append(pltpu.make_async_copy(done.at[z - 4], out.at[z - 4], sems.at[z - 4]))
        stores[-1].start()
    for store in stores:
        store.wait()


def on_device(divergence, density, zones):
    n_h, n_p = lax.axis_size("height"), lax.axis_size("plan")
    odd = lax.rem(lax.axis_index("height"), 2)
    cores = [[i, i + 1] for i in range(0, n_h, 2)]

    def reach(step, others):
        pairs = [(i, i + step) for i in range(1, n_h - step, 2)] + others
        ends = sorted(set(range(n_h)) - {i for both in pairs for i in both})
        groups = [[i * n_p + t, j * n_p + t] for i, j in pairs for t in range(n_p)]
        return groups + [[i * n_p + t, i * n_p + t + 1] for i in ends for t in range(0, n_p, 2)]

    def meet(x, groups):
        return lax.all_gather(x, ("height", "plan"), axis=0, tiled=False, axis_index_groups=groups)

    def pair(x):
        return lax.all_gather(x, "height", axis=0, tiled=False, axis_index_groups=cores)

    links, leaps = reach(1, []), reach(5, [(0, 4), (n_h - 5, n_h - 1)])
    own = conductance(divergence, density, zones)
    core = pair(own)
    across = [[(2 * i + 1) * n_p + t, 2 * i * n_p + t + 1] for i in range(n_h // 2) for t in range(n_p - 1)]
    across += [[(2 * i + 1) * n_p + n_p - 1, (2 * i + 3) * n_p + n_p - 1] for i in range(0, n_h // 2, 2)]
    across += [[2 * i * n_p, (2 * i + 2) * n_p] for i in range(0, n_h // 2, 2)]

    def both_sides(edge):
        return pair(lax.dynamic_index_in_dim(meet(edge, across), odd, 0, keepdims=False))

    sides = both_sides(call(k_edges0, (8, 8, 512), [], core))
    near = meet(call(k_message0, (MESSAGE, 512), [], core, sides), links)
    box = (12, 24, 512)
    eight, six, seven = (8, 24, 512), (6, 24, 512), (7, 24, 512)
    *level0, pack = call(
        k_level0,
        [eight, six, six, six, six, seven, (2, 16, 256)],
        [box] * 6 + [(4, 24, 512), box, (4, 24, 512), (4, 16, 512), (10, 4, 24, 128)],
        core, near, sides,
    )
    chip = pair(pack).reshape(4, 16, 256)
    sides = both_sides(call(k_edges1, (4, 8, 256), [], chip))
    full = jnp.concatenate([chip, sides[0], sides[1]], axis=1)
    near = meet(full, links)
    box = (6, 16, 256)
    tiles = call(k_level1, (2 * n_p, 8, 128), [box] * 7 + [(2, 16, 256), (2, 16, 256), (4, 2, 16, 128)], full, near)
    two = pair(lax.dynamic_index_in_dim(near, odd, 0, keepdims=False))
    box = (10, 16, 256)
    eight, six, seven = (8, 16, 256), (6, 16, 256), (7, 16, 256)
    level1 = call(k_level1_wide, [eight, six, six, six, six, seven], [box] * 6, full, two)
    groups = [[(2 * i + k) * n_p + t for k in range(2) for t in range(n_p)] for i in range(n_h // 2)]
    block = lax.all_to_all(tiles, ("height", "plan"), split_axis=0, concat_axis=0, tiled=True, axis_index_groups=groups)
    near = meet(block, links)
    far = meet(near, leaps)
    side = jnp.where(odd == 0, jnp.concatenate([far[0], near[0:1]]), jnp.concatenate([near[1:2], far[1]]))
    outer = pair(side)
    wide = n_p * 4
    flat = (13, wide, 128)
    arrays = (block, outer, *level1, *level0)
    scratch = [(14, 2 * wide, 128)] + [flat] * 9
    scratch += [(5, wide + 16, 128), (5, 16, 256), (8, 16, 256), (6, 32, 512), (8, 24, 512), (5, 2, 16, 128), (4, 4, 32, 128), (4, 16, 512)]
    return pl.pallas_call(
        k_up,
        out_shape=jax.ShapeDtypeStruct((4, 16, 512), F32),
        in_specs=vmem(len(arrays)),
        out_specs=pl.BlockSpec(memory_space=pl.ANY),
        scratch_shapes=[pltpu.SemaphoreType.DMA((4,))] + [pltpu.VMEM(s, F32) for s in scratch],
        compiler_params=pltpu.CompilerParams(vmem_limit_bytes=40 << 20),
    )(*arrays)


def solution(mesh):
    return jax.shard_map(
        on_device,
        mesh=mesh,
        in_specs=(P("height", "plan", None), P("height", "plan", None), P("height", "plan", None)),
        out_specs=P("height", "plan", None),
        check_vma=False,
    )
```

```python
import jax
import jax.numpy as jnp
from jax import lax
from jax.experimental import pallas as pl
from jax.experimental.pallas import tpu as pltpu
from jax.sharding import PartitionSpec as P

PERMEABILITY = (1.0, 0.1, 0.6, 0.8, 0.25)
OMEGA = 2.0 / 3.0
F32 = jnp.float32


def vmem(count):
    return [pl.BlockSpec(memory_space=pltpu.VMEM)] * count


def position():
    return lax.axis_index("height"), lax.axis_index("plan"), lax.axis_size("height"), lax.axis_size("plan")


def call(body, outs, scratch, *arrays):
    many = isinstance(outs, list)
    shapes = [pltpu.VMEM(s, F32) if isinstance(s, tuple) else s for s in (outs if many else [outs])]
    return pl.pallas_call(
        body,
        out_shape=shapes if many else shapes[0],
        in_specs=vmem(len(arrays)),
        out_specs=vmem(len(shapes)) if many else vmem(1)[0],
        scratch_shapes=[pltpu.VMEM(s, F32) for s in scratch],
        compiler_params=pltpu.CompilerParams(vmem_limit_bytes=40 << 20),
    )(*arrays)


def harmonic(a, b):
    return 2.0 * a * b / (a + b)


def iota(shape, dim):
    return lax.broadcasted_iota(jnp.int32, shape, dim)


def ahead(x, axis):
    return pltpu.roll(x, x.shape[axis] - 1, axis)


def behind(x, axis):
    return pltpu.roll(x, 1, axis)


def y_faces(c):
    lane = iota(c.shape, 1)
    last = c.shape[1] - 1
    full = harmonic(c, jnp.where(lane == last, 1.0, ahead(c, 1)))
    link = jnp.where(lane == last, 0.0, full)
    first = jnp.where(iota((c.shape[0], 128), 1) == 0, harmonic(c[:, 0:128], 1.0), 0.0)
    if c.shape[1] > 128:
        first = jnp.concatenate([first, jnp.zeros((c.shape[0], c.shape[1] - 128), F32)], axis=1)
    return link, full + behind(link, 1) + first


def spread(p, below, above, cz0, cz1, cx, cy):
    total = cz0 * below + cz1 * above
    total = total + cx * ahead(p, 0) + behind(cx * p, 0)
    return total + cy * ahead(p, 1) + behind(cy * p, 1)


def pair_matrix(wide):
    shape = (wide, wide // 2)
    return (lax.shift_right_logical(iota(shape, 0), 1) == iota(shape, 1)).astype(jnp.bfloat16)


def copy_matrix(narrow):
    shape = (narrow, narrow * 2)
    return (iota(shape, 0) == lax.shift_right_logical(iota(shape, 1), 1)).astype(jnp.bfloat16)


def dot(a, ones):
    total = None
    for _ in range(3):
        part = a.astype(jnp.bfloat16)
        a = a - part.astype(F32)
        term = jnp.dot(part, ones, preferred_element_type=F32)
        total = term if total is None else total + term
    return total


def pair_rows(s, x, start, count):
    tiles = x.shape[1] // 128
    for t in range(tiles):
        s[t, 0 : x.shape[0]] = x[:, 128 * t : 128 * t + 128]
    parts = [s[t, pl.ds(start, count, stride=2), :] + s[t, pl.ds(start + 1, count, stride=2), :] for t in range(tiles)]
    return jnp.concatenate(parts, axis=1)


def copy_rows(s, x):
    tiles, count = x.shape[1] // 128, x.shape[0]
    for t in range(tiles):
        s[t, pl.ds(0, count, stride=2), :] = x[:, 128 * t : 128 * t + 128]
        s[t, pl.ds(1, count, stride=2), :] = x[:, 128 * t : 128 * t + 128]
    return jnp.concatenate([s[t, 0 : 2 * count] for t in range(tiles)], axis=1)


def inside(first, index, count):
    at = first + index
    return jnp.logical_and(at >= 0, at < count)


def k_conduct(div, density, zones, out, dens, zone_ids, sems):
    loads = []
    for z in range(4):
        loads.append(pltpu.make_async_copy(density.at[z], dens.at[z], sems.at[0, z]))
        loads.append(pltpu.make_async_copy(zones.at[z], zone_ids.at[z], sems.at[1, z]))
    loads += [pltpu.make_async_copy(div.at[z], out.at[1, z], sems.at[2, z]) for z in range(4)]
    for load in loads:
        load.start()
    for z in range(4):
        loads[2 * z].wait()
        loads[2 * z + 1].wait()
        zone = zone_ids[z]
        perm = jnp.where(zone == 0, PERMEABILITY[0], 0.0)
        for zone_id in range(1, 5):
            perm = jnp.where(zone == zone_id, PERMEABILITY[zone_id], perm)
        out[0, z] = perm / dens[z]
    for load in loads[8:]:
        load.wait()


def conductance(divergence, density, zones):
    shape = divergence.shape
    return pl.pallas_call(
        k_conduct,
        out_shape=pltpu.VMEM((2,) + shape, F32),
        in_specs=[pl.BlockSpec(memory_space=pl.ANY)] * 3,
        out_specs=vmem(1)[0],
        scratch_shapes=[pltpu.VMEM(shape, F32), pltpu.VMEM(shape, jnp.int32), pltpu.SemaphoreType.DMA((3, 4))],
    )(divergence, density, zones)


BESIDE = ((1, 112, 3, 2), (2, 122, 2, 1), (3, 128, 1, 0))
MESSAGE = 136


def k_message0(core, sides, out):
    odd = lax.rem(lax.axis_index("height"), 2)
    out[128:136] = jnp.zeros((8, 512), F32)
    for par in range(2):

        @pl.when(odd == par)
        def _():
            for d in range(1, 5):
                out[16 * d - 16 : 16 * d] = core[par, 0, 4 - d if par else d - 1]
                if d < 4:
                    out[48 + 16 * d : 64 + 16 * d] = core[par, 1, 4 - d if par else d - 1]
            for d, at, n_cond, n_div in BESIDE:
                layer = 8 - d if par else d - 1
                for side in range(2):
                    cond, div = (0, 4) if side else (4 - n_cond, 7 - n_div)
                    out[at : at + n_cond] = sides[side, layer, cond : cond + n_cond]
                    if n_div:
                        out[at + n_cond : at + n_cond + n_div] = sides[side, layer, div : div + n_div]
                    at += n_cond + n_div


def stack0(core, near, put):
    h, _, high, _ = position()
    odd = lax.rem(h, 2)

    def far(par, d):
        return near[par, 16 * d - 16 : 16 * d], near[par, 48 + 16 * d : 64 + 16 * d] if d < 4 else None

    @pl.when(odd == 0)
    def _():
        for z in range(4):
            put(z, *far(0, 4 - z), h == 0)
            put(z + 4, core[0, 0, z], core[0, 1, z], None)
            put(z + 8, core[1, 0, z], core[1, 1, z], None)

    @pl.when(odd == 1)
    def _():
        for z in range(4):
            put(z, core[0, 0, z], core[0, 1, z], None)
            put(z + 4, core[1, 0, z], core[1, 1, z], None)
            put(z + 8, *far(1, z + 1), h == high - 1)


def k_edges0(core, edge):
    odd = lax.rem(lax.axis_index("height"), 2)
    for side in range(2):

        @pl.when(odd == side)
        def _():
            for z in range(8):
                edge[z, 0:4] = core[z // 4, 0, z % 4, 12 * side : 12 * side + 4]
                edge[z, 4:7] = core[z // 4, 1, z % 4, 13 * side : 13 * side + 3]
                edge[z, 7:8] = jnp.zeros((1, 512), F32)


def k_level0(core, near, sides, p, w, g, cx, cy, cz, pack, c, dg, rs, c1, st):
    h, plan, n_h, n_p = position()

    def put(z, cond, div, outside):
        c[z, 4:20] = cond if outside is None else jnp.where(outside, 1.0, cond)
        if div is not None:
            g[z, 4:20] = div

    stack0(core, near, put)
    for z in range(12):
        for first in (0, 20):
            c[z, first : first + 4] = jnp.ones((4, 512), F32)
            g[z, first : first + 4] = jnp.zeros((4, 512), F32)
    odd = lax.rem(h, 2)
    for par in range(2):

        @pl.when(odd == par)
        def _():
            for z in range(1, 8) if par else range(4, 11):
                for side, first, end in ((0, 0, plan == 0), (1, 20, plan == n_p - 1)):
                    rows = sides.at[side, z if par else z - 4]
                    c[z, first : first + 4] = jnp.where(end, 1.0, rows[0:4])
                    g[z, first + 1 - side : first + 4 - side] = rows[4:7]
            for d, at, n_cond, n_div in BESIDE:
                z = 7 + d if par else 4 - d
                for side, end in ((0, plan == 0), (1, plan == n_p - 1)):
                    out = jnp.logical_or(end, h == (n_h - 1 if par else 0))
                    first = 20 if side else 4 - n_cond
                    c[z, first : first + n_cond] = jnp.where(out, 1.0, near[par, at : at + n_cond])
                    first = 20 if side else 4 - n_div
                    if n_div:
                        g[z, first : first + n_div] = near[par, at + n_cond : at + n_cond + n_div]
                    at += n_cond + n_div

    row = iota((24, 512), 0) + (plan * 16 - 4)
    row_in = jnp.logical_and(row >= 0, row < n_p * 16).astype(F32) * OMEGA
    for z in range(11):
        cz[z] = harmonic(c[z], c[z + 1])
    for z in range(1, 11):
        here = c[z]
        fx = harmonic(here, ahead(here, 0))
        link, both = y_faces(here)
        diag = cz[z - 1] + cz[z] + fx + behind(fx, 0) + both
        weight = jnp.where(inside(h * 4 - 4, z, n_h * 4), row_in, 0.0) / diag
        cx[z] = fx
        cy[z] = link
        w[z] = weight
        if 4 <= z <= 7:
            dg[z - 4] = diag
            rs[z - 4] = g[z]
        g[z] = weight * g[z]
    for z in range(2, 10):
        here = g[z]
        total = spread(here, g[z - 1], g[z + 1], cz[z - 1], cz[z], cx[z], cy[z])
        p[z] = here * (1.0 / 3.0) + here + w[z] * total
    for z in range(4, 8):
        here = p[z]
        total = spread(here, p[z - 1], p[z + 1], cz[z - 1], cz[z], cx[z], cy[z])
        rs[z - 4] = rs[z - 4] - dg[z - 4] * here + total
    rows = [pair_rows(st.at[z], rs[2 * z] + rs[2 * z + 1], 4, 8) for z in range(2)]
    for z in range(4):
        sums = c[2 * z + 2] + c[2 * z + 3]
        c1[z, 0:8] = pair_rows(st.at[2 + 2 * z], sums, 0, 8)
        c1[z, 8:12] = pair_rows(st.at[3 + 2 * z], sums[16:24], 0, 4)
        c1[z, 12:16] = jnp.full((4, 512), 4.0, F32)
    pairs = pair_matrix(512)
    f1 = 0.5 * dot(jnp.concatenate(rows, axis=0), pairs)
    k1 = 0.125 * dot(jnp.concatenate([c1[z] for z in range(4)], axis=0), pairs)
    k1 = [k1[16 * z : 16 * z + 16] for z in range(4)]
    for z in range(2):
        here = k1[z + 1]
        fx = harmonic(here, ahead(here, 0))
        link, both = y_faces(here)
        diag = harmonic(here, k1[z]) + harmonic(here, k1[z + 2]) + fx + behind(fx, 0) + both
        c1[z, :, 0:256] = here
        c1[z, :, 256:512] = diag
        pack[z, 0:8] = OMEGA * f1[8 * z : 8 * z + 8] / c1[z, 2:10, 256:512]
        pack[z, 8:16] = c1[z, 2:10, 0:256]


def k_edges1(chip, edge):
    odd = lax.rem(lax.axis_index("height"), 2)
    for side in range(2):

        @pl.when(odd == side)
        def _():
            for z in range(4):
                edge[z, 0:4] = chip[z, 4 * side : 4 * side + 4]
                edge[z, 4:8] = chip[z, 4 * side + 8 : 4 * side + 12]


def window1(even_layers, odd_layers, first, g, c):
    h, plan, n_h, n_p = position()
    for side, layers in ((0, even_layers), (1, odd_layers)):

        @pl.when(lax.rem(h, 2) == side)
        def _():
            for z, rows in enumerate(layers):
                keep = inside(first, z, n_h * 2)
                low, high = jnp.logical_and(keep, plan > 0), jnp.logical_and(keep, plan < n_p - 1)
                g[z, 4:12] = jnp.where(keep, rows[0:8], 0.0)
                c[z, 4:12] = jnp.where(keep, rows[8:16], 1.0)
                g[z, 0:4] = jnp.where(low, rows[16:20], 0.0)
                c[z, 0:4] = jnp.where(low, rows[20:24], 1.0)
                g[z, 12:16] = jnp.where(high, rows[24:28], 0.0)
                c[z, 12:16] = jnp.where(high, rows[28:32], 1.0)


def couple1(count, first, c, w, cx, cy, cz):
    h, plan, n_h, n_p = position()
    row = iota((16, 256), 0) + (plan * 8 - 4)
    row_in = jnp.logical_and(row >= 0, row < n_p * 8).astype(F32) * OMEGA
    for z in range(count - 1):
        cz[z] = harmonic(c[z], c[z + 1])
    diags = {}
    for z in range(1, count - 1):
        here = c[z]
        fx = harmonic(here, ahead(here, 0))
        link, both = y_faces(here)
        diags[z] = cz[z - 1] + cz[z] + fx + behind(fx, 0) + both
        cx[z] = fx
        cy[z] = link
        w[z] = jnp.where(inside(first, z, n_h * 2), row_in, 0.0) / diags[z]
    return diags


def k_level1_wide(full, two, pre, w_out, g_out, cx_out, cy_out, cz_out, twice2, twice1, c, g, w, cx, cy, cz):
    first = lax.axis_index("height") * 2 - 4
    layers = [two.at[0, z] for z in range(4)] + [full.at[z] for z in range(4)] + [two.at[1, z] for z in range(4)]
    window1(layers[0:10], layers[2:12], first, g, c)
    twice2[...] = copy_matrix(128)
    twice1[...] = copy_matrix(256)
    couple1(10, first, c, w, cx, cy, cz)
    for z in range(1, 9):
        here = g[z]
        total = spread(here, g[z - 1], g[z + 1], cz[z - 1], cz[z], cx[z], cy[z])
        pre[z - 1] = here * (1.0 / 3.0) + here + w[z] * total
    for z in range(2, 8):
        w_out[z - 2] = w[z]
        g_out[z - 2] = g[z]
        cx_out[z - 2] = cx[z]
        cy_out[z - 2] = cy[z]
    for z in range(1, 8):
        cz_out[z - 1] = cz[z]


def k_level1(full, near, copies, c, g, w, cx, cy, cz, p, rs, dg, st):
    first = lax.axis_index("height") * 2 - 2
    middle = [full.at[z] for z in range(4)]
    window1([near.at[0, 2], near.at[0, 3]] + middle, middle + [near.at[1, 0], near.at[1, 1]], first, g, c)
    diags = couple1(6, first, c, w, cx, cy, cz)
    for z in range(2):
        rs[z] = diags[z + 2]
    for z in range(1, 5):
        here = g[z]
        total = spread(here, g[z - 1], g[z + 1], cz[z - 1], cz[z], cx[z], cy[z])
        p[z] = here * (1.0 / 3.0) + here + w[z] * total
    for z in range(2, 4):
        here = p[z]
        total = spread(here, p[z - 1], p[z + 1], cz[z - 1], cz[z], cx[z], cy[z])
        rs[z - 2] = (g[z] - OMEGA * here + w[z] * total) * rs[z - 2] * 1.5
    rows = [pair_rows(st.at[0], rs[0] + rs[1], 0, 8)]
    rows += [pair_rows(st.at[z + 1], c[2 * z] + c[2 * z + 1], 0, 8) for z in range(3)]
    pairs = pair_matrix(256)
    both = jnp.concatenate(rows, axis=0)
    down = dot(both, pairs)
    f2 = 0.5 * down[0:8]
    k2 = [0.125 * down[8 * z + 8 : 8 * z + 16] for z in range(3)]
    here = k2[1]
    fx = harmonic(here, ahead(here, 0))
    link, share = y_faces(here)
    diag = harmonic(here, k2[0]) + harmonic(here, k2[2]) + fx + behind(fx, 0) + share
    dg[0, 0:8, 0:128] = diag
    dg[0, 8:16, 0:128] = here
    tile_g = OMEGA * f2[2:6] / dg[0, 2:6, 0:128]
    tile_c = dg[0, 10:14, 0:128]
    for i in range(copies.shape[0]):
        copies[i, 0:4] = tile_g
        copies[i, 4:8] = tile_c


def k_up(block, outer, pre1, w1, g1, cx1, cy1, cz1, twice2, twice1, pre0, w0, g0, cx0, cy0, cz0, out, sems, s, c, g, w, cx, cy, cz, dg, pa, pb, p2, u1, q1, u0, q0, s1, s0, done):
    h, plan, n_h, _ = position()
    wide = s.shape[1] // 2
    tiles = wide // 4
    for z in range(14):
        for t in range(tiles):
            at = tiles * (z % 2) + t
            rows = block.at[at] if 6 <= z < 8 else outer.at[z // 8, z % 8 // 2, at]
            s[z, 4 * t : 4 * t + 4] = rows[0:4]
            s[z, wide + 4 * t : wide + 4 * t + 4] = rows[4:8]
    q = lax.rem(h, 2)
    for z in range(13):
        keep = inside(h - 6, z, n_h)
        g[z] = jnp.where(keep, s[q + z, 0:wide], 0.0)
        c[z] = jnp.where(keep, s[q + z, wide : 2 * wide], 1.0)
    row = iota((wide, 128), 0)
    for z in range(12):
        cz[z] = harmonic(c[z], c[z + 1])
    for z in range(1, 12):
        here = c[z]
        full = harmonic(here, jnp.where(row == wide - 1, 1.0, ahead(here, 0)))
        fx = jnp.where(row == wide - 1, 0.0, full)
        first = jnp.where(row[0:8] == 0, harmonic(here[0:8], 1.0), 0.0)
        first = jnp.concatenate([first, jnp.zeros((wide - 8, 128), F32)], axis=0)
        link, both = y_faces(here)
        diag = cz[z - 1] + cz[z] + full + behind(fx, 0) + first + both
        cx[z] = fx
        cy[z] = link
        w[z] = jnp.where(inside(h - 6, z, n_h), OMEGA, 0.0) / diag
        dg[z] = diag

    def step(source, z):
        here = source[z]
        total = spread(here, source[z - 1], source[z + 1], cz[z - 1], cz[z], cx[z], cy[z])
        return here * (1.0 / 3.0) + g[z] + w[z] * total

    for z in range(1, 12):
        pa[z] = step(g, z)
    for z in range(2, 11):
        pb[z] = step(pa, z)
    for z in range(3, 10):
        pa[z] = step(pb, z)
    for z in range(4, 9):
        here = pa[z]
        extra = (step(pa, z) - here) * dg[z] * 1.5
        line = jnp.sum(extra, axis=0, keepdims=True) / jnp.sum(dg[z], axis=0, keepdims=True)
        p2[z - 4, 0:8] = jnp.zeros((8, 128), F32)
        p2[z - 4, wide + 8 : wide + 16] = jnp.zeros((8, 128), F32)
        p2[z - 4, 8 : wide + 8] = here + line
    rows = jnp.concatenate([p2[z, pl.ds(plan * 4 + 6, 8), :] for z in range(5)], axis=0)
    rows = dot(rows, twice2[...])
    for z in range(5):
        u1[z] = copy_rows(s1.at[z], rows[8 * z : 8 * z + 8])
    for z in range(1, 9):
        q1[z - 1] = pre1[z - 1] + u1[z // 2]
    mid = []
    for z in range(2, 8):
        here = q1[z - 1]
        total = spread(here, q1[z - 2], q1[z], cz1[z - 2], cz1[z - 1], cx1[z - 2], cy1[z - 2])
        pb_rows = here * (1.0 / 3.0) + g1[z - 2] + w1[z - 2] * total
        mid.append(pb_rows)
    for z in range(6):
        q1[z] = mid[z]
    low = []
    for z in range(3, 7):
        here = q1[z - 2]
        total = spread(here, q1[z - 3], q1[z - 1], cz1[z - 2], cz1[z - 1], cx1[z - 2], cy1[z - 2])
        low.append(here * (1.0 / 3.0) + g1[z - 2] + w1[z - 2] * total)
    for z in range(4):
        q1[z] = low[z]
    rows = jnp.concatenate([q1[z] for z in range(4)], axis=0)
    rows = dot(rows, twice1[...])
    for z in range(4):
        u0[z] = copy_rows(s0.at[z], rows[16 * z : 16 * z + 16])
    for z in range(2, 10):
        q0[z - 2] = pre0[z] + u0[z // 2 - 1, 4:28]
    for z in range(3, 9):
        here = q0[z - 2]
        total = spread(here, q0[z - 3], q0[z - 1], cz0[z - 1], cz0[z], cx0[z], cy0[z])
        u0[z - 3, 0:24] = here * (1.0 / 3.0) + g0[z] + w0[z] * total
    stores = []
    for z in range(4, 8):
        here = u0[z - 3, 0:24]
        total = spread(here, u0[z - 4, 0:24], u0[z - 2, 0:24], cz0[z - 1], cz0[z], cx0[z], cy0[z])
        q0[z - 4] = here * (1.0 / 3.0) + g0[z] + w0[z] * total
        done[z - 4] = q0[z - 4, 4:20]
        stores.append(pltpu.make_async_copy(done.at[z - 4], out.at[z - 4], sems.at[z - 4]))
        stores[-1].start()
    for store in stores:
        store.wait()


def on_device(divergence, density, zones):
    n_h, n_p = lax.axis_size("height"), lax.axis_size("plan")
    odd = lax.rem(lax.axis_index("height"), 2)
    cores = [[i, i + 1] for i in range(0, n_h, 2)]

    def reach(step, others):
        pairs = [(i, i + step) for i in range(1, n_h - step, 2)] + others
        ends = sorted(set(range(n_h)) - {i for both in pairs for i in both})
        groups = [[i * n_p + t, j * n_p + t] for i, j in pairs for t in range(n_p)]
        return groups + [[i * n_p + t, i * n_p + t + 1] for i in ends for t in range(0, n_p, 2)]

    def meet(x, groups):
        return lax.all_gather(x, ("height", "plan"), axis=0, tiled=False, axis_index_groups=groups)

    def pair(x):
        return lax.all_gather(x, "height", axis=0, tiled=False, axis_index_groups=cores)

    links, leaps = reach(1, []), reach(5, [(0, 4), (n_h - 5, n_h - 1)])
    own = conductance(divergence, density, zones)
    core = pair(own)
    across = [[(2 * i + 1) * n_p + t, 2 * i * n_p + t + 1] for i in range(n_h // 2) for t in range(n_p - 1)]
    across += [[(2 * i + 1) * n_p + n_p - 1, (2 * i + 3) * n_p + n_p - 1] for i in range(0, n_h // 2, 2)]
    across += [[2 * i * n_p, (2 * i + 2) * n_p] for i in range(0, n_h // 2, 2)]

    def both_sides(edge):
        return pair(lax.dynamic_index_in_dim(meet(edge, across), odd, 0, keepdims=False))

    sides = both_sides(call(k_edges0, (8, 8, 512), [], core))
    near = meet(call(k_message0, (MESSAGE, 512), [], core, sides), links)
    box = (12, 24, 512)
    eight, six, seven = (8, 24, 512), (6, 24, 512), (7, 24, 512)
    *level0, pack = call(
        k_level0,
        [box] * 6 + [(2, 16, 256)],
        [box, (4, 24, 512), (4, 24, 512), (4, 16, 512), (10, 4, 24, 128)],
        core, near, sides,
    )
    chip = pair(pack).reshape(4, 16, 256)
    sides = both_sides(call(k_edges1, (4, 8, 256), [], chip))
    full = jnp.concatenate([chip, sides[0], sides[1]], axis=1)
    near = meet(full, links)
    box = (6, 16, 256)
    tiles = call(k_level1, (2 * n_p, 8, 128), [box] * 7 + [(2, 16, 256), (2, 16, 256), (4, 2, 16, 128)], full, near)
    two = pair(lax.dynamic_index_in_dim(near, odd, 0, keepdims=False))
    box = (10, 16, 256)
    eight, six, seven = (8, 16, 256), (6, 16, 256), (7, 16, 256)
    twice = [pltpu.VMEM((128, 256), jnp.bfloat16), pltpu.VMEM((256, 512), jnp.bfloat16)]
    level1 = call(k_level1_wide, [eight, six, six, six, six, seven, *twice], [box] * 6, full, two)
    groups = [[(2 * i + k) * n_p + t for k in range(2) for t in range(n_p)] for i in range(n_h // 2)]
    block = lax.all_to_all(tiles, ("height", "plan"), split_axis=0, concat_axis=0, tiled=True, axis_index_groups=groups)
    near = meet(block, links)
    far = meet(near, leaps)
    side = jnp.where(odd == 0, jnp.concatenate([far[0], near[0:1]]), jnp.concatenate([near[1:2], far[1]]))
    outer = pair(side)
    wide = n_p * 4
    flat = (13, wide, 128)
    arrays = (block, outer, *level1, *level0)
    scratch = [(14, 2 * wide, 128)] + [flat] * 9
    scratch += [(5, wide + 16, 128), (5, 16, 256), (8, 16, 256), (6, 32, 512), (8, 24, 512), (5, 2, 16, 128), (4, 4, 32, 128), (4, 16, 512)]
    return pl.pallas_call(
        k_up,
        out_shape=jax.ShapeDtypeStruct((4, 16, 512), F32),
        in_specs=vmem(len(arrays)),
        out_specs=pl.BlockSpec(memory_space=pl.ANY),
        scratch_shapes=[pltpu.SemaphoreType.DMA((4,))] + [pltpu.VMEM(s, F32) for s in scratch],
        compiler_params=pltpu.CompilerParams(vmem_limit_bytes=40 << 20),
    )(*arrays)


def solution(mesh):
    return jax.shard_map(
        on_device,
        mesh=mesh,
        in_specs=(P("height", "plan", None), P("height", "plan", None), P("height", "plan", None)),
        out_specs=P("height", "plan", None),
        check_vma=False,
    )
```

```python
import jax
import jax.numpy as jnp
from jax import lax
from jax.experimental import pallas as pl
from jax.experimental.pallas import tpu as pltpu
from jax.sharding import PartitionSpec as P

PERMEABILITY = (1.0, 0.1, 0.6, 0.8, 0.25)
OMEGA = 2.0 / 3.0
F32 = jnp.float32


def vmem(count):
    return [pl.BlockSpec(memory_space=pltpu.VMEM)] * count


def position():
    return lax.axis_index("height"), lax.axis_index("plan"), lax.axis_size("height"), lax.axis_size("plan")


def call(body, outs, scratch, *arrays):
    many = isinstance(outs, list)
    shapes = [pltpu.VMEM(s, F32) for s in (outs if many else [outs])]
    return pl.pallas_call(
        body,
        out_shape=shapes if many else shapes[0],
        in_specs=vmem(len(arrays)),
        out_specs=vmem(len(shapes)) if many else vmem(1)[0],
        scratch_shapes=[pltpu.VMEM(s, F32) for s in scratch],
        compiler_params=pltpu.CompilerParams(vmem_limit_bytes=40 << 20),
    )(*arrays)


def harmonic(a, b):
    return 2.0 * a * b / (a + b)


def iota(shape, dim):
    return lax.broadcasted_iota(jnp.int32, shape, dim)


def ahead(x, axis):
    return pltpu.roll(x, x.shape[axis] - 1, axis)


def behind(x, axis):
    return pltpu.roll(x, 1, axis)


def y_faces(c):
    lane = iota(c.shape, 1)
    last = c.shape[1] - 1
    full = harmonic(c, jnp.where(lane == last, 1.0, ahead(c, 1)))
    link = jnp.where(lane == last, 0.0, full)
    first = jnp.where(iota((c.shape[0], 128), 1) == 0, harmonic(c[:, 0:128], 1.0), 0.0)
    if c.shape[1] > 128:
        first = jnp.concatenate([first, jnp.zeros((c.shape[0], c.shape[1] - 128), F32)], axis=1)
    return link, full + behind(link, 1) + first


def spread(p, below, above, cz0, cz1, cx, cy):
    total = cz0 * below + cz1 * above
    total = total + cx * ahead(p, 0) + behind(cx * p, 0)
    return total + cy * ahead(p, 1) + behind(cy * p, 1)


def pair_matrix(wide):
    shape = (wide, wide // 2)
    return (lax.shift_right_logical(iota(shape, 0), 1) == iota(shape, 1)).astype(jnp.bfloat16)


def copy_matrix(narrow):
    shape = (narrow, narrow * 2)
    return (iota(shape, 0) == lax.shift_right_logical(iota(shape, 1), 1)).astype(jnp.bfloat16)


def dot(a, ones):
    total = None
    for _ in range(3):
        part = a.astype(jnp.bfloat16)
        a = a - part.astype(F32)
        term = jnp.dot(part, ones, preferred_element_type=F32)
        total = term if total is None else total + term
    return total


def pair_rows(s, x, start, count):
    tiles = x.shape[1] // 128
    for t in range(tiles):
        s[t, 0 : x.shape[0]] = x[:, 128 * t : 128 * t + 128]
    parts = [s[t, pl.ds(start, count, stride=2), :] + s[t, pl.ds(start + 1, count, stride=2), :] for t in range(tiles)]
    return jnp.concatenate(parts, axis=1)


def copy_rows(s, x):
    tiles, count = x.shape[1] // 128, x.shape[0]
    for t in range(tiles):
        s[t, pl.ds(0, count, stride=2), :] = x[:, 128 * t : 128 * t + 128]
        s[t, pl.ds(1, count, stride=2), :] = x[:, 128 * t : 128 * t + 128]
    return jnp.concatenate([s[t, 0 : 2 * count] for t in range(tiles)], axis=1)


def inside(first, index, count):
    at = first + index
    return jnp.logical_and(at >= 0, at < count)


def k_conduct(div, density, zones, out, dens, zone_ids, sems):
    loads = []
    for z in range(4):
        loads.append(pltpu.make_async_copy(density.at[z], dens.at[z], sems.at[0, z]))
        loads.append(pltpu.make_async_copy(zones.at[z], zone_ids.at[z], sems.at[1, z]))
    loads += [pltpu.make_async_copy(div.at[z], out.at[1, z], sems.at[2, z]) for z in range(4)]
    for load in loads:
        load.start()
    for z in range(4):
        loads[2 * z].wait()
        loads[2 * z + 1].wait()
        zone = zone_ids[z]
        perm = jnp.where(zone == 0, PERMEABILITY[0], 0.0)
        for zone_id in range(1, 5):
            perm = jnp.where(zone == zone_id, PERMEABILITY[zone_id], perm)
        out[0, z] = perm / dens[z]
    for load in loads[8:]:
        load.wait()


def conductance(divergence, density, zones):
    shape = divergence.shape
    return pl.pallas_call(
        k_conduct,
        out_shape=pltpu.VMEM((2,) + shape, F32),
        in_specs=[pl.BlockSpec(memory_space=pl.ANY)] * 3,
        out_specs=vmem(1)[0],
        scratch_shapes=[pltpu.VMEM(shape, F32), pltpu.VMEM(shape, jnp.int32), pltpu.SemaphoreType.DMA((3, 4))],
    )(divergence, density, zones)


BESIDE = ((1, 112, 3, 2), (2, 122, 2, 1), (3, 128, 1, 0))
MESSAGE = 136


def k_message0(core, sides, out):
    odd = lax.rem(lax.axis_index("height"), 2)
    out[128:136] = jnp.zeros((8, 512), F32)
    for par in range(2):

        @pl.when(odd == par)
        def _():
            for d in range(1, 5):
                out[16 * d - 16 : 16 * d] = core[par, 0, 4 - d if par else d - 1]
                if d < 4:
                    out[48 + 16 * d : 64 + 16 * d] = core[par, 1, 4 - d if par else d - 1]
            for d, at, n_cond, n_div in BESIDE:
                layer = 8 - d if par else d - 1
                for side in range(2):
                    cond, div = (0, 4) if side else (4 - n_cond, 7 - n_div)
                    out[at : at + n_cond] = sides[side, layer, cond : cond + n_cond]
                    if n_div:
                        out[at + n_cond : at + n_cond + n_div] = sides[side, layer, div : div + n_div]
                    at += n_cond + n_div


def stack0(core, near, put):
    h, _, high, _ = position()
    odd = lax.rem(h, 2)

    def far(par, d):
        return near[par, 16 * d - 16 : 16 * d], near[par, 48 + 16 * d : 64 + 16 * d] if d < 4 else None

    @pl.when(odd == 0)
    def _():
        for z in range(4):
            put(z, *far(0, 4 - z), h == 0)
            put(z + 4, core[0, 0, z], core[0, 1, z], None)
            put(z + 8, core[1, 0, z], core[1, 1, z], None)

    @pl.when(odd == 1)
    def _():
        for z in range(4):
            put(z, core[0, 0, z], core[0, 1, z], None)
            put(z + 4, core[1, 0, z], core[1, 1, z], None)
            put(z + 8, *far(1, z + 1), h == high - 1)


def k_edges0(core, edge):
    odd = lax.rem(lax.axis_index("height"), 2)
    for side in range(2):

        @pl.when(odd == side)
        def _():
            for z in range(8):
                edge[z, 0:4] = core[z // 4, 0, z % 4, 12 * side : 12 * side + 4]
                edge[z, 4:7] = core[z // 4, 1, z % 4, 13 * side : 13 * side + 3]
                edge[z, 7:8] = jnp.zeros((1, 512), F32)


def k_level0(core, near, sides, pre, w_out, g_out, cx_out, cy_out, cz_out, pack, c, g, w, cx, cy, cz, dg, p, rs, c1, st):
    h, plan, n_h, n_p = position()

    def put(z, cond, div, outside):
        c[z, 4:20] = cond if outside is None else jnp.where(outside, 1.0, cond)
        if div is not None:
            g[z, 4:20] = div

    stack0(core, near, put)
    for z in range(12):
        for first in (0, 20):
            c[z, first : first + 4] = jnp.ones((4, 512), F32)
            g[z, first : first + 4] = jnp.zeros((4, 512), F32)
    odd = lax.rem(h, 2)
    for par in range(2):

        @pl.when(odd == par)
        def _():
            for z in range(1, 8) if par else range(4, 11):
                for side, first, end in ((0, 0, plan == 0), (1, 20, plan == n_p - 1)):
                    rows = sides.at[side, z if par else z - 4]
                    c[z, first : first + 4] = jnp.where(end, 1.0, rows[0:4])
                    g[z, first + 1 - side : first + 4 - side] = rows[4:7]
            for d, at, n_cond, n_div in BESIDE:
                z = 7 + d if par else 4 - d
                for side, end in ((0, plan == 0), (1, plan == n_p - 1)):
                    out = jnp.logical_or(end, h == (n_h - 1 if par else 0))
                    first = 20 if side else 4 - n_cond
                    c[z, first : first + n_cond] = jnp.where(out, 1.0, near[par, at : at + n_cond])
                    first = 20 if side else 4 - n_div
                    if n_div:
                        g[z, first : first + n_div] = near[par, at + n_cond : at + n_cond + n_div]
                    at += n_cond + n_div

    row = iota((24, 512), 0) + (plan * 16 - 4)
    row_in = jnp.logical_and(row >= 0, row < n_p * 16).astype(F32) * OMEGA
    for z in range(11):
        cz[z] = harmonic(c[z], c[z + 1])
    for z in range(1, 11):
        here = c[z]
        fx = harmonic(here, ahead(here, 0))
        link, both = y_faces(here)
        diag = cz[z - 1] + cz[z] + fx + behind(fx, 0) + both
        weight = jnp.where(inside(h * 4 - 4, z, n_h * 4), row_in, 0.0) / diag
        cx[z] = fx
        cy[z] = link
        w[z] = weight
        if 4 <= z <= 7:
            dg[z - 4] = diag
            rs[z - 4] = g[z]
        g[z] = weight * g[z]
    for z in range(2, 10):
        here = g[z]
        total = spread(here, g[z - 1], g[z + 1], cz[z - 1], cz[z], cx[z], cy[z])
        p[z] = here * (1.0 / 3.0) + here + w[z] * total
    for z in range(4, 8):
        here = p[z]
        total = spread(here, p[z - 1], p[z + 1], cz[z - 1], cz[z], cx[z], cy[z])
        rs[z - 4] = rs[z - 4] - dg[z - 4] * here + total
    for z in range(2, 10):
        pre[z - 2] = p[z]
    for z in range(3, 9):
        w_out[z - 3] = w[z]
        g_out[z - 3] = g[z]
        cx_out[z - 3] = cx[z]
        cy_out[z - 3] = cy[z]
    for z in range(2, 9):
        cz_out[z - 2] = cz[z]
    rows = [pair_rows(st.at[z], rs[2 * z] + rs[2 * z + 1], 4, 8) for z in range(2)]
    for z in range(4):
        sums = c[2 * z + 2] + c[2 * z + 3]
        c1[z, 0:8] = pair_rows(st.at[2 + 2 * z], sums, 0, 8)
        c1[z, 8:12] = pair_rows(st.at[3 + 2 * z], sums[16:24], 0, 4)
        c1[z, 12:16] = jnp.full((4, 512), 4.0, F32)
    pairs = pair_matrix(512)
    f1 = 0.5 * dot(jnp.concatenate(rows, axis=0), pairs)
    k1 = 0.125 * dot(jnp.concatenate([c1[z] for z in range(4)], axis=0), pairs)
    k1 = [k1[16 * z : 16 * z + 16] for z in range(4)]
    for z in range(2):
        here = k1[z + 1]
        fx = harmonic(here, ahead(here, 0))
        link, both = y_faces(here)
        diag = harmonic(here, k1[z]) + harmonic(here, k1[z + 2]) + fx + behind(fx, 0) + both
        c1[z, :, 0:256] = here
        c1[z, :, 256:512] = diag
        pack[z, 0:8] = OMEGA * f1[8 * z : 8 * z + 8] / c1[z, 2:10, 256:512]
        pack[z, 8:16] = c1[z, 2:10, 0:256]


def k_edges1(chip, edge):
    odd = lax.rem(lax.axis_index("height"), 2)
    for side in range(2):

        @pl.when(odd == side)
        def _():
            for z in range(4):
                edge[z, 0:4] = chip[z, 4 * side : 4 * side + 4]
                edge[z, 4:8] = chip[z, 4 * side + 8 : 4 * side + 12]


def window1(even_layers, odd_layers, first, g, c):
    h, plan, n_h, n_p = position()
    for side, layers in ((0, even_layers), (1, odd_layers)):

        @pl.when(lax.rem(h, 2) == side)
        def _():
            for z, rows in enumerate(layers):
                keep = inside(first, z, n_h * 2)
                low, high = jnp.logical_and(keep, plan > 0), jnp.logical_and(keep, plan < n_p - 1)
                g[z, 4:12] = jnp.where(keep, rows[0:8], 0.0)
                c[z, 4:12] = jnp.where(keep, rows[8:16], 1.0)
                g[z, 0:4] = jnp.where(low, rows[16:20], 0.0)
                c[z, 0:4] = jnp.where(low, rows[20:24], 1.0)
                g[z, 12:16] = jnp.where(high, rows[24:28], 0.0)
                c[z, 12:16] = jnp.where(high, rows[28:32], 1.0)


def couple1(count, first, c, w, cx, cy, cz):
    h, plan, n_h, n_p = position()
    row = iota((16, 256), 0) + (plan * 8 - 4)
    row_in = jnp.logical_and(row >= 0, row < n_p * 8).astype(F32) * OMEGA
    for z in range(count - 1):
        cz[z] = harmonic(c[z], c[z + 1])
    diags = {}
    for z in range(1, count - 1):
        here = c[z]
        fx = harmonic(here, ahead(here, 0))
        link, both = y_faces(here)
        diags[z] = cz[z - 1] + cz[z] + fx + behind(fx, 0) + both
        cx[z] = fx
        cy[z] = link
        w[z] = jnp.where(inside(first, z, n_h * 2), row_in, 0.0) / diags[z]
    return diags


def k_level1_wide(full, two, pre, w_out, g_out, cx_out, cy_out, cz_out, c, g, w, cx, cy, cz):
    first = lax.axis_index("height") * 2 - 4
    layers = [two.at[0, z] for z in range(4)] + [full.at[z] for z in range(4)] + [two.at[1, z] for z in range(4)]
    window1(layers[0:10], layers[2:12], first, g, c)
    couple1(10, first, c, w, cx, cy, cz)
    for z in range(1, 9):
        here = g[z]
        total = spread(here, g[z - 1], g[z + 1], cz[z - 1], cz[z], cx[z], cy[z])
        pre[z - 1] = here * (1.0 / 3.0) + here + w[z] * total
    for z in range(2, 8):
        w_out[z - 2] = w[z]
        g_out[z - 2] = g[z]
        cx_out[z - 2] = cx[z]
        cy_out[z - 2] = cy[z]
    for z in range(1, 8):
        cz_out[z - 1] = cz[z]


def k_level1(full, near, copies, c, g, w, cx, cy, cz, p, rs, dg, st):
    first = lax.axis_index("height") * 2 - 2
    middle = [full.at[z] for z in range(4)]
    window1([near.at[0, 2], near.at[0, 3]] + middle, middle + [near.at[1, 0], near.at[1, 1]], first, g, c)
    diags = couple1(6, first, c, w, cx, cy, cz)
    for z in range(2):
        rs[z] = diags[z + 2]
    for z in range(1, 5):
        here = g[z]
        total = spread(here, g[z - 1], g[z + 1], cz[z - 1], cz[z], cx[z], cy[z])
        p[z] = here * (1.0 / 3.0) + here + w[z] * total
    for z in range(2, 4):
        here = p[z]
        total = spread(here, p[z - 1], p[z + 1], cz[z - 1], cz[z], cx[z], cy[z])
        rs[z - 2] = (g[z] - OMEGA * here + w[z] * total) * rs[z - 2] * 1.5
    rows = [pair_rows(st.at[0], rs[0] + rs[1], 0, 8)]
    rows += [pair_rows(st.at[z + 1], c[2 * z] + c[2 * z + 1], 0, 8) for z in range(3)]
    pairs = pair_matrix(256)
    both = jnp.concatenate(rows, axis=0)
    down = dot(both, pairs)
    f2 = 0.5 * down[0:8]
    k2 = [0.125 * down[8 * z + 8 : 8 * z + 16] for z in range(3)]
    here = k2[1]
    fx = harmonic(here, ahead(here, 0))
    link, share = y_faces(here)
    diag = harmonic(here, k2[0]) + harmonic(here, k2[2]) + fx + behind(fx, 0) + share
    dg[0, 0:8, 0:128] = diag
    dg[0, 8:16, 0:128] = here
    tile_g = OMEGA * f2[2:6] / dg[0, 2:6, 0:128]
    tile_c = dg[0, 10:14, 0:128]
    for i in range(copies.shape[0]):
        copies[i, 0:4] = tile_g
        copies[i, 4:8] = tile_c


def k_up(block, outer, pre1, w1, g1, cx1, cy1, cz1, pre0, w0, g0, cx0, cy0, cz0, out, sems, s, c, g, w, cx, cy, cz, dg, pa, pb, p2, u1, q1, u0, q0, s1, s0, done):
    h, plan, n_h, _ = position()
    wide = s.shape[1] // 2
    tiles = wide // 4
    places = ((0, 0), (1, 0), (0, 1), None, (1, 1), (0, 2), (1, 2))
    for z in range(14):
        for t in range(tiles):
            at = tiles * (z % 2) + t
            rows = block.at[at] if 6 <= z < 8 else outer.at[*places[z // 2], at]
            s[z, 4 * t : 4 * t + 4] = rows[0:4]
            s[z, wide + 4 * t : wide + 4 * t + 4] = rows[4:8]
    q = lax.rem(h, 2)
    for z in range(13):
        keep = inside(h - 6, z, n_h)
        g[z] = jnp.where(keep, s[q + z, 0:wide], 0.0)
        c[z] = jnp.where(keep, s[q + z, wide : 2 * wide], 1.0)
    row = iota((wide, 128), 0)
    for z in range(12):
        cz[z] = harmonic(c[z], c[z + 1])
    for z in range(1, 12):
        here = c[z]
        full = harmonic(here, jnp.where(row == wide - 1, 1.0, ahead(here, 0)))
        fx = jnp.where(row == wide - 1, 0.0, full)
        first = jnp.where(row[0:8] == 0, harmonic(here[0:8], 1.0), 0.0)
        first = jnp.concatenate([first, jnp.zeros((wide - 8, 128), F32)], axis=0)
        link, both = y_faces(here)
        diag = cz[z - 1] + cz[z] + full + behind(fx, 0) + first + both
        cx[z] = fx
        cy[z] = link
        w[z] = jnp.where(inside(h - 6, z, n_h), OMEGA, 0.0) / diag
        dg[z] = diag

    def step(source, z):
        here = source[z]
        total = spread(here, source[z - 1], source[z + 1], cz[z - 1], cz[z], cx[z], cy[z])
        return here * (1.0 / 3.0) + g[z] + w[z] * total

    for z in range(1, 12):
        pa[z] = step(g, z)
    for z in range(2, 11):
        pb[z] = step(pa, z)
    for z in range(3, 10):
        pa[z] = step(pb, z)
    for z in range(4, 9):
        here = pa[z]
        extra = (step(pa, z) - here) * dg[z] * 1.5
        line = jnp.sum(extra, axis=0, keepdims=True) / jnp.sum(dg[z], axis=0, keepdims=True)
        p2[z - 4, 0:8] = jnp.zeros((8, 128), F32)
        p2[z - 4, wide + 8 : wide + 16] = jnp.zeros((8, 128), F32)
        p2[z - 4, 8 : wide + 8] = here + line
    rows = jnp.concatenate([p2[z, pl.ds(plan * 4 + 6, 8), :] for z in range(5)], axis=0)
    rows = dot(rows, copy_matrix(128))
    for z in range(5):
        u1[z] = copy_rows(s1.at[z], rows[8 * z : 8 * z + 8])
    for z in range(1, 9):
        q1[z - 1] = pre1[z - 1] + u1[z // 2]
    mid = []
    for z in range(2, 8):
        here = q1[z - 1]
        total = spread(here, q1[z - 2], q1[z], cz1[z - 2], cz1[z - 1], cx1[z - 2], cy1[z - 2])
        pb_rows = here * (1.0 / 3.0) + g1[z - 2] + w1[z - 2] * total
        mid.append(pb_rows)
    for z in range(6):
        q1[z] = mid[z]
    low = []
    for z in range(3, 7):
        here = q1[z - 2]
        total = spread(here, q1[z - 3], q1[z - 1], cz1[z - 2], cz1[z - 1], cx1[z - 2], cy1[z - 2])
        low.append(here * (1.0 / 3.0) + g1[z - 2] + w1[z - 2] * total)
    for z in range(4):
        q1[z] = low[z]
    rows = jnp.concatenate([q1[z] for z in range(4)], axis=0)
    rows = dot(rows, copy_matrix(256))
    for z in range(4):
        u0[z] = copy_rows(s0.at[z], rows[16 * z : 16 * z + 16])
    for z in range(2, 10):
        q0[z - 2] = pre0[z - 2] + u0[z // 2 - 1, 4:28]
    for z in range(3, 9):
        here = q0[z - 2]
        total = spread(here, q0[z - 3], q0[z - 1], cz0[z - 3], cz0[z - 2], cx0[z - 3], cy0[z - 3])
        u0[z - 3, 0:24] = here * (1.0 / 3.0) + g0[z - 3] + w0[z - 3] * total
    stores = []
    for z in range(4, 8):
        here = u0[z - 3, 0:24]
        total = spread(here, u0[z - 4, 0:24], u0[z - 2, 0:24], cz0[z - 3], cz0[z - 2], cx0[z - 3], cy0[z - 3])
        q0[z - 4] = here * (1.0 / 3.0) + g0[z - 3] + w0[z - 3] * total
        done[z - 4] = q0[z - 4, 4:20]
        stores.append(pltpu.make_async_copy(done.at[z - 4], out.at[z - 4], sems.at[z - 4]))
        stores[-1].start()
    for store in stores:
        store.wait()


def on_device(divergence, density, zones):
    n_h, n_p = lax.axis_size("height"), lax.axis_size("plan")
    odd = lax.rem(lax.axis_index("height"), 2)
    cores = [[i, i + 1] for i in range(0, n_h, 2)]

    def reach(step, others):
        pairs = [(i, i + step) for i in range(1, n_h - step, 2)] + others
        ends = sorted(set(range(n_h)) - {i for both in pairs for i in both})
        groups = [[i * n_p + t, j * n_p + t] for i, j in pairs for t in range(n_p)]
        return groups + [[i * n_p + t, i * n_p + t + 1] for i in ends for t in range(0, n_p, 2)]

    def meet(x, groups):
        return lax.all_gather(x, ("height", "plan"), axis=0, tiled=False, axis_index_groups=groups)

    def pair(x):
        return lax.all_gather(x, "height", axis=0, tiled=False, axis_index_groups=cores)

    links, leaps = reach(1, []), reach(5, [(0, 4), (n_h - 5, n_h - 1)])
    own = conductance(divergence, density, zones)
    core = pair(own)
    across = [[(2 * i + 1) * n_p + t, 2 * i * n_p + t + 1] for i in range(n_h // 2) for t in range(n_p - 1)]
    across += [[(2 * i + 1) * n_p + n_p - 1, (2 * i + 3) * n_p + n_p - 1] for i in range(0, n_h // 2, 2)]
    across += [[2 * i * n_p, (2 * i + 2) * n_p] for i in range(0, n_h // 2, 2)]

    def both_sides(edge):
        return pair(lax.dynamic_index_in_dim(meet(edge, across), odd, 0, keepdims=False))

    sides = both_sides(call(k_edges0, (8, 8, 512), [], core))
    near = meet(call(k_message0, (MESSAGE, 512), [], core, sides), links)
    box = (12, 24, 512)
    eight, six, seven = (8, 24, 512), (6, 24, 512), (7, 24, 512)
    *level0, pack = call(
        k_level0,
        [eight, six, six, six, six, seven, (2, 16, 256)],
        [box] * 6 + [(4, 24, 512), box, (4, 24, 512), (4, 16, 512), (10, 4, 24, 128)],
        core, near, sides,
    )
    chip = pair(pack).reshape(4, 16, 256)
    sides = both_sides(call(k_edges1, (4, 8, 256), [], chip))
    full = jnp.concatenate([chip, sides[0], sides[1]], axis=1)
    near = meet(full, links)
    box = (6, 16, 256)
    tiles = call(k_level1, (2 * n_p, 8, 128), [box] * 7 + [(2, 16, 256), (2, 16, 256), (4, 2, 16, 128)], full, near)
    two = pair(lax.dynamic_index_in_dim(near, odd, 0, keepdims=False))
    box = (10, 16, 256)
    eight, six, seven = (8, 16, 256), (6, 16, 256), (7, 16, 256)
    level1 = call(k_level1_wide, [eight, six, six, six, six, seven], [box] * 6, full, two)
    groups = [[(2 * i + k) * n_p + t for k in range(2) for t in range(n_p)] for i in range(n_h // 2)]
    block = lax.all_to_all(tiles, ("height", "plan"), split_axis=0, concat_axis=0, tiled=True, axis_index_groups=groups)
    far = meet(block, leaps)
    near = meet(far, links)
    side = jnp.where(odd == 0, jnp.stack([near[1, 0], near[0, 0], near[0, 1]]), jnp.stack([near[1, 0], near[1, 1], near[0, 1]]))
    outer = pair(side)
    wide = n_p * 4
    flat = (13, wide, 128)
    arrays = (block, outer, *level1, *level0)
    scratch = [(14, 2 * wide, 128)] + [flat] * 9
    scratch += [(5, wide + 16, 128), (5, 16, 256), (8, 16, 256), (6, 32, 512), (8, 24, 512), (5, 2, 16, 128), (4, 4, 32, 128), (4, 16, 512)]
    return pl.pallas_call(
        k_up,
        out_shape=jax.ShapeDtypeStruct((4, 16, 512), F32),
        in_specs=vmem(len(arrays)),
        out_specs=pl.BlockSpec(memory_space=pl.ANY),
        scratch_shapes=[pltpu.SemaphoreType.DMA((4,))] + [pltpu.VMEM(s, F32) for s in scratch],
        compiler_params=pltpu.CompilerParams(vmem_limit_bytes=40 << 20),
    )(*arrays)


def solution(mesh):
    return jax.shard_map(
        on_device,
        mesh=mesh,
        in_specs=(P("height", "plan", None), P("height", "plan", None), P("height", "plan", None)),
        out_specs=P("height", "plan", None),
        check_vma=False,
    )
```
